32 devices in a mesh: seq: 4 (over z), mp: 8 (over y, x, core).
Axes of the slice: x: 2, y: 2, z: 4, core: 2. Of those that a mesh axis runs over, the one named last changes fastest.
Arguments:
- ids: int32 [16, 1024], P('seq'), may hold values from 0 to 274
- lengths: int32 [1024], replicated, may hold values from 1 to 16, 12288 in all
- order: int32 [1024], replicated, may hold values from 0 to 1023, each once
- h_init: bfloat16 [2, 1024, 2048], P(None, 'seq', 'mp'), may hold values from -3 to 3
- c_init: float32 [2, 1024, 2048], P(None, 'seq', 'mp'), may hold values from -5 to 5
- embed: bfloat16 [2, 275, 100], replicated, may hold values from -5 to 5
- w_in: bfloat16 [2, 100, 8192], P(None, None, 'mp'), may hold values from -0.625 to 0.625
- w_rec: bfloat16 [2, 2048, 8192], P(None, None, 'mp'), may hold values from -0.125 to 0.125
- bias: float32 [2, 8192], P(None, 'mp'), may hold values from -3 to 3
- w_dec: bfloat16 [2, 2048, 275], P(None, 'mp'), may hold values from -0.75 to 0.75
- b_dec: float32 [2, 275], replicated, may hold values from -3 to 3
Outputs:
- loss: float32 [], replicated
- h_init_grad: float32 [2, 1024, 2048], P(None, 'seq', 'mp')
- c_init_grad: float32 [2, 1024, 2048], P(None, 'seq', 'mp')
- embed_grad: float32 [2, 275, 100], replicated
- w_in_grad: float32 [2, 100, 8192], P(None, None, ('mp', 'seq'))
- w_rec_grad: float32 [2, 2048, 8192], P(None, 'seq', 'mp')
- bias_grad: float32 [2, 8192], P(None, ('mp', 'seq'))
- w_dec_grad: float32 [2, 2048, 275], P(None, ('mp', 'seq'))
- b_dec_grad: float32 [2, 275], replicated
- rms_embed: float32 [2], replicated
- rms_hidden: float32 [2], replicated
- rms_logits: float32 [2], replicated
The draws below stay inside these ranges and needn't reach their ends.
Inputs may be any that keep to these rules, and one draw needn't show every extreme that they name: `lengths`: they add up to 12288, and the longest stream is valid over all 16 positions. `order`: every stream stands in exactly one slot.
All inputs are finite; a program needn't handle non-finite values.
Results may differ from the reference program's by a relative error of at most 0.018.
Values may be sent and summed in bfloat16 or wider, within the bound.
A program may use at most 256 MiB of HBM per device.

```python
import math
from functools import partial
import jax
import jax.numpy as jnp
import numpy as np
from jax import lax

H = 2048
E = 100
VOCAB = 275
LENGTH = 16
STREAMS = 1024


def place_ends(entries, key, least, high):
    longest = entries.shape.index(max(entries.shape))
    spots = []
    for shift in (0, 1):
        where = [jax.random.randint(jax.random.fold_in(key, axis), (), 0, length) for axis, length in enumerate(entries.shape)]
        where[longest] = (where[longest] + shift) % entries.shape[longest]
        spots.append(tuple(where))
    return entries.at[spots[0]].set(least).at[spots[1]].set(high)


def block_scale(rng, dims, cuts, low, high):
    gain, own = 1.0, jax.random.fold_in(rng, 6)
    for axis_at, blocks in cuts:
        steps = jnp.exp(jax.random.uniform(jax.random.fold_in(own, axis_at), (blocks,), jnp.float32, low / len(cuts), high / len(cuts)))
        gain = gain * jnp.repeat(steps, dims[axis_at] // blocks).reshape([-1 if axis == axis_at else 1 for axis in range(len(dims))])
    return gain


def cumulative_ranks(number_of, slope):
    loads = [(1 << 20) // math.isqrt(rank ** slope) + 1 for rank in range(1, number_of + 1)]
    spread = 1 + sum(loads) // (1 << 30)
    return np.cumsum(np.array([max(1, weight // spread) for weight in loads]))


def ranked_ids(own_key, extent, count, lean):
    table = cumulative_ranks(count, lean)
    pick = jax.random.randint(jax.random.fold_in(own_key, 1), extent, 0, int(table[count - 1]))
    standing = jnp.searchsorted(jnp.asarray(table, jnp.int32), pick, side="right")
    return jax.random.permutation(jax.random.fold_in(own_key, 2), count)[standing].astype(jnp.int32)


def length_profile(count, total, limit, slope):
    portions = [(1 << 20) // math.isqrt(standing ** slope) + 1 for standing in range(2, count + 1)]
    rest, holding = total - limit - (count - 1), [1] * (count - 1)
    while rest > 0:
        free = [i for i in range(count - 1) if holding[i] < limit]
        whole, left = sum([portions[i] for i in free]), rest
        for i in free:
            extra = min(limit - holding[i], max(1, left * portions[i] // whole), rest)
            holding[i] = holding[i] + extra
            rest = rest - extra
    return np.array([limit] + holding)


def uneven(key, amount, total, bound, lean):
    if amount == 2:
        one = jax.random.randint(key, (), max(1, total - bound), min(bound, total - 1) + 1)
        return jnp.stack([one, total - one])
    tallies = jnp.asarray(length_profile(amount, total, bound, lean), jnp.int32)
    pairs = (amount - 1) // 2
    giver, sink = tallies[1:1 + 2 * pairs:2], tallies[2:2 + 2 * pairs:2]
    room = jnp.minimum(giver - 1, bound - sink)
    passed = jax.random.randint(jax.random.fold_in(key, 1), (pairs,), 0, 1 << 20) % (room + 1)
    tallies = tallies.at[1:1 + 2 * pairs:2].set(giver - passed).at[2:2 + 2 * pairs:2].set(sink + passed)
    return tallies[jax.random.permutation(jax.random.fold_in(key, 2), amount)]


def noise(key, shape, scale, reach, pieces=(), kind=jnp.bfloat16):
    array = scale * jax.random.normal(key, shape, jnp.float32)
    if pieces:
        array = array * block_scale(key, shape, pieces, -0.22, 0.18)
    return jnp.clip(array, -reach, reach).astype(kind)


def setup_inputs(seed: int = 0) -> dict:
    splits = jax.random.split(jax.random.key(seed), 12)
    ids = place_ends(ranked_ids(splits[0], (LENGTH, STREAMS), VOCAB, 2), jax.random.fold_in(splits[0], 3), 0, VOCAB - 1).astype(jnp.int32)
    lengths = uneven(splits[1], STREAMS, STREAMS * LENGTH * 3 // 4, LENGTH, 2).astype(jnp.int32)
    order = jax.random.permutation(splits[2], STREAMS).astype(jnp.int32)
    h_init = noise(splits[3], (2, STREAMS, H), 0.5, 3.0, ((1, 4), (2, 8)))
    c_init = noise(splits[4], (2, STREAMS, H), 1.0, 5.0, ((1, 4), (2, 8)), jnp.float32)
    embed = noise(splits[5], (2, VOCAB, E), 1.0, 5.0)
    w_in = noise(splits[6], (2, E, 4 * H), E ** -0.5, 0.625, ((2, 8),))
    w_rec = noise(splits[7], (2, H, 4 * H), H ** -0.5, 0.125, ((2, 8),))
    bias = noise(splits[8], (2, 4 * H), 0.5, 3.0, ((1, 8),), jnp.float32)
    w_dec = noise(splits[9], (2, H, VOCAB), (H // 32) ** -0.5, 0.75, ((1, 8),))
    b_dec = noise(splits[10], (2, VOCAB), 0.5, 3.0, (), jnp.float32)
    return {"ids": ids, "lengths": lengths, "order": order, "h_init": h_init, "c_init": c_init, "embed": embed, "w_in": w_in, "w_rec": w_rec, "bias": bias, "w_dec": w_dec, "b_dec": b_dec}


@jax.custom_vjp
def low(v):
    return lax.optimization_barrier(v.astype(jnp.bfloat16)).astype(jnp.float32)

@jax.custom_vjp
def low_back(v):
    return v

def low_keep(v):
    return (low(v), None)

def low_pass(kept, grad):
    return (grad,)

def back_keep(v):
    return (v, None)

def back_low(kept, grad):
    return (low(grad),)
low.defvjp(low_keep, low_pass)
low_back.defvjp(back_keep, back_low)

def product(form, left, right):
    return jnp.einsum(form, left, right, precision=lax.Precision.HIGHEST)

def lstm_step(weights, carry, inputs):
    w_in_one, w_rec_one, bias_one = weights
    hidden, cell = carry
    letter_row, mask = inputs
    gates_in = low(product('be,ekg->bkg', letter_row, w_in_one))
    pre_gate = low_back(gates_in + product('bh,hkg->bkg', hidden, w_rec_one) + bias_one)
    in_gate = jax.nn.sigmoid(pre_gate[:, 0])
    forget = jax.nn.sigmoid(pre_gate[:, 1])
    cell_gate = jnp.tanh(pre_gate[:, 2])
    out_gate = jax.nn.sigmoid(pre_gate[:, 3])
    new_cell = forget * cell + in_gate * cell_gate
    column = mask[:, None]
    cell = column * new_cell + (1.0 - column) * cell
    hidden = low(column * out_gate * jnp.tanh(new_cell) + (1.0 - column) * hidden)
    return ((hidden, cell), hidden)

def direction_loss(index, params, onehot, live, targets, valid, letters):
    embed, w_in, w_rec, bias, w_dec, b_dec, h_init, c_init = params
    w_in_one = jnp.transpose(w_in[index].reshape(E, H, 4), (0, 2, 1))
    w_rec_one = jnp.transpose(w_rec[index].reshape(H, H, 4), (0, 2, 1))
    bias_one = jnp.transpose(bias[index].reshape(H, 4), (1, 0))
    letter_rows = product('tbv,ve->tbe', onehot, embed[index])
    mask_seq = live
    if index == 1:
        letter_rows = letter_rows[::-1]
        mask_seq = live[::-1]
    stepper = jax.checkpoint(partial(lstm_step, (w_in_one, w_rec_one, bias_one)))
    final_state, hiddens = lax.scan(stepper, (h_init[index], c_init[index]), (letter_rows, mask_seq))
    if index == 1:
        hiddens = hiddens[::-1]
    logits = low_back(product('tbh,hv->tbv', hiddens, w_dec[index]) + b_dec[index])
    log_total = jax.nn.logsumexp(logits, axis=-1)
    picked = lax.optimization_barrier(jnp.sum(jnp.where(targets[index][:, :, None] == letters, logits, 0.0), axis=-1))
    hidden_squares = jnp.sum(live[:, :, None] * hiddens * hiddens)
    logit_squares = jnp.sum(valid[index][:, :, None] * logits * logits)
    return (jnp.sum(valid[index] * (log_total - picked)), (hidden_squares, logit_squares))

def reference(ids, lengths, order, h_init, c_init, embed, w_in, w_rec, bias, w_dec, b_dec):
    slot_ids = jnp.take(ids, order, axis=1).astype(jnp.int32)
    slot_len = jnp.take(lengths, order).astype(jnp.int32)
    times = jnp.arange(LENGTH, dtype=jnp.int32)[:, None]
    live = (times < slot_len[None, :]).astype(jnp.float32)
    count = 2.0 * jnp.sum(slot_len - 1).astype(jnp.float32)
    live_total = jnp.sum(slot_len).astype(jnp.float32)
    letters = jnp.arange(VOCAB, dtype=jnp.int32)
    onehot = (slot_ids[:, :, None] == letters).astype(jnp.float32)
    blank = jnp.zeros((1, STREAMS), jnp.int32)
    ahead = jnp.concatenate([slot_ids[1:].astype(jnp.int32), blank], axis=0)
    behind = jnp.concatenate([blank, slot_ids[:-1].astype(jnp.int32)], axis=0)
    targets = (ahead, behind)
    fore_valid = (times + 1 < slot_len[None, :]).astype(jnp.float32)
    back_valid = ((times >= 1) & (times < slot_len[None, :])).astype(jnp.float32)
    valid = (fore_valid, back_valid)

    def total_loss(*params):
        summed, fore_aux = direction_loss(0, params, onehot, live, targets, valid, letters)
        back_sum, back_aux = direction_loss(1, params, onehot, live, targets, valid, letters)
        hidden_sq = jnp.stack([fore_aux[0], back_aux[0]])
        logit_sq = jnp.stack([fore_aux[1], back_aux[1]])
        return ((summed + back_sum) / count, (hidden_sq, logit_sq))
    params = (embed.astype(jnp.float32), w_in.astype(jnp.float32), w_rec.astype(jnp.float32), bias.astype(jnp.float32), w_dec.astype(jnp.float32), b_dec.astype(jnp.float32), h_init.astype(jnp.float32), c_init.astype(jnp.float32))
    loss, pullback, extras = jax.vjp(total_loss, *params, has_aux=True)
    grads = pullback(jnp.ones((), jnp.float32))
    embed_wide = embed.astype(jnp.float32)
    rms_embed = jnp.sqrt(lax.optimization_barrier(jnp.mean(embed_wide * embed_wide, axis=(1, 2))))
    rms_hidden = jnp.sqrt(extras[0] / (H * live_total))
    rms_logits = jnp.sqrt(extras[1] / (VOCAB * count / 2.0))
    return (loss, grads[6], grads[7], grads[0], grads[1], grads[2], grads[3], grads[4], grads[5], rms_embed, rms_hidden, rms_logits)
```

```python
import jax
import jax.numpy as jnp
from jax import lax
from jax.sharding import PartitionSpec as P


def column_order(own_units):
    lanes = min(128, own_units)
    source = jnp.arange(4 * lanes, dtype=jnp.int32)
    place = (source % 4) * lanes + source // 4
    matrix = (place[:, None] == jnp.arange(4 * lanes, dtype=jnp.int32)[None, :]).astype(jnp.bfloat16)
    return lanes, matrix


def grouped(x, matrix):
    width = matrix.shape[0]
    parts = x.reshape(x.shape[:-1] + (x.shape[-1] // width, width))
    out = jnp.einsum("...gc,cp->...gp", parts, matrix, preferred_element_type=jnp.float32)
    return out.astype(x.dtype).reshape(x.shape)


def ungrouped(x, matrix):
    return grouped(x, matrix.T)


def ungrouped_wide(x, lanes):
    parts = x.reshape(x.shape[:-1] + (x.shape[-1] // (4 * lanes), 4, lanes))
    return jnp.swapaxes(parts, -1, -2).reshape(x.shape)


def gates_of(pre, lanes):
    parts = pre.reshape(pre.shape[:-1] + (pre.shape[-1] // (4 * lanes), 4, lanes))
    flat = pre.shape[:-1] + (pre.shape[-1] // 4,)
    return tuple(parts[..., k, :].reshape(flat) for k in range(4))


def joined_gates(gates, lanes):
    split = [g.reshape(g.shape[:-1] + (g.shape[-1] // lanes, 1, lanes)) for g in gates]
    joined = jnp.concatenate(split, axis=-2)
    return joined.reshape(gates[0].shape[:-1] + (4 * gates[0].shape[-1],))


def recurrences(step_ids, own_len, h_init, c_init, embed, w_in, w_rec, bias, w_dec, wd_full, b_dec, count, lanes):
    length, per_dev = step_ids.shape[1:]
    letter_count = embed.shape[1]
    steps = jnp.arange(length, dtype=jnp.int32)
    live_steps = jnp.stack(
        [steps[:, None] < own_len[None, :], (length - 1 - steps)[:, None] < own_len[None, :]], axis=1
    )[..., None]
    letters = jnp.arange(letter_count, dtype=jnp.int32)
    onehot = (jnp.swapaxes(step_ids, 0, 1)[..., None] == letters).astype(jnp.bfloat16)
    letter_rows = jnp.einsum(
        "sdbv,dve->sdbe", onehot, embed, preferred_element_type=jnp.float32
    ).astype(jnp.bfloat16)
    gates_in = jnp.einsum(
        "sdbe,dec->sdbc", letter_rows, w_in, preferred_element_type=jnp.float32
    ).astype(jnp.bfloat16)

    def forward_step(carry, inputs):
        hidden, cell = carry
        gate_in, live = inputs
        whole = lax.all_gather(hidden, "mp", axis=2, tiled=True)
        recurrent = jnp.einsum("dbh,dhc->dbc", whole, w_rec, preferred_element_type=jnp.float32)
        pre = gate_in.astype(jnp.float32) + recurrent + bias[:, None]
        in_pre, forget_pre, cell_pre, out_pre = gates_of(pre, lanes)
        in_gate, forget, out_gate = (jax.nn.sigmoid(x) for x in (in_pre, forget_pre, out_pre))
        cell_gate = jnp.tanh(cell_pre)
        new_cell = forget * cell + in_gate * cell_gate
        cell_next = jnp.where(live, new_cell, cell)
        hidden_next = jnp.where(
            live, out_gate * jnp.tanh(new_cell), hidden.astype(jnp.float32)
        ).astype(jnp.bfloat16)
        return ((hidden_next, cell_next), (whole, cell, in_gate, forget, cell_gate, out_gate))

    (last_hidden, last_cell), (wholes, cells, *gates) = lax.scan(
        forward_step, (h_init, c_init), (gates_in, live_steps)
    )
    last_whole = lax.all_gather(last_hidden, "mp", axis=2, tiled=True)
    after = jnp.concatenate([wholes[1:], last_whole[None]], axis=0)
    own = h_init.shape[2]
    mine = lax.dynamic_slice_in_dim(after, lax.axis_index("mp") * own, own, axis=3)
    mine_wide = mine.astype(jnp.float32)
    hidden_sq = jnp.sum(jnp.where(live_steps, mine_wide * mine_wide, 0.0), axis=(0, 2, 3))
    logits = (
        jnp.einsum("sdbh,dhv->sdbv", after, wd_full, preferred_element_type=jnp.float32) + b_dec[None, :, None]
    )
    targets = jnp.swapaxes(jnp.concatenate([step_ids[:, 1:], step_ids[:, :1]], axis=1), 0, 1)
    fore_valid = (steps[:, None] + 1 < own_len[None, :])
    back_valid = (steps[:, None] < length - 1) & ((length - 1 - steps)[:, None] < own_len[None, :])
    valid = jnp.stack([fore_valid, back_valid], axis=1).astype(jnp.float32)
    logit_sq = jnp.sum(valid[..., None] * logits * logits, axis=(0, 2, 3))
    top = jnp.max(logits, axis=-1, keepdims=True)
    log_total = top + jnp.log(jnp.sum(jnp.exp(logits - top), axis=-1, keepdims=True))
    target_hot = targets[..., None] == letters
    picked = jnp.sum(jnp.where(target_hot, logits, 0.0), axis=-1)
    loss = jnp.sum(valid * (log_total[..., 0] - picked))
    grad_logits = (
        valid[..., None] * (jnp.exp(logits - log_total) - target_hot.astype(jnp.float32)) / count
    ).astype(jnp.bfloat16)
    dec_bias = jnp.sum(grad_logits.astype(jnp.float32), axis=(0, 2))
    dec_grad = jnp.einsum("sdbh,sdbv->dhv", mine, grad_logits, preferred_element_type=jnp.float32)

    def backward_step(carry, inputs):
        grad_hidden, grad_cell = carry
        live, cell, in_gate, forget, cell_gate, out_gate, grad_logit = inputs
        grad_hidden = grad_hidden + jnp.einsum(
            "dbv,dhv->dbh", grad_logit, w_dec, preferred_element_type=jnp.float32
        )
        squash = jnp.tanh(forget * cell + in_gate * cell_gate)
        grad_new = jnp.where(live, grad_cell + grad_hidden * out_gate * (1.0 - squash * squash), 0.0)
        grad_out = jnp.where(live, grad_hidden * squash, 0.0)
        grad_pre = joined_gates(
            [
                grad_new * cell_gate * in_gate * (1.0 - in_gate),
                grad_new * cell * forget * (1.0 - forget),
                grad_new * in_gate * (1.0 - cell_gate * cell_gate),
                grad_out * out_gate * (1.0 - out_gate),
            ],
            lanes,
        ).astype(jnp.bfloat16)
        grad_cell_prev = grad_new * forget + jnp.where(live, 0.0, grad_cell)
        held = jnp.where(live, 0.0, grad_hidden)
        terms = jnp.einsum("dbc,dhc->dbh", grad_pre, w_rec, preferred_element_type=jnp.float32)
        through = lax.psum_scatter(
            terms.astype(jnp.bfloat16), "mp", scatter_dimension=2, tiled=True
        ).astype(jnp.float32)
        return ((held + through, grad_cell_prev), grad_pre)

    start = jnp.zeros(c_init.shape, jnp.float32)
    (hidden_grad, cell_grad), grad_pres = lax.scan(
        backward_step, (start, start), (live_steps, cells, *gates, grad_logits), reverse=True
    )
    rec_grad = jnp.einsum("sdbh,sdbc->dhc", wholes, grad_pres, preferred_element_type=jnp.float32)
    letter_grad = jnp.einsum("sdbv,sdbc->dvc", onehot, grad_pres, preferred_element_type=jnp.float32)
    return loss, hidden_sq, logit_sq, dec_bias, dec_grad, hidden_grad, cell_grad, rec_grad, letter_grad


def per_device(ids, lengths, order, h_init, c_init, embed, w_in, w_rec, bias, w_dec, b_dec):
    seq_rank = lax.axis_index("seq")
    first_mp = (lax.axis_index("mp") == 0).astype(jnp.float32)
    streams = ids.shape[1]
    per_dev = h_init.shape[1]
    own_units, all_units = h_init.shape[2], w_rec.shape[1]
    letter_count = embed.shape[1]
    wd_full = lax.all_gather(w_dec, "mp", axis=1, tiled=True)
    whole_ids = lax.all_gather(ids, "seq", axis=0, tiled=True)
    own_order = lax.dynamic_slice_in_dim(order, seq_rank * per_dev, per_dev)
    slot_ids = jnp.take(whole_ids, own_order, axis=1)
    own_len = jnp.take(lengths, own_order)
    live_total = jnp.sum(lengths).astype(jnp.float32)
    count = 2.0 * (jnp.sum(lengths) - streams).astype(jnp.float32)
    step_ids = jnp.stack([slot_ids, jnp.flip(slot_ids, 0)])
    lanes, matrix = column_order(own_units)
    w_rec_grouped = grouped(w_rec, matrix)
    w_in_grouped = grouped(w_in, matrix)
    bias_grouped = jnp.swapaxes(
        bias.reshape(2, own_units // lanes, lanes, 4), -1, -2
    ).reshape(bias.shape)
    loss, hidden_sq, logit_sq, dec_bias, dec_grad, hidden_grad, cell_grad, rec_grad, letter_grad = recurrences(
        step_ids, own_len, h_init, c_init, embed, w_in_grouped, w_rec_grouped, bias_grouped, w_dec, wd_full,
        b_dec, count, lanes,
    )
    embed_wide = embed.astype(jnp.float32)
    in_grad = jnp.einsum("dve,dvc->dec", embed_wide, letter_grad, precision=lax.Precision.HIGHEST)
    bias_grad = jnp.sum(letter_grad, axis=1, keepdims=True)
    embed_part = jnp.einsum(
        "dvc,dec->dve", letter_grad, w_in_grouped.astype(jnp.float32), precision=lax.Precision.HIGHEST
    )
    edge = ungrouped_wide(jnp.concatenate([in_grad, bias_grad], axis=1), lanes)
    rec_part = lax.psum_scatter(rec_grad.astype(jnp.bfloat16), "seq", scatter_dimension=1, tiled=True)
    edge_part = lax.psum_scatter(edge.astype(jnp.bfloat16), "seq", scatter_dimension=2, tiled=True)
    dec_part = lax.psum_scatter(dec_grad.astype(jnp.bfloat16), "seq", scatter_dimension=1, tiled=True)
    loss_sum, hidden_all, logit_all, dec_bias_grad, embed_grad = lax.psum(
        (loss * first_mp, hidden_sq, logit_sq * first_mp, dec_bias * first_mp, embed_part), ("seq", "mp")
    )
    rec_out = ungrouped(rec_part, matrix).astype(jnp.float32)
    rms_embed = jnp.sqrt(jnp.mean(embed_wide * embed_wide, axis=(1, 2)))
    return (
        loss_sum / count,
        hidden_grad,
        cell_grad,
        embed_grad,
        edge_part[:, :-1].astype(jnp.float32),
        rec_out,
        edge_part[:, -1].astype(jnp.float32),
        dec_part.astype(jnp.float32),
        dec_bias_grad,
        rms_embed,
        jnp.sqrt(hidden_all / (all_units * live_total)),
        jnp.sqrt(logit_all / (letter_count * count / 2.0)),
    )


def solution(mesh):
    in_specs = (
        P("seq", None),
        P(),
        P(),
        P(None, "seq", "mp"),
        P(None, "seq", "mp"),
        P(),
        P(None, None, "mp"),
        P(None, None, "mp"),
        P(None, "mp"),
        P(None, "mp", None),
        P(),
    )
    out_specs = (
        P(),
        P(None, "seq", "mp"),
        P(None, "seq", "mp"),
        P(),
        P(None, None, ("mp", "seq")),
        P(None, "seq", "mp"),
        P(None, ("mp", "seq")),
        P(None, ("mp", "seq"), None),
        P(),
        P(),
        P(),
        P(),
    )
    return jax.shard_map(
        per_device, mesh=mesh, in_specs=in_specs, out_specs=out_specs, check_vma=False
    )
```

```python
import functools

import jax
import jax.numpy as jnp
from jax import lax
from jax.experimental import pallas as pl
from jax.experimental.pallas import tpu as pltpu
from jax.sharding import PartitionSpec as P

VMEM_LIMIT = 56 * 2**20


def column_order(own_units):
    lanes = min(128, own_units)
    source = jnp.arange(4 * lanes, dtype=jnp.int32)
    place = (source % 4) * lanes + source // 4
    matrix = (place[:, None] == jnp.arange(4 * lanes, dtype=jnp.int32)[None, :]).astype(jnp.bfloat16)
    return lanes, matrix


def grouped(x, matrix):
    width = matrix.shape[0]
    parts = x.reshape(x.shape[:-1] + (x.shape[-1] // width, width))
    out = jnp.einsum("...gc,cp->...gp", parts, matrix, preferred_element_type=jnp.float32)
    return out.astype(x.dtype).reshape(x.shape)


def ungrouped(x, matrix):
    return grouped(x, matrix.T)


def ungrouped_wide(x, lanes):
    parts = x.reshape(x.shape[:-1] + (x.shape[-1] // (4 * lanes), 4, lanes))
    return jnp.swapaxes(parts, -1, -2).reshape(x.shape)


def gates_of(pre, lanes):
    parts = pre.reshape(pre.shape[:-1] + (pre.shape[-1] // (4 * lanes), 4, lanes))
    flat = pre.shape[:-1] + (pre.shape[-1] // 4,)
    return tuple(parts[..., k, :].reshape(flat) for k in range(4))


def joined_gates(gates, lanes):
    split = [g.reshape(g.shape[:-1] + (g.shape[-1] // lanes, 1, lanes)) for g in gates]
    joined = jnp.concatenate(split, axis=-2)
    return joined.reshape(gates[0].shape[:-1] + (4 * gates[0].shape[-1],))


def recurrences(step_ids, own_len, h_init, c_init, embed, w_in, w_rec, bias, w_dec, wd_full, b_dec, count, lanes):
    length, per_dev = step_ids.shape[1:]
    letter_count = embed.shape[1]
    steps = jnp.arange(length, dtype=jnp.int32)
    live_steps = jnp.stack(
        [steps[:, None] < own_len[None, :], (length - 1 - steps)[:, None] < own_len[None, :]], axis=1
    )[..., None]
    letters = jnp.arange(letter_count, dtype=jnp.int32)
    onehot = (jnp.swapaxes(step_ids, 0, 1)[..., None] == letters).astype(jnp.bfloat16)
    letter_rows = jnp.einsum(
        "sdbv,dve->sdbe", onehot, embed, preferred_element_type=jnp.float32
    ).astype(jnp.bfloat16)
    gates_in = jnp.einsum(
        "sdbe,dec->sdbc", letter_rows, w_in, preferred_element_type=jnp.float32
    ).astype(jnp.bfloat16)

    def forward_step(carry, inputs):
        hidden, cell = carry
        gate_in, live = inputs
        whole = lax.all_gather(hidden, "mp", axis=2, tiled=True)
        recurrent = jnp.einsum("dbh,dhc->dbc", whole, w_rec, preferred_element_type=jnp.float32)
        pre = gate_in.astype(jnp.float32) + recurrent + bias[:, None]
        in_pre, forget_pre, cell_pre, out_pre = gates_of(pre, lanes)
        in_gate, forget, out_gate = (jax.nn.sigmoid(x) for x in (in_pre, forget_pre, out_pre))
        cell_gate = jnp.tanh(cell_pre)
        new_cell = forget * cell + in_gate * cell_gate
        cell_next = jnp.where(live, new_cell, cell)
        hidden_next = jnp.where(
            live, out_gate * jnp.tanh(new_cell), hidden.astype(jnp.float32)
        ).astype(jnp.bfloat16)
        return ((hidden_next, cell_next), (whole, cell, in_gate, forget, cell_gate, out_gate))

    (last_hidden, last_cell), (wholes, cells, *gates) = lax.scan(
        forward_step, (h_init, c_init), (gates_in, live_steps)
    )
    last_whole = lax.all_gather(last_hidden, "mp", axis=2, tiled=True)
    after = jnp.concatenate([wholes[1:], last_whole[None]], axis=0)
    own = h_init.shape[2]
    mine = lax.dynamic_slice_in_dim(after, lax.axis_index("mp") * own, own, axis=3)
    mine_wide = mine.astype(jnp.float32)
    hidden_sq = jnp.sum(jnp.where(live_steps, mine_wide * mine_wide, 0.0), axis=(0, 2, 3))
    logits = (
        jnp.einsum("sdbh,dhv->sdbv", after, wd_full, preferred_element_type=jnp.float32) + b_dec[None, :, None]
    )
    targets = jnp.swapaxes(jnp.concatenate([step_ids[:, 1:], step_ids[:, :1]], axis=1), 0, 1)
    fore_valid = (steps[:, None] + 1 < own_len[None, :])
    back_valid = (steps[:, None] < length - 1) & ((length - 1 - steps)[:, None] < own_len[None, :])
    valid = jnp.stack([fore_valid, back_valid], axis=1).astype(jnp.float32)
    logit_sq = jnp.sum(valid[..., None] * logits * logits, axis=(0, 2, 3))
    top = jnp.max(logits, axis=-1, keepdims=True)
    log_total = top + jnp.log(jnp.sum(jnp.exp(logits - top), axis=-1, keepdims=True))
    target_hot = targets[..., None] == letters
    picked = jnp.sum(jnp.where(target_hot, logits, 0.0), axis=-1)
    loss = jnp.sum(valid * (log_total[..., 0] - picked))
    grad_logits = (
        valid[..., None] * (jnp.exp(logits - log_total) - target_hot.astype(jnp.float32)) / count
    ).astype(jnp.bfloat16)
    dec_bias = jnp.sum(grad_logits.astype(jnp.float32), axis=(0, 2))
    dec_grad = jnp.einsum("sdbh,sdbv->dhv", mine, grad_logits, preferred_element_type=jnp.float32)

    def backward_step(carry, inputs):
        grad_hidden, grad_cell = carry
        live, cell, in_gate, forget, cell_gate, out_gate, grad_logit = inputs
        grad_hidden = grad_hidden + jnp.einsum(
            "dbv,dhv->dbh", grad_logit, w_dec, preferred_element_type=jnp.float32
        )
        squash = jnp.tanh(forget * cell + in_gate * cell_gate)
        grad_new = jnp.where(live, grad_cell + grad_hidden * out_gate * (1.0 - squash * squash), 0.0)
        grad_out = jnp.where(live, grad_hidden * squash, 0.0)
        grad_pre = joined_gates(
            [
                grad_new * cell_gate * in_gate * (1.0 - in_gate),
                grad_new * cell * forget * (1.0 - forget),
                grad_new * in_gate * (1.0 - cell_gate * cell_gate),
                grad_out * out_gate * (1.0 - out_gate),
            ],
            lanes,
        ).astype(jnp.bfloat16)
        grad_cell_prev = grad_new * forget + jnp.where(live, 0.0, grad_cell)
        held = jnp.where(live, 0.0, grad_hidden)
        terms = jnp.einsum("dbc,dhc->dbh", grad_pre, w_rec, preferred_element_type=jnp.float32)
        through = lax.psum_scatter(
            terms.astype(jnp.bfloat16), "mp", scatter_dimension=2, tiled=True
        ).astype(jnp.float32)
        return ((held + through, grad_cell_prev), grad_pre)

    start = jnp.zeros(c_init.shape, jnp.float32)
    (hidden_grad, cell_grad), grad_pres = lax.scan(
        backward_step, (start, start), (live_steps, cells, *gates, grad_logits), reverse=True
    )
    rec_grad = jnp.einsum("sdbh,sdbc->dhc", wholes, grad_pres, preferred_element_type=jnp.float32)
    letter_grad = jnp.einsum("sdbv,sdbc->dvc", onehot, grad_pres, preferred_element_type=jnp.float32)
    return loss, hidden_sq, logit_sq, dec_bias, dec_grad, hidden_grad, cell_grad, rec_grad, letter_grad


MESH = pl.DeviceIdType.MESH
LANES = 128
VOCAB_PAD = 384
CHUNK = 32
NT = (((1,), (1,)), ((), ()))
TN = (((0,), (0,)), ((), ()))


def sigmoid(x):
    return 0.5 * jnp.tanh(0.5 * x) + 0.5


def matmul(left, right, dims=(((1,), (0,)), ((), ()))):
    return lax.dot_general(left, right, dims, preferred_element_type=jnp.float32)


def neighbours():
    me = lax.axis_index("mp")
    row, column, core = me // 4, (me // 2) % 2, me % 2
    sibling = row * 4 + column * 2 + (1 - core)
    across = (1 - row) * 4 + (1 - column) * 2 + core
    side = row * 4 + (1 - column) * 2 + core
    up = (1 - row) * 4 + column * 2 + core
    return me, sibling, (across, side, up)


def greet(peers):
    seq = lax.axis_index("seq")
    barrier = pltpu.get_barrier_semaphore()
    for peer in peers:
        pl.semaphore_signal(barrier, inc=1, device_id=(seq, peer), device_id_type=MESH)
    pl.semaphore_wait(barrier, len(peers))


def remote(src, dst, send, recv, peer):
    return pltpu.make_async_remote_copy(
        src_ref=src, dst_ref=dst, send_sem=send, recv_sem=recv,
        device_id=(lax.axis_index("seq"), peer), device_id_type=MESH,
    )


def other_core(peer):
    return (peer // 2) * 2 + (1 - peer % 2)


def column_of(table, lane):
    lanes = lax.broadcasted_iota(jnp.int32, table.shape, 1)
    return jnp.sum(jnp.where(lanes == lane, table, 0.0), axis=1, keepdims=True)


def time_of(direction, step, length):
    return step if direction == 0 else length - 1 - step


def forward_kernel(
    length, letters, info, inverse, h_in, c_in, embed, w_in, bias, b_dec, wd_hbm, w_hbm,
    wholes, acts, grads, loss, logit_sq, hidden_sq, dec_bias, dec_grad,
    w, wd, buf, cell, acc, logit, stage, grad, load_sem, send_sem, recv_sem, save_sem, act_sem, grad_sem,
):
    me, sibling, peers = neighbours()
    blocks, rows, units = buf.shape[2:]
    groups = units // LANES
    load_w = pltpu.make_async_copy(w_hbm, w, load_sem.at[0])
    load_wd = pltpu.make_async_copy(wd_hbm, wd, load_sem.at[1])
    load_w.start()
    load_wd.start()
    greet((sibling,) + peers)
    for ref in (loss, logit_sq, hidden_sq, dec_bias, dec_grad):
        ref[...] = jnp.zeros(ref.shape, ref.dtype)
    cell[...] = c_in[...]

    def direct(d, step):
        slot, par = step % 3, step % 2
        block = buf.at[d, slot, me]
        return [
            remote(block, block, send_sem.at[d, par, n], recv_sem.at[d, slot, me], peer)
            for n, peer in enumerate(peers + (sibling,))
        ]

    def relay(d, step, n):
        slot, par = step % 3, step % 2
        block = buf.at[d, slot, peers[n]]
        return remote(block, block, send_sem.at[d, par, 4 + n], recv_sem.at[d, slot, peers[n]], sibling)

    def arrival(d, step, source):
        slot = step % 3
        block = buf.at[d, slot, source]
        return remote(block, block, send_sem.at[d, step % 2, 0], recv_sem.at[d, slot, source], sibling)

    def save(d, step):
        return pltpu.make_async_copy(buf.at[d, step % 3], wholes.at[step, d], save_sem.at[d, step % 2])

    def save_acts(d, step):
        return pltpu.make_async_copy(stage.at[d], acts.at[step, d], act_sem.at[d])

    def save_grad(d, step):
        return pltpu.make_async_copy(grad.at[d], grads.at[step, d], grad_sem.at[d])

    def finish_sends(d, step):
        for copy in direct(d, step):
            copy.wait_send()
        for n in range(3):
            relay(d, step, n).wait_send()

    def gates(d, step):
        slot, later = step % 3, (step + 1) % 3
        when = time_of(d, step, length)

        def chunk(i, carry):
            at = pl.ds(pl.multiple_of(i * CHUNK, CHUNK), CHUNK)
            live = info[d, at, LANES - 1:LANES] > when.astype(jnp.float32)
            for g in range(groups):
                lanes = slice(g * LANES, (g + 1) * LANES)
                pre = [acc[at, (4 * g + k) * LANES:(4 * g + k + 1) * LANES] for k in range(4)]
                in_gate, forget, out_gate = sigmoid(pre[0]), sigmoid(pre[1]), sigmoid(pre[3])
                cell_gate = jnp.tanh(pre[2])
                old = cell[d, at, lanes]
                new = forget * old + in_gate * cell_gate
                for k, value in enumerate((in_gate, forget, cell_gate, out_gate, old)):
                    stage[d, k, at, lanes] = value
                cell[d, at, lanes] = jnp.where(live, new, old)
                before = buf[d, slot, me, at, lanes].astype(jnp.float32)
                hidden = jnp.where(live, out_gate * jnp.tanh(new), before).astype(jnp.bfloat16)
                buf[d, later, me, at, lanes] = hidden
                wide = hidden.astype(jnp.float32)
                hidden_sq[d] += jnp.where(live, wide * wide, 0.0)
            return carry

        lax.fori_loop(0, rows // CHUNK, chunk, 0)

    def decode(d, step):
        slot = step % 3
        total = jnp.broadcast_to(b_dec[d], logit.shape)
        for b in range(blocks):
            total += matmul(buf[d, slot, b], wd[d, b])
        logit[...] = total
        when = time_of(d, step - 1, length)
        reach = when + 1 if d == 0 else when
        scale = inverse[0, 0]

        def chunk(i, carry):
            at = pl.ds(pl.multiple_of(i * CHUNK, CHUNK), CHUNK)
            table = info[d, at, :]
            valid = (table[:, LANES - 1:LANES] > reach.astype(jnp.float32)) & (step < length)
            target = column_of(table, step)
            value = logit[at, :]
            lanes = lax.broadcasted_iota(jnp.int32, value.shape, 1)
            hot = lanes.astype(jnp.float32) == target
            top = jnp.max(value, axis=1, keepdims=True)
            power = jnp.exp(value - top)
            total = jnp.sum(power, axis=1, keepdims=True)
            picked = jnp.sum(jnp.where(hot, value, 0.0), axis=1, keepdims=True)
            loss[d] += jnp.broadcast_to(jnp.where(valid, top + jnp.log(total) - picked, 0.0), (CHUNK, LANES))
            kept = jnp.where(valid & (lanes < letters), value, 0.0)
            square = kept * kept
            logit_sq[d] += sum(square[:, n * LANES:(n + 1) * LANES] for n in range(VOCAB_PAD // LANES))
            slope = jnp.where(
                valid, (power * (1.0 / total) - jnp.where(hot, 1.0, 0.0)) * scale, 0.0
            ).astype(jnp.bfloat16)
            grad[d, at, :] = slope
            wide = slope.astype(jnp.float32)
            dec_bias[d] += sum(wide[n * 8:(n + 1) * 8] for n in range(CHUNK // 8))
            return carry

        lax.fori_loop(0, rows // CHUNK, chunk, 0)
        dec_grad[d] += matmul(buf[d, slot, me], grad[d], TN)

    def half(step, d):
        @pl.when(step < length)
        def _():
            ids = column_of(info[d], step)
            hot = (lax.broadcasted_iota(jnp.int32, (rows, VOCAB_PAD), 1).astype(jnp.float32) == ids)
            row = matmul(hot.astype(jnp.bfloat16), embed[d]).astype(jnp.bfloat16)
            acc[...] = matmul(row, w_in[d]).astype(jnp.bfloat16).astype(jnp.float32) + bias[d]

        for n, peer in enumerate(peers):
            arrival(d, step, peer).wait_recv()
            relay(d, step, n).start()

        if d == 0:
            @pl.when(step == 0)
            def _():
                load_w.wait()
                load_wd.wait()

        slot = step % 3

        def advance(block):
            acc[...] += matmul(buf[d, slot, block], w[d, block])

        @pl.when(step < length)
        def _():
            for block in (me,) + peers:
                advance(block)

        for block in (sibling,) + tuple(other_core(peer) for peer in peers):
            arrival(d, step, block).wait_recv()

        @pl.when(step < length)
        def _():
            save(d, step).start()
            for block in (sibling,) + tuple(other_core(peer) for peer in peers):
                advance(block)

            @pl.when(step > 0)
            def _():
                save_acts(d, step - 1).wait()

            gates(d, step)
            save_acts(d, step).start()

            @pl.when(step > 0)
            def _():
                save(d, step - 1).wait()
                finish_sends(d, step - 1)

            for copy in direct(d, step + 1):
                copy.start()

        @pl.when(step > 0)
        def _():
            @pl.when(step > 1)
            def _():
                save_grad(d, step - 2).wait()

            decode(d, step)
            save_grad(d, step - 1).start()

    for d in range(2):
        buf[d, 0, me] = h_in[d]
        for copy in direct(d, 0):
            copy.start()

    def both(step, carry):
        for d in range(2):
            half(step, d)
        return carry

    lax.fori_loop(0, length + 1, both, 0)
    for d in range(2):
        save(d, length - 1).wait()
        save_acts(d, length - 1).wait()
        save_grad(d, length - 1).wait()
        finish_sends(d, length - 1)
        finish_sends(d, length)


def backward_kernel(
    length, info, w_dec, acts, grads, w_hbm,
    pres, hidden_grad, cell_grad,
    w, stage, grad, pre, held, own, sent, got, passed, taken, load_sem, act_sem, grad_sem, pre_sem,
    core_send, core_recv, chip_send, chip_recv,
):
    me, sibling, peers = neighbours()
    rows, units = held.shape[1:]
    groups = units // LANES
    load_w = pltpu.make_async_copy(w_hbm, w, load_sem)
    load_w.start()

    def load_acts(d, step):
        return pltpu.make_async_copy(acts.at[step, d], stage.at[d], act_sem.at[d])

    def load_grad(d, step):
        return pltpu.make_async_copy(grads.at[step, d], grad.at[d], grad_sem.at[d])

    def save_pre(d, step):
        return pltpu.make_async_copy(pre.at[d], pres.at[step, d], pre_sem.at[d])

    for d in range(2):
        load_acts(d, length - 1).start()
        load_grad(d, length - 1).start()
    greet((sibling,) + peers)
    held[...] = jnp.zeros(held.shape, held.dtype)
    own[...] = jnp.zeros(own.shape, own.dtype)
    cell_grad[...] = jnp.zeros(cell_grad.shape, cell_grad.dtype)

    def to_core(d, turn, n):
        return remote(
            sent.at[d, n], got.at[d, turn % 2, n], core_send.at[d, n], core_recv.at[d, turn % 2, n], sibling
        )

    def to_chip(d, turn, n):
        return remote(
            passed.at[d, n], taken.at[d, turn % 2, n], chip_send.at[d, n], chip_recv.at[d, turn % 2, n], peers[n]
        )

    def half(turn, d):
        step = length - 1 - turn
        when = time_of(d, step, length)
        load_acts(d, step).wait()
        load_grad(d, step).wait()
        held[d] += matmul(grad[d], w_dec[d], NT)

        @pl.when(turn > 0)
        def _():
            for n in range(3):
                to_chip(d, turn - 1, n).wait_recv()
            save_pre(d, step + 1).wait()

        def chunk(i, carry):
            at = pl.ds(pl.multiple_of(i * CHUNK, CHUNK), CHUNK)
            live = info[d, at, LANES - 1:LANES] > when.astype(jnp.float32)
            for g in range(groups):
                lanes = slice(g * LANES, (g + 1) * LANES)
                through = own[d, at, lanes]
                for n in range(3):
                    through += jnp.where(turn > 0, taken[d, (turn + 1) % 2, n, at, lanes].astype(jnp.float32), 0.0)
                total = held[d, at, lanes] + through
                in_gate, forget, cell_gate, out_gate, old = (stage[d, k, at, lanes] for k in range(5))
                squash = jnp.tanh(forget * old + in_gate * cell_gate)
                later = cell_grad[d, at, lanes]
                new = jnp.where(live, later + total * out_gate * (1.0 - squash * squash), 0.0)
                out = jnp.where(live, total * squash, 0.0)
                values = (
                    new * cell_gate * in_gate * (1.0 - in_gate),
                    new * old * forget * (1.0 - forget),
                    new * in_gate * (1.0 - cell_gate * cell_gate),
                    out * out_gate * (1.0 - out_gate),
                )
                for k, value in enumerate(values):
                    pre[d, at, (4 * g + k) * LANES:(4 * g + k + 1) * LANES] = value.astype(jnp.bfloat16)
                cell_grad[d, at, lanes] = new * forget + jnp.where(live, 0.0, later)
                held[d, at, lanes] = jnp.where(live, 0.0, total)
            return carry

        lax.fori_loop(0, rows // CHUNK, chunk, 0)
        save_pre(d, step).start()

        @pl.when(turn < length - 1)
        def _():
            load_acts(d, step - 1).start()
            load_grad(d, step - 1).start()

        @pl.when(turn > 0)
        def _():
            for n in range(4):
                to_core(d, turn - 1, n).wait_send()
            for n in range(3):
                to_chip(d, turn - 1, n).wait_send()

        if d == 0:
            @pl.when(turn == 0)
            def _():
                load_w.wait()

        for n, block in enumerate(tuple(other_core(peer) for peer in peers) + (sibling,)):
            sent[d, n] = matmul(pre[d], w[d, block], NT).astype(jnp.bfloat16)
            to_core(d, turn, n).start()
        for n, block in enumerate(peers + (me,)):
            share = matmul(pre[d], w[d, block], NT)
            to_core(d, turn, n).wait_recv()
            share += got[d, turn % 2, n].astype(jnp.float32)
            if n < 3:
                passed[d, n] = share.astype(jnp.bfloat16)
                to_chip(d, turn, n).start()
            else:
                own[d] = share

    def both(turn, carry):
        for d in range(2):
            half(turn, d)
        return carry

    lax.fori_loop(0, length, both, 0)
    for d in range(2):
        for n in range(3):
            to_chip(d, length - 1, n).wait_recv()
        total = held[d] + own[d]
        for n in range(3):
            total += taken[d, (length - 1) % 2, n].astype(jnp.float32)
        hidden_grad[d] = total
        save_pre(d, 0).wait()
        for n in range(4):
            to_core(d, length - 1, n).wait_send()
        for n in range(3):
            to_chip(d, length - 1, n).wait_send()


def kernel_recurrences(step_ids, own_len, h_init, c_init, embed, w_in, w_rec, bias, w_dec, wd_full, b_dec, count):
    length, rows = step_ids.shape[1:]
    letters, width = embed.shape[1:]
    units, columns = h_init.shape[2], w_rec.shape[2]
    blocks = w_rec.shape[1] // units
    any_space, vmem = pl.BlockSpec(memory_space=pl.ANY), pl.BlockSpec(memory_space=pltpu.VMEM)
    ids = jnp.swapaxes(step_ids, 1, 2).astype(jnp.float32)
    reach = jnp.broadcast_to(own_len.astype(jnp.float32)[None, :, None], (2, rows, 1))
    info = jnp.concatenate([ids, jnp.full((2, rows, LANES - 1 - length), -1.0, jnp.float32), reach], axis=2)
    pad_letters = VOCAB_PAD - letters
    embed_pad = jnp.pad(embed, ((0, 0), (0, pad_letters), (0, LANES - width)))
    w_in_pad = jnp.pad(w_in, ((0, 0), (0, LANES - width), (0, 0)))
    wd_pad = jnp.pad(wd_full, ((0, 0), (0, 0), (0, pad_letters))).reshape(2, blocks, units, VOCAB_PAD)
    w_dec_pad = jnp.pad(w_dec, ((0, 0), (0, 0), (0, pad_letters)))
    b_dec_pad = jnp.pad(b_dec, ((0, 0), (0, pad_letters)), constant_values=-1e30)[:, None]
    w_blocks = w_rec.reshape(2, blocks, units, columns)
    inverse = (1.0 / count).reshape(1, 1)
    f32, bf16 = jnp.float32, jnp.bfloat16
    dma = pltpu.SemaphoreType.DMA
    shape = jax.ShapeDtypeStruct
    wholes, acts, grads, loss, logit_sq, hidden_sq, dec_bias, dec_grad = pl.pallas_call(
        functools.partial(forward_kernel, length, letters),
        out_shape=(
            shape((length, 2, blocks, rows, units), bf16),
            shape((length, 2, 5, rows, units), f32),
            shape((length, 2, rows, VOCAB_PAD), bf16),
            shape((2, CHUNK, LANES), f32),
            shape((2, CHUNK, LANES), f32),
            shape((2, CHUNK, LANES), f32),
            shape((2, 8, VOCAB_PAD), f32),
            shape((2, units, VOCAB_PAD), f32),
        ),
        in_specs=[vmem, pl.BlockSpec(memory_space=pltpu.SMEM)] + [vmem] * 6 + [any_space] * 2,
        out_specs=(any_space,) * 3 + (vmem,) * 5,
        scratch_shapes=[
            pltpu.VMEM((2, blocks, units, columns), bf16),
            pltpu.VMEM((2, blocks, units, VOCAB_PAD), bf16),
            pltpu.VMEM((2, 3, blocks, rows, units), bf16),
            pltpu.VMEM((2, rows, units), f32),
            pltpu.VMEM((rows, columns), f32),
            pltpu.VMEM((rows, VOCAB_PAD), f32),
            pltpu.VMEM((2, 5, rows, units), f32),
            pltpu.VMEM((2, rows, VOCAB_PAD), bf16),
            dma((2,)),
            dma((2, 2, 7)),
            dma((2, 3, blocks)),
            dma((2, 2)),
            dma((2,)),
            dma((2,)),
        ],
        compiler_params=pltpu.CompilerParams(
            collective_id=0, has_side_effects=True, vmem_limit_bytes=VMEM_LIMIT
        ),
        name="forward_visits",
    )(info, inverse, h_init, c_init, embed_pad, w_in_pad, bias[:, None], b_dec_pad, wd_pad, w_blocks)
    pres, hidden_grad, cell_grad = pl.pallas_call(
        functools.partial(backward_kernel, length),
        out_shape=(
            shape((length, 2, rows, columns), bf16),
            shape((2, rows, units), f32),
            shape((2, rows, units), f32),
        ),
        in_specs=[vmem] * 2 + [any_space] * 3,
        out_specs=(any_space, vmem, vmem),
        scratch_shapes=[
            pltpu.VMEM((2, blocks, units, columns), bf16),
            pltpu.VMEM((2, 5, rows, units), f32),
            pltpu.VMEM((2, rows, VOCAB_PAD), bf16),
            pltpu.VMEM((2, rows, columns), bf16),
            pltpu.VMEM((2, rows, units), f32),
            pltpu.VMEM((2, rows, units), f32),
            pltpu.VMEM((2, 4, rows, units), bf16),
            pltpu.VMEM((2, 2, 4, rows, units), bf16),
            pltpu.VMEM((2, 3, rows, units), bf16),
            pltpu.VMEM((2, 2, 3, rows, units), bf16),
            dma,
            dma((2,)),
            dma((2,)),
            dma((2,)),
            dma((2, 4)),
            dma((2, 2, 4)),
            dma((2, 3)),
            dma((2, 2, 3)),
        ],
        compiler_params=pltpu.CompilerParams(
            collective_id=1, has_side_effects=True, vmem_limit_bytes=VMEM_LIMIT
        ),
        name="backward_visits",
    )(info, w_dec_pad, acts, grads, w_blocks)
    rec_grad = jnp.einsum("sdnbu,sdbc->dnuc", wholes, pres, preferred_element_type=f32)
    onehot = (jnp.swapaxes(step_ids, 0, 1)[..., None] == jnp.arange(letters, dtype=jnp.int32)).astype(bf16)
    letter_grad = jnp.einsum("sdbv,sdbc->dvc", onehot, pres, preferred_element_type=f32)
    return (
        jnp.sum(loss[:, :, 0]),
        jnp.sum(hidden_sq, axis=(1, 2)),
        jnp.sum(logit_sq, axis=(1, 2)),
        jnp.sum(dec_bias, axis=1)[:, :letters],
        dec_grad[:, :, :letters],
        hidden_grad,
        cell_grad,
        rec_grad.reshape(2, blocks * units, columns),
        letter_grad,
    )


def per_device(ids, lengths, order, h_init, c_init, embed, w_in, w_rec, bias, w_dec, b_dec):
    seq_rank = lax.axis_index("seq")
    first_mp = (lax.axis_index("mp") == 0).astype(jnp.float32)
    streams = ids.shape[1]
    per_dev = h_init.shape[1]
    own_units, all_units = h_init.shape[2], w_rec.shape[1]
    letter_count = embed.shape[1]
    wd_full = lax.all_gather(w_dec, "mp", axis=1, tiled=True)
    whole_ids = lax.all_gather(ids, "seq", axis=0, tiled=True)
    own_order = lax.dynamic_slice_in_dim(order, seq_rank * per_dev, per_dev)
    slot_ids = jnp.take(whole_ids, own_order, axis=1)
    own_len = jnp.take(lengths, own_order)
    live_total = jnp.sum(lengths).astype(jnp.float32)
    count = 2.0 * (jnp.sum(lengths) - streams).astype(jnp.float32)
    step_ids = jnp.stack([slot_ids, jnp.flip(slot_ids, 0)])
    lanes, matrix = column_order(own_units)
    w_rec_grouped = grouped(w_rec, matrix)
    w_in_grouped = grouped(w_in, matrix)
    bias_grouped = jnp.swapaxes(
        bias.reshape(2, own_units // lanes, lanes, 4), -1, -2
    ).reshape(bias.shape)
    operands = (
        step_ids, own_len, h_init, c_init, embed, w_in_grouped, w_rec_grouped, bias_grouped, w_dec, wd_full,
        b_dec, count,
    )
    if lax.axis_size("mp") == 8 and own_units % LANES == 0 and per_dev % CHUNK == 0:
        results = kernel_recurrences(*operands)
    else:
        results = recurrences(*operands, lanes)
    loss, hidden_sq, logit_sq, dec_bias, dec_grad, hidden_grad, cell_grad, rec_grad, letter_grad = results
    embed_wide = embed.astype(jnp.float32)
    in_grad = jnp.einsum("dve,dvc->dec", embed_wide, letter_grad, precision=lax.Precision.HIGHEST)
    bias_grad = jnp.sum(letter_grad, axis=1, keepdims=True)
    embed_part = jnp.einsum(
        "dvc,dec->dve", letter_grad, w_in_grouped.astype(jnp.float32), precision=lax.Precision.HIGHEST
    )
    edge = ungrouped_wide(jnp.concatenate([in_grad, bias_grad], axis=1), lanes)
    rec_part = lax.psum_scatter(rec_grad.astype(jnp.bfloat16), "seq", scatter_dimension=1, tiled=True)
    edge_part = lax.psum_scatter(edge.astype(jnp.bfloat16), "seq", scatter_dimension=2, tiled=True)
    dec_part = lax.psum_scatter(dec_grad.astype(jnp.bfloat16), "seq", scatter_dimension=1, tiled=True)
    loss_sum, hidden_all, logit_all, dec_bias_grad, embed_grad = lax.psum(
        (loss * first_mp, hidden_sq, logit_sq * first_mp, dec_bias * first_mp, embed_part), ("seq", "mp")
    )
    rec_out = ungrouped(rec_part, matrix).astype(jnp.float32)
    rms_embed = jnp.sqrt(jnp.mean(embed_wide * embed_wide, axis=(1, 2)))
    return (
        loss_sum / count,
        hidden_grad,
        cell_grad,
        embed_grad,
        edge_part[:, :-1].astype(jnp.float32),
        rec_out,
        edge_part[:, -1].astype(jnp.float32),
        dec_part.astype(jnp.float32),
        dec_bias_grad,
        rms_embed,
        jnp.sqrt(hidden_all / (all_units * live_total)),
        jnp.sqrt(logit_all / (letter_count * count / 2.0)),
    )


def solution(mesh):
    in_specs = (
        P("seq", None),
        P(),
        P(),
        P(None, "seq", "mp"),
        P(None, "seq", "mp"),
        P(),
        P(None, None, "mp"),
        P(None, None, "mp"),
        P(None, "mp"),
        P(None, "mp", None),
        P(),
    )
    out_specs = (
        P(),
        P(None, "seq", "mp"),
        P(None, "seq", "mp"),
        P(),
        P(None, None, ("mp", "seq")),
        P(None, "seq", "mp"),
        P(None, ("mp", "seq")),
        P(None, ("mp", "seq"), None),
        P(),
        P(),
        P(),
        P(),
    )
    return jax.shard_map(
        per_device, mesh=mesh, in_specs=in_specs, out_specs=out_specs, check_vma=False
    )
```

```python
import functools

import jax
import jax.numpy as jnp
from jax import lax
from jax.experimental import pallas as pl
from jax.experimental.pallas import tpu as pltpu
from jax.sharding import PartitionSpec as P

VMEM_LIMIT = 56 * 2**20


def column_order(own_units):
    lanes = min(128, own_units)
    source = jnp.arange(4 * lanes, dtype=jnp.int32)
    place = (source % 4) * lanes + source // 4
    matrix = (place[:, None] == jnp.arange(4 * lanes, dtype=jnp.int32)[None, :]).astype(jnp.bfloat16)
    return lanes, matrix


def grouped(x, matrix):
    width = matrix.shape[0]
    parts = x.reshape(x.shape[:-1] + (x.shape[-1] // width, width))
    out = jnp.einsum("...gc,cp->...gp", parts, matrix, preferred_element_type=jnp.float32)
    return out.astype(x.dtype).reshape(x.shape)


def ungrouped(x, matrix):
    return grouped(x, matrix.T)


def ungrouped_wide(x, lanes):
    parts = x.reshape(x.shape[:-1] + (x.shape[-1] // (4 * lanes), 4, lanes))
    return jnp.swapaxes(parts, -1, -2).reshape(x.shape)


def gates_of(pre, lanes):
    parts = pre.reshape(pre.shape[:-1] + (pre.shape[-1] // (4 * lanes), 4, lanes))
    flat = pre.shape[:-1] + (pre.shape[-1] // 4,)
    return tuple(parts[..., k, :].reshape(flat) for k in range(4))


def joined_gates(gates, lanes):
    split = [g.reshape(g.shape[:-1] + (g.shape[-1] // lanes, 1, lanes)) for g in gates]
    joined = jnp.concatenate(split, axis=-2)
    return joined.reshape(gates[0].shape[:-1] + (4 * gates[0].shape[-1],))


def recurrences(step_ids, own_len, h_init, c_init, embed, w_in, w_rec, bias, w_dec, wd_full, b_dec, count, lanes):
    length, per_dev = step_ids.shape[1:]
    letter_count = embed.shape[1]
    steps = jnp.arange(length, dtype=jnp.int32)
    live_steps = jnp.stack(
        [steps[:, None] < own_len[None, :], (length - 1 - steps)[:, None] < own_len[None, :]], axis=1
    )[..., None]
    letters = jnp.arange(letter_count, dtype=jnp.int32)
    onehot = (jnp.swapaxes(step_ids, 0, 1)[..., None] == letters).astype(jnp.bfloat16)
    letter_rows = jnp.einsum(
        "sdbv,dve->sdbe", onehot, embed, preferred_element_type=jnp.float32
    ).astype(jnp.bfloat16)
    gates_in = jnp.einsum(
        "sdbe,dec->sdbc", letter_rows, w_in, preferred_element_type=jnp.float32
    ).astype(jnp.bfloat16)

    def forward_step(carry, inputs):
        hidden, cell = carry
        gate_in, live = inputs
        whole = lax.all_gather(hidden, "mp", axis=2, tiled=True)
        recurrent = jnp.einsum("dbh,dhc->dbc", whole, w_rec, preferred_element_type=jnp.float32)
        pre = gate_in.astype(jnp.float32) + recurrent + bias[:, None]
        in_pre, forget_pre, cell_pre, out_pre = gates_of(pre, lanes)
        in_gate, forget, out_gate = (jax.nn.sigmoid(x) for x in (in_pre, forget_pre, out_pre))
        cell_gate = jnp.tanh(cell_pre)
        new_cell = forget * cell + in_gate * cell_gate
        cell_next = jnp.where(live, new_cell, cell)
        hidden_next = jnp.where(
            live, out_gate * jnp.tanh(new_cell), hidden.astype(jnp.float32)
        ).astype(jnp.bfloat16)
        return ((hidden_next, cell_next), (whole, cell, in_gate, forget, cell_gate, out_gate))

    (last_hidden, last_cell), (wholes, cells, *gates) = lax.scan(
        forward_step, (h_init, c_init), (gates_in, live_steps)
    )
    last_whole = lax.all_gather(last_hidden, "mp", axis=2, tiled=True)
    after = jnp.concatenate([wholes[1:], last_whole[None]], axis=0)
    own = h_init.shape[2]
    mine = lax.dynamic_slice_in_dim(after, lax.axis_index("mp") * own, own, axis=3)
    mine_wide = mine.astype(jnp.float32)
    hidden_sq = jnp.sum(jnp.where(live_steps, mine_wide * mine_wide, 0.0), axis=(0, 2, 3))
    logits = (
        jnp.einsum("sdbh,dhv->sdbv", after, wd_full, preferred_element_type=jnp.float32) + b_dec[None, :, None]
    )
    targets = jnp.swapaxes(jnp.concatenate([step_ids[:, 1:], step_ids[:, :1]], axis=1), 0, 1)
    fore_valid = (steps[:, None] + 1 < own_len[None, :])
    back_valid = (steps[:, None] < length - 1) & ((length - 1 - steps)[:, None] < own_len[None, :])
    valid = jnp.stack([fore_valid, back_valid], axis=1).astype(jnp.float32)
    logit_sq = jnp.sum(valid[..., None] * logits * logits, axis=(0, 2, 3))
    top = jnp.max(logits, axis=-1, keepdims=True)
    log_total = top + jnp.log(jnp.sum(jnp.exp(logits - top), axis=-1, keepdims=True))
    target_hot = targets[..., None] == letters
    picked = jnp.sum(jnp.where(target_hot, logits, 0.0), axis=-1)
    loss = jnp.sum(valid * (log_total[..., 0] - picked))
    grad_logits = (
        valid[..., None] * (jnp.exp(logits - log_total) - target_hot.astype(jnp.float32)) / count
    ).astype(jnp.bfloat16)
    dec_bias = jnp.sum(grad_logits.astype(jnp.float32), axis=(0, 2))
    dec_grad = jnp.einsum("sdbh,sdbv->dhv", mine, grad_logits, preferred_element_type=jnp.float32)

    def backward_step(carry, inputs):
        grad_hidden, grad_cell = carry
        live, cell, in_gate, forget, cell_gate, out_gate, grad_logit = inputs
        grad_hidden = grad_hidden + jnp.einsum(
            "dbv,dhv->dbh", grad_logit, w_dec, preferred_element_type=jnp.float32
        )
        squash = jnp.tanh(forget * cell + in_gate * cell_gate)
        grad_new = jnp.where(live, grad_cell + grad_hidden * out_gate * (1.0 - squash * squash), 0.0)
        grad_out = jnp.where(live, grad_hidden * squash, 0.0)
        grad_pre = joined_gates(
            [
                grad_new * cell_gate * in_gate * (1.0 - in_gate),
                grad_new * cell * forget * (1.0 - forget),
                grad_new * in_gate * (1.0 - cell_gate * cell_gate),
                grad_out * out_gate * (1.0 - out_gate),
            ],
            lanes,
        ).astype(jnp.bfloat16)
        grad_cell_prev = grad_new * forget + jnp.where(live, 0.0, grad_cell)
        held = jnp.where(live, 0.0, grad_hidden)
        terms = jnp.einsum("dbc,dhc->dbh", grad_pre, w_rec, preferred_element_type=jnp.float32)
        through = lax.psum_scatter(
            terms.astype(jnp.bfloat16), "mp", scatter_dimension=2, tiled=True
        ).astype(jnp.float32)
        return ((held + through, grad_cell_prev), grad_pre)

    start = jnp.zeros(c_init.shape, jnp.float32)
    (hidden_grad, cell_grad), grad_pres = lax.scan(
        backward_step, (start, start), (live_steps, cells, *gates, grad_logits), reverse=True
    )
    rec_grad = jnp.einsum("sdbh,sdbc->dhc", wholes, grad_pres, preferred_element_type=jnp.float32)
    letter_grad = jnp.einsum("sdbv,sdbc->dvc", onehot, grad_pres, preferred_element_type=jnp.float32)
    return loss, hidden_sq, logit_sq, dec_bias, dec_grad, hidden_grad, cell_grad, rec_grad, letter_grad


MESH = pl.DeviceIdType.MESH
LANES = 128
VOCAB_PAD = 384
CHUNK = 256
NT = (((1,), (1,)), ((), ()))
TN = (((0,), (0,)), ((), ()))


def sigmoid(x):
    return 0.5 * jnp.tanh(0.5 * x) + 0.5


def matmul(left, right, dims=(((1,), (0,)), ((), ()))):
    return lax.dot_general(left, right, dims, preferred_element_type=jnp.float32)


def neighbours():
    me = lax.axis_index("mp")
    row, column, core = me // 4, (me // 2) % 2, me % 2
    sibling = row * 4 + column * 2 + (1 - core)
    across = (1 - row) * 4 + (1 - column) * 2 + core
    side = row * 4 + (1 - column) * 2 + core
    up = (1 - row) * 4 + column * 2 + core
    return me, sibling, (across, side, up)


def greet(peers):
    seq = lax.axis_index("seq")
    barrier = pltpu.get_barrier_semaphore()
    for peer in peers:
        pl.semaphore_signal(barrier, inc=1, device_id=(seq, peer), device_id_type=MESH)
    pl.semaphore_wait(barrier, len(peers))


def remote(src, dst, send, recv, peer):
    return pltpu.make_async_remote_copy(
        src_ref=src, dst_ref=dst, send_sem=send, recv_sem=recv,
        device_id=(lax.axis_index("seq"), peer), device_id_type=MESH,
    )


def other_core(peer):
    return (peer // 2) * 2 + (1 - peer % 2)


def folded(x):
    return jnp.sum(x.reshape(x.shape[0] // 8, 8, x.shape[1]), axis=0)


def column_of(table, lane):
    lanes = lax.broadcasted_iota(jnp.int32, table.shape, 1)
    return jnp.sum(jnp.where(lanes == lane, table, 0.0), axis=1, keepdims=True)


def time_of(direction, step, length):
    return step if direction == 0 else length - 1 - step


def forward_kernel(
    length, letters, info, inverse, h_in, c_in, embed, w_in, bias, b_dec, wd_hbm, w_hbm,
    wholes, acts, grads, loss, logit_sq, hidden_sq, dec_bias, dec_grad,
    w, wd, buf, cell, acc, logit, stage, grad, load_sem, send_sem, recv_sem, save_sem, act_sem, grad_sem,
):
    me, sibling, peers = neighbours()
    blocks, rows, units = buf.shape[2:]
    groups = units // LANES
    load_w = pltpu.make_async_copy(w_hbm, w, load_sem.at[0])
    load_wd = pltpu.make_async_copy(wd_hbm, wd, load_sem.at[1])
    load_w.start()
    load_wd.start()
    greet((sibling,) + peers)
    for ref in (loss, logit_sq, hidden_sq, dec_bias, dec_grad):
        ref[...] = jnp.zeros(ref.shape, ref.dtype)
    cell[...] = c_in[...]

    def direct(d, step):
        slot, par = step % 3, step % 2
        block = buf.at[d, slot, me]
        return [
            remote(block, block, send_sem.at[d, par, n], recv_sem.at[d, slot, me], peer)
            for n, peer in enumerate(peers + (sibling,))
        ]

    def relay(d, step, n):
        slot, par = step % 3, step % 2
        block = buf.at[d, slot, peers[n]]
        return remote(block, block, send_sem.at[d, par, 4 + n], recv_sem.at[d, slot, peers[n]], sibling)

    def arrival(d, step, source):
        slot = step % 3
        block = buf.at[d, slot, source]
        return remote(block, block, send_sem.at[d, step % 2, 0], recv_sem.at[d, slot, source], sibling)

    def save(d, step):
        return pltpu.make_async_copy(buf.at[d, step % 3], wholes.at[step, d], save_sem.at[d, step % 2])

    def save_acts(d, step):
        return pltpu.make_async_copy(stage.at[d], acts.at[step, d], act_sem.at[d])

    def save_grad(d, step):
        return pltpu.make_async_copy(grad.at[d], grads.at[step, d], grad_sem.at[d])

    def finish_sends(d, step):
        for copy in direct(d, step):
            copy.wait_send()
        for n in range(3):
            relay(d, step, n).wait_send()

    def gates(d, step):
        slot, later = step % 3, (step + 1) % 3
        when = time_of(d, step, length)

        def chunk(i, carry):
            at = pl.ds(pl.multiple_of(i * CHUNK, CHUNK), CHUNK)
            live = info[d, at, LANES - 1:LANES] > when.astype(jnp.float32)
            for g in range(groups):
                lanes = slice(g * LANES, (g + 1) * LANES)
                pre = [acc[at, (4 * g + k) * LANES:(4 * g + k + 1) * LANES] for k in range(4)]
                in_gate, forget, out_gate = sigmoid(pre[0]), sigmoid(pre[1]), sigmoid(pre[3])
                cell_gate = jnp.tanh(pre[2])
                old = cell[d, at, lanes]
                new = forget * old + in_gate * cell_gate
                for k, value in enumerate((in_gate, forget, cell_gate, out_gate, old)):
                    stage[d, k, at, lanes] = value
                cell[d, at, lanes] = jnp.where(live, new, old)
                before = buf[d, slot, me, at, lanes].astype(jnp.float32)
                hidden = jnp.where(live, out_gate * jnp.tanh(new), before).astype(jnp.bfloat16)
                buf[d, later, me, at, lanes] = hidden
                wide = hidden.astype(jnp.float32)
                hidden_sq[d] += folded(jnp.where(live, wide * wide, 0.0))
            return carry

        lax.fori_loop(0, rows // CHUNK, chunk, 0)

    def decode(d, step):
        slot = step % 3
        total = jnp.broadcast_to(b_dec[d], logit.shape)
        for b in range(blocks):
            total += matmul(buf[d, slot, b], wd[d, b])
        logit[...] = total
        when = time_of(d, step - 1, length)
        reach = when + 1 if d == 0 else when
        scale = inverse[0, 0]

        def chunk(i, carry):
            at = pl.ds(pl.multiple_of(i * CHUNK, CHUNK), CHUNK)
            table = info[d, at, :]
            valid = (table[:, LANES - 1:LANES] > reach.astype(jnp.float32)) & (step < length)
            target = column_of(table, step)
            value = logit[at, :]
            lanes = lax.broadcasted_iota(jnp.int32, value.shape, 1)
            hot = lanes.astype(jnp.float32) == target
            top = jnp.max(value, axis=1, keepdims=True)
            power = jnp.exp(value - top)
            total = jnp.sum(power, axis=1, keepdims=True)
            picked = jnp.sum(jnp.where(hot, value, 0.0), axis=1, keepdims=True)
            loss[d] += folded(jnp.broadcast_to(jnp.where(valid, top + jnp.log(total) - picked, 0.0), (CHUNK, LANES)))
            kept = jnp.where(valid & (lanes < letters), value, 0.0)
            square = kept * kept
            logit_sq[d] += folded(sum(square[:, n * LANES:(n + 1) * LANES] for n in range(VOCAB_PAD // LANES)))
            slope = jnp.where(
                valid, (power * (1.0 / total) - jnp.where(hot, 1.0, 0.0)) * scale, 0.0
            ).astype(jnp.bfloat16)
            grad[d, at, :] = slope
            wide = slope.astype(jnp.float32)
            dec_bias[d] += folded(wide)
            return carry

        lax.fori_loop(0, rows // CHUNK, chunk, 0)
        dec_grad[d] += matmul(buf[d, slot, me], grad[d], TN)

    def half(step, d):
        @pl.when(step < length)
        def _():
            ids = column_of(info[d], step)
            hot = (lax.broadcasted_iota(jnp.int32, (rows, VOCAB_PAD), 1).astype(jnp.float32) == ids)
            row = matmul(hot.astype(jnp.bfloat16), embed[d]).astype(jnp.bfloat16)
            acc[...] = matmul(row, w_in[d]).astype(jnp.bfloat16).astype(jnp.float32) + bias[d]

        for n, peer in enumerate(peers):
            arrival(d, step, peer).wait_recv()
            relay(d, step, n).start()

        if d == 0:
            @pl.when(step == 0)
            def _():
                load_w.wait()
                load_wd.wait()

        slot = step % 3

        def advance(block):
            acc[...] += matmul(buf[d, slot, block], w[d, block])

        @pl.when(step < length)
        def _():
            for block in (me,) + peers:
                advance(block)

        for block in (sibling,) + tuple(other_core(peer) for peer in peers):
            arrival(d, step, block).wait_recv()

        @pl.when(step < length)
        def _():
            save(d, step).start()
            for block in (sibling,) + tuple(other_core(peer) for peer in peers):
                advance(block)

            @pl.when(step > 0)
            def _():
                save_acts(d, step - 1).wait()

            gates(d, step)
            save_acts(d, step).start()

            @pl.when(step > 0)
            def _():
                save(d, step - 1).wait()
                finish_sends(d, step - 1)

            for copy in direct(d, step + 1):
                copy.start()

        @pl.when(step > 0)
        def _():
            @pl.when(step > 1)
            def _():
                save_grad(d, step - 2).wait()

            decode(d, step)
            save_grad(d, step - 1).start()

    for d in range(2):
        buf[d, 0, me] = h_in[d]
        for copy in direct(d, 0):
            copy.start()

    def both(step, carry):
        for d in range(2):
            half(step, d)
        return carry

    lax.fori_loop(0, length + 1, both, 0)
    for d in range(2):
        save(d, length - 1).wait()
        save_acts(d, length - 1).wait()
        save_grad(d, length - 1).wait()
        finish_sends(d, length - 1)
        finish_sends(d, length)


def backward_kernel(
    length, info, ids, w_dec, acts, grads, wholes, w_hbm,
    rec_out, letter_grad, hidden_grad, cell_grad,
    w, rec, stage, grad, whole, pre, held, own, sent, got, passed, taken, load_sem, act_sem, grad_sem, whole_sem,
    core_send, core_recv, chip_send, chip_recv,
):
    me, sibling, peers = neighbours()
    rows, units = held.shape[1:]
    groups = units // LANES
    load_w = pltpu.make_async_copy(w_hbm, w, load_sem)
    load_w.start()

    def load_acts(d, step):
        return pltpu.make_async_copy(acts.at[step, d], stage.at[d], act_sem.at[d])

    def load_grad(d, step):
        return pltpu.make_async_copy(grads.at[step, d], grad.at[d], grad_sem.at[d])

    def load_whole(d, step):
        return pltpu.make_async_copy(wholes.at[step, d], whole.at[d], whole_sem.at[d])

    for d in range(2):
        load_acts(d, length - 1).start()
        load_grad(d, length - 1).start()
        load_whole(d, length - 1).start()
    greet((sibling,) + peers)
    held[...] = jnp.zeros(held.shape, held.dtype)
    own[...] = jnp.zeros(own.shape, own.dtype)
    cell_grad[...] = jnp.zeros(cell_grad.shape, cell_grad.dtype)
    letter_grad[...] = jnp.zeros(letter_grad.shape, letter_grad.dtype)

    def clear(b, carry):
        for d in range(2):
            rec[d, b] = jnp.zeros(rec.shape[2:], rec.dtype)
        return carry

    lax.fori_loop(0, w.shape[1], clear, 0)

    def to_core(d, turn, n):
        return remote(
            sent.at[d, n], got.at[d, turn % 2, n], core_send.at[d, n], core_recv.at[d, turn % 2, n], sibling
        )

    def to_chip(d, turn, n):
        return remote(
            passed.at[d, n], taken.at[d, turn % 2, n], chip_send.at[d, n], chip_recv.at[d, turn % 2, n], peers[n]
        )

    def half(turn, d):
        step = length - 1 - turn
        when = time_of(d, step, length)
        load_acts(d, step).wait()
        load_grad(d, step).wait()
        held[d] += matmul(grad[d], w_dec[d], NT)

        @pl.when(turn > 0)
        def _():
            for n in range(3):
                to_chip(d, turn - 1, n).wait_recv()

        def chunk(i, carry):
            at = pl.ds(pl.multiple_of(i * CHUNK, CHUNK), CHUNK)
            live = info[d, at, LANES - 1:LANES] > when.astype(jnp.float32)
            for g in range(groups):
                lanes = slice(g * LANES, (g + 1) * LANES)
                through = own[d, at, lanes]
                for n in range(3):
                    through += jnp.where(turn > 0, taken[d, (turn + 1) % 2, n, at, lanes].astype(jnp.float32), 0.0)
                total = held[d, at, lanes] + through
                in_gate, forget, cell_gate, out_gate, old = (stage[d, k, at, lanes] for k in range(5))
                squash = jnp.tanh(forget * old + in_gate * cell_gate)
                later = cell_grad[d, at, lanes]
                new = jnp.where(live, later + total * out_gate * (1.0 - squash * squash), 0.0)
                out = jnp.where(live, total * squash, 0.0)
                values = (
                    new * cell_gate * in_gate * (1.0 - in_gate),
                    new * old * forget * (1.0 - forget),
                    new * in_gate * (1.0 - cell_gate * cell_gate),
                    out * out_gate * (1.0 - out_gate),
                )
                for k, value in enumerate(values):
                    pre[d, at, (4 * g + k) * LANES:(4 * g + k + 1) * LANES] = value.astype(jnp.bfloat16)
                cell_grad[d, at, lanes] = new * forget + jnp.where(live, 0.0, later)
                held[d, at, lanes] = jnp.where(live, 0.0, total)
            return carry

        lax.fori_loop(0, rows // CHUNK, chunk, 0)

        @pl.when(turn < length - 1)
        def _():
            load_acts(d, step - 1).start()
            load_grad(d, step - 1).start()

        @pl.when(turn > 0)
        def _():
            for n in range(4):
                to_core(d, turn - 1, n).wait_send()
            for n in range(3):
                to_chip(d, turn - 1, n).wait_send()

        if d == 0:
            @pl.when(turn == 0)
            def _():
                load_w.wait()

        for n, block in enumerate(tuple(other_core(peer) for peer in peers) + (sibling,)):
            sent[d, n] = matmul(pre[d], w[d, block], NT).astype(jnp.bfloat16)
            to_core(d, turn, n).start()
        for n, block in enumerate(peers + (me,)):
            share = matmul(pre[d], w[d, block], NT)
            to_core(d, turn, n).wait_recv()
            share += got[d, turn % 2, n].astype(jnp.float32)
            if n < 3:
                passed[d, n] = share.astype(jnp.bfloat16)
                to_chip(d, turn, n).start()
            else:
                own[d] = share
        load_whole(d, step).wait()

        for b in range(w.shape[1]):
            rec[d, b] += matmul(whole[d, b], pre[d], TN)

        @pl.when(turn < length - 1)
        def _():
            load_whole(d, step - 1).start()

        letters = lax.broadcasted_iota(jnp.int32, (VOCAB_PAD, rows), 0).astype(jnp.float32)
        hot = letters == ids[d, pl.ds(step, 1), :]
        letter_grad[d] += matmul(hot.astype(jnp.bfloat16), pre[d])

    def both(turn, carry):
        for d in range(2):
            half(turn, d)
        return carry

    lax.fori_loop(0, length, both, 0)
    for d in range(2):
        for n in range(3):
            to_chip(d, length - 1, n).wait_recv()
        total = held[d] + own[d]
        for n in range(3):
            total += taken[d, (length - 1) % 2, n].astype(jnp.float32)
        hidden_grad[d] = total
        for n in range(4):
            to_core(d, length - 1, n).wait_send()
        for n in range(3):
            to_chip(d, length - 1, n).wait_send()

    def narrow(b, carry):
        for d in range(2):
            w[d, b] = rec[d, b].astype(jnp.bfloat16)
        return carry

    lax.fori_loop(0, w.shape[1], narrow, 0)
    store = pltpu.make_async_copy(w, rec_out, load_sem)
    store.start()
    store.wait()


def kernel_step(step_ids, own_len, h_init, c_init, embed, w_in, w_rec, bias, w_dec, wd_full, b_dec, count, matrix):
    length, rows = step_ids.shape[1:]
    letters, width = embed.shape[1:]
    units, columns = h_init.shape[2], w_rec.shape[2]
    blocks = w_rec.shape[1] // units
    any_space, vmem = pl.BlockSpec(memory_space=pl.ANY), pl.BlockSpec(memory_space=pltpu.VMEM)
    ids = jnp.swapaxes(step_ids, 1, 2).astype(jnp.float32)
    reach = jnp.broadcast_to(own_len.astype(jnp.float32)[None, :, None], (2, rows, 1))
    info = jnp.concatenate([ids, jnp.full((2, rows, LANES - 1 - length), -1.0, jnp.float32), reach], axis=2)
    pad_letters = VOCAB_PAD - letters
    embed_pad = jnp.pad(embed, ((0, 0), (0, pad_letters), (0, LANES - width)))
    w_in_pad = jnp.pad(w_in, ((0, 0), (0, LANES - width), (0, 0)))
    wd_pad = jnp.pad(wd_full, ((0, 0), (0, 0), (0, pad_letters))).reshape(2, blocks, units, VOCAB_PAD)
    w_dec_pad = jnp.pad(w_dec, ((0, 0), (0, 0), (0, pad_letters)))
    b_dec_pad = jnp.pad(b_dec, ((0, 0), (0, pad_letters)), constant_values=-1e30)[:, None]
    w_blocks = w_rec.reshape(2, blocks, units, columns)
    inverse = (1.0 / count).reshape(1, 1)
    f32, bf16 = jnp.float32, jnp.bfloat16
    dma = pltpu.SemaphoreType.DMA
    shape = jax.ShapeDtypeStruct
    wholes, acts, grads, loss, logit_sq, hidden_sq, dec_bias, dec_grad = pl.pallas_call(
        functools.partial(forward_kernel, length, letters),
        out_shape=(
            shape((length, 2, blocks, rows, units), bf16),
            shape((length, 2, 5, rows, units), f32),
            shape((length, 2, rows, VOCAB_PAD), bf16),
            shape((2, 8, LANES), f32),
            shape((2, 8, LANES), f32),
            shape((2, 8, LANES), f32),
            shape((2, 8, VOCAB_PAD), f32),
            shape((2, units, VOCAB_PAD), f32),
        ),
        in_specs=[vmem, pl.BlockSpec(memory_space=pltpu.SMEM)] + [vmem] * 6 + [any_space] * 2,
        out_specs=(any_space,) * 3 + (vmem,) * 5,
        scratch_shapes=[
            pltpu.VMEM((2, blocks, units, columns), bf16),
            pltpu.VMEM((2, blocks, units, VOCAB_PAD), bf16),
            pltpu.VMEM((2, 3, blocks, rows, units), bf16),
            pltpu.VMEM((2, rows, units), f32),
            pltpu.VMEM((rows, columns), f32),
            pltpu.VMEM((rows, VOCAB_PAD), f32),
            pltpu.VMEM((2, 5, rows, units), f32),
            pltpu.VMEM((2, rows, VOCAB_PAD), bf16),
            dma((2,)),
            dma((2, 2, 7)),
            dma((2, 3, blocks)),
            dma((2, 2)),
            dma((2,)),
            dma((2,)),
        ],
        compiler_params=pltpu.CompilerParams(
            collective_id=0, has_side_effects=True, vmem_limit_bytes=VMEM_LIMIT
        ),
        name="forward_visits",
    )(info, inverse, h_init, c_init, embed_pad, w_in_pad, bias[:, None], b_dec_pad, wd_pad, w_blocks)
    rec_grad, letter_grad, hidden_grad, cell_grad = pl.pallas_call(
        functools.partial(backward_kernel, length),
        out_shape=(
            shape((2, blocks, units, columns), bf16),
            shape((2, VOCAB_PAD, columns), f32),
            shape((2, rows, units), f32),
            shape((2, rows, units), f32),
        ),
        in_specs=[vmem] * 3 + [any_space] * 4,
        out_specs=(any_space, vmem, vmem, vmem),
        scratch_shapes=[
            pltpu.VMEM((2, blocks, units, columns), bf16),
            pltpu.VMEM((2, blocks, units, columns), f32),
            pltpu.VMEM((2, 5, rows, units), f32),
            pltpu.VMEM((2, rows, VOCAB_PAD), bf16),
            pltpu.VMEM((2, blocks, rows, units), bf16),
            pltpu.VMEM((2, rows, columns), bf16),
            pltpu.VMEM((2, rows, units), f32),
            pltpu.VMEM((2, rows, units), f32),
            pltpu.VMEM((2, 4, rows, units), bf16),
            pltpu.VMEM((2, 2, 4, rows, units), bf16),
            pltpu.VMEM((2, 3, rows, units), bf16),
            pltpu.VMEM((2, 2, 3, rows, units), bf16),
            dma,
            dma((2,)),
            dma((2,)),
            dma((2,)),
            dma((2, 4)),
            dma((2, 2, 4)),
            dma((2, 3)),
            dma((2, 2, 3)),
        ],
        compiler_params=pltpu.CompilerParams(
            collective_id=1, has_side_effects=True, vmem_limit_bytes=VMEM_LIMIT
        ),
        name="backward_visits",
    )(info, step_ids.astype(f32), w_dec_pad, acts, grads, wholes, w_blocks)
    rec_part, edge_part, dec_part, small = kernel_sums(
        rec_grad, letter_grad, embed_pad, w_in_pad, matrix, width, letters, dec_grad,
        (loss, logit_sq, hidden_sq, dec_bias),
    )
    at = 2 * TABLE
    return (
        small[at, 0],
        jnp.sum(small[at + 3:at + 5], axis=1),
        jnp.sum(small[at + 1:at + 3], axis=1),
        small[at + 5:at + 5 + 2 * (VOCAB_PAD // LANES)].reshape(2, VOCAB_PAD)[:, :letters],
        dec_part[:, :, :letters],
        hidden_grad,
        cell_grad,
        rec_part.reshape(2, -1, columns),
        edge_part[:, :width],
        edge_part[:, width],
        small[:at].reshape(2, TABLE, LANES)[:, :letters, :width],
    )


PIECE = 128
LAG = 3
WINDOW = 3
TABLE = 280


def spread(letter_grad, other, dims):
    high = letter_grad.astype(jnp.bfloat16)
    low = (letter_grad - high.astype(jnp.float32)).astype(jnp.bfloat16)
    return matmul(high, other, dims) + matmul(low, other, dims)


def reduce_kernel(
    width, rec_hbm, letter_grad, embed, w_in, matrix, dec_grad, loss, logit_sq, hidden_sq, dec_bias,
    rec_out, edge_out, dec_out, small_out,
    own, ahead, behind, edge, edge_in, dec, dec_in, small, part, small_in, part_in, summed,
    load_sem, line_send, line_recv, back_send, back_recv, edge_send, edge_recv, dec_send, dec_recv,
    scatter_send, scatter_recv, seq_send, seq_recv, gather_send, gather_recv,
):
    seq, me = lax.axis_index("seq"), lax.axis_index("mp")
    count, parts = own.shape[1], own.shape[2]
    peers = lax.axis_size("mp")
    share = small.shape[0] // peers
    half = seq // (count // 2)
    place = seq + half * (count - 1 - 2 * seq)
    onward = 1 - 2 * half
    inner = count // 2 - 1
    lag = LAG + (inner - place) * 5
    load = pltpu.make_async_copy(rec_hbm, own, load_sem)
    load.start()

    def other_seq(n):
        return (seq + n) % count

    def other_mp(n):
        return (me + n) % peers

    barrier = pltpu.get_barrier_semaphore()
    for n in range(1, count):
        pl.semaphore_signal(barrier, inc=1, device_id=(other_seq(n), me), device_id_type=MESH)
    for n in range(1, peers):
        pl.semaphore_signal(barrier, inc=1, device_id=(seq, other_mp(n)), device_id_type=MESH)
    pl.semaphore_wait(barrier, count + peers - 2)
    load.wait()

    def send(src, dst, send_sem, recv_sem, seq_to, mp_to):
        return pltpu.make_async_remote_copy(
            src_ref=src, dst_ref=dst, send_sem=send_sem, recv_sem=recv_sem,
            device_id=(seq_to, mp_to), device_id_type=MESH,
        )

    def actual(chunk):
        return chunk + half * (count - 1 - 2 * chunk)

    pieces = 2 * parts

    def slot(k):
        return k // pieces, (k % pieces) // parts, k % parts

    def piece(chunk, d, r):
        return own.at[d, actual(chunk), r]

    def line_copy(k, crossing):
        i, d, r = slot(k)
        target = behind.at[i, d, r] if crossing else ahead.at[i, d, r]
        sem = back_recv.at[i, d, r] if crossing else line_recv.at[i, d, r]
        return send(piece(count - 1 - i, d, r), target, line_send.at[i, d, r], sem, seq + onward, me)

    def back_copy(k):
        i, d, r = slot(k)
        return send(
            piece(i, d, r), behind.at[i, d, r], back_send.at[i, d, r], back_recv.at[i, d, r], seq - onward, me
        )

    def add(chunk, d, r, term):
        ref = piece(chunk, d, r)
        ref[...] = (ref[...].astype(jnp.float32) + term[...].astype(jnp.float32)).astype(jnp.bfloat16)

    def line(k):
        i, d, r = slot(k)

        @pl.when((place > 0) & (i <= count - 1 - place))
        def _():
            line_copy(k, False).wait_recv()
            add(count - 1 - i, d, r, ahead.at[i, d, r])

        @pl.when((place == 0) & (k >= WINDOW))
        def _():
            line_copy(k - WINDOW, False).wait_send()

        @pl.when((i <= count - 2 - place) & (place < inner))
        def _():
            line_copy(k, False).start()

        @pl.when((i <= count - 2 - place) & (place == inner))
        def _():
            line_copy(k, True).start()

    def back(k):
        i, d, r = slot(k)

        @pl.when(i <= place)
        def _():
            back_copy(k).wait_recv()
            add(i, d, r, behind.at[i, d, r])

        @pl.when(i < place)
        def _():
            back_copy(k).start()

    def advance(k, carry):
        @pl.when(k < (count - 1) * pieces)
        def _():
            line(k)

        @pl.when((k >= lag) & (k - lag < (count // 2) * pieces))
        def _():
            back(k - lag)

        return carry

    def edge_copy(n):
        to = other_seq(n)
        return send(edge.at[to], edge_in.at[n - 1], edge_send.at[n - 1], edge_recv.at[n - 1], to, me)

    def dec_copy(n):
        to = other_seq(n)
        return send(dec.at[to], dec_in.at[n - 1], dec_send.at[n - 1], dec_recv.at[n - 1], to, me)

    def scatter_copy(n):
        to = other_mp(n)
        rows = pl.ds(pl.multiple_of(to * share, 8), share)
        return send(small.at[rows], small_in.at[n - 1], scatter_send.at[n - 1], scatter_recv.at[n - 1], seq, to)

    def seq_copy(n):
        return send(part, part_in.at[n - 1], seq_send.at[n - 1], seq_recv.at[n - 1], other_seq(n), me)

    own_rows = pl.ds(pl.multiple_of(me * share, 8), share)

    def gather_copy(n):
        return send(
            summed.at[own_rows], summed.at[own_rows], gather_send.at[n - 1], gather_recv.at[me], seq, other_mp(n)
        )

    def gather_arrival(n):
        source = other_mp(n)
        rows = pl.ds(pl.multiple_of(source * share, 8), share)
        return send(summed.at[rows], summed.at[rows], gather_send.at[n - 1], gather_recv.at[source], seq, source)

    start = 6
    lax.fori_loop(0, 2, advance, 0)
    first = jnp.where(me == 0, 1.0, 0.0)
    for d in range(2):
        small[d * TABLE:(d + 1) * TABLE] = spread(letter_grad[d], w_in[d], NT)[:TABLE]
    small[2 * TABLE:] = jnp.zeros((small.shape[0] - 2 * TABLE, LANES), jnp.float32)
    at = 2 * TABLE
    small[at:at + 1] = jnp.sum(loss[0] + loss[1], axis=0, keepdims=True) * first
    for d in range(2):
        small[at + 1 + d:at + 2 + d] = jnp.sum(logit_sq[d], axis=0, keepdims=True) * first
        small[at + 3 + d:at + 4 + d] = jnp.sum(hidden_sq[d], axis=0, keepdims=True)
        row = jnp.sum(dec_bias[d], axis=0, keepdims=True) * first
        for n in range(VOCAB_PAD // LANES):
            line_at = at + 5 + d * (VOCAB_PAD // LANES) + n
            small[line_at:line_at + 1] = row[:, n * LANES:(n + 1) * LANES]
    for n in range(1, peers):
        scatter_copy(n).start()
    rows = edge.shape[2]
    span = matrix.shape[0]
    wide = own.shape[-1] // count
    for d in range(2):
        full = spread_left(embed[d], letter_grad[d]).astype(jnp.bfloat16)
        flat = [
            matmul(full[:, g * span:(g + 1) * span], matrix[...], NT).astype(jnp.bfloat16)
            for g in range(own.shape[-1] // span)
        ]
        for q in range(count):
            group, offset = (q * wide) // span, (q * wide) % span
            edge[q, d] = flat[group][:rows, offset:offset + wide]
            depth = dec.shape[2]
            dec[q, d] = dec_grad[d, q * depth:(q + 1) * depth].astype(jnp.bfloat16)
    for n in range(1, count):
        edge_copy(n).start()
        dec_copy(n).start()
    lax.fori_loop(2, start, advance, 0)
    for n in range(1, peers):
        scatter_copy(n).wait()
    total = small[own_rows, :]
    for n in range(1, peers):
        total += small_in[n - 1]
    part[...] = total
    for n in range(1, count):
        seq_copy(n).start()
    lax.fori_loop(start, 2 * start, advance, 0)
    for n in range(1, count):
        seq_copy(n).wait()
        total += part_in[n - 1]
    summed[own_rows, :] = total
    for n in range(1, peers):
        gather_copy(n).start()
    lax.fori_loop(2 * start, (count - 1) * pieces + LAG, advance, 0)
    for n in range(1, peers):
        gather_copy(n).wait_send()
        gather_arrival(n).wait_recv()
    small_out[...] = summed[...]
    for n in range(1, count):
        edge_copy(n).wait()
        dec_copy(n).wait()
    for d in range(2):
        edge_out[d] = edge[seq, d].astype(jnp.float32) + sum(
            edge_in[n, d].astype(jnp.float32) for n in range(count - 1)
        )
        dec_out[d] = dec[seq, d].astype(jnp.float32) + sum(
            dec_in[n, d].astype(jnp.float32) for n in range(count - 1)
        )
        for r in range(parts):
            for g in range(own.shape[-1] // span):
                columns = slice(g * span, (g + 1) * span)
                rec_out[d, r, :, columns] = matmul(own[d, seq, r, :, columns], matrix[...], NT)

    def finish(k, carry):
        i, d, r = slot(k)

        @pl.when((i <= count - 2 - place) & ((place > 0) | (k >= (count - 1) * pieces - WINDOW)))
        def _():
            line_copy(k, False).wait_send()

        @pl.when((i < place) & (k < (count // 2) * pieces))
        def _():
            back_copy(k).wait_send()

        return carry

    lax.fori_loop(0, (count - 1) * pieces, finish, 0)


def spread_left(other, letter_grad):
    high = letter_grad.astype(jnp.bfloat16)
    low = (letter_grad - high.astype(jnp.float32)).astype(jnp.bfloat16)
    return matmul(other, high, TN) + matmul(other, low, TN)


def kernel_sums(rec_grad, letter_grad, embed_pad, w_in_pad, matrix, width, letters, dec_grad, stats):
    count = lax.axis_size("seq")
    peers = lax.axis_size("mp")
    columns = rec_grad.shape[-1]
    all_rows = rec_grad.shape[1] * rec_grad.shape[2]
    parts = all_rows // count // PIECE
    units = dec_grad.shape[1]
    edge_rows = -(-(width + 1) // 8) * 8
    small_rows = -(-(2 * TABLE + 16) // (8 * peers)) * 8 * peers
    share = small_rows // peers
    f32, bf16 = jnp.float32, jnp.bfloat16
    dma = pltpu.SemaphoreType.DMA
    shape = jax.ShapeDtypeStruct
    vmem = pl.BlockSpec(memory_space=pltpu.VMEM)
    ones = (jnp.arange(VOCAB_PAD) < letters).astype(bf16)
    embed_one = embed_pad.at[:, :, width].set(ones[None])
    return pl.pallas_call(
        functools.partial(reduce_kernel, width),
        out_shape=(
            shape((2, parts, PIECE, columns), f32),
            shape((2, edge_rows, columns // count), f32),
            shape((2, units // count, VOCAB_PAD), f32),
            shape((small_rows, LANES), f32),
        ),
        in_specs=[pl.BlockSpec(memory_space=pl.ANY)] + [vmem] * 9,
        out_specs=(vmem,) * 4,
        scratch_shapes=[
            pltpu.VMEM((2, count, parts, PIECE, columns), bf16),
            pltpu.VMEM((count - 1, 2, parts, PIECE, columns), bf16),
            pltpu.VMEM((count // 2, 2, parts, PIECE, columns), bf16),
            pltpu.VMEM((count, 2, edge_rows, columns // count), bf16),
            pltpu.VMEM((count - 1, 2, edge_rows, columns // count), bf16),
            pltpu.VMEM((count, 2, units // count, VOCAB_PAD), bf16),
            pltpu.VMEM((count - 1, 2, units // count, VOCAB_PAD), bf16),
            pltpu.VMEM((small_rows, LANES), f32),
            pltpu.VMEM((share, LANES), f32),
            pltpu.VMEM((peers - 1, share, LANES), f32),
            pltpu.VMEM((count - 1, share, LANES), f32),
            pltpu.VMEM((small_rows, LANES), f32),
            dma,
            dma((count - 1, 2, parts)),
            dma((count - 1, 2, parts)),
            dma((count // 2, 2, parts)),
            dma((count // 2, 2, parts)),
            dma((count - 1,)),
            dma((count - 1,)),
            dma((count - 1,)),
            dma((count - 1,)),
            dma((peers - 1,)),
            dma((peers - 1,)),
            dma((count - 1,)),
            dma((count - 1,)),
            dma((peers - 1,)),
            dma((peers,)),
        ],
        compiler_params=pltpu.CompilerParams(
            collective_id=2, has_side_effects=True, vmem_limit_bytes=VMEM_LIMIT
        ),
        name="gradient_sums",
    )(
        rec_grad.reshape(2, count, parts, PIECE, columns), letter_grad, embed_one, w_in_pad, matrix, dec_grad,
        *stats,
    )


def plain_step(
    step_ids, own_len, h_init, c_init, embed, w_in, w_rec, bias, w_dec, wd_full, b_dec, count, matrix
):
    lanes = matrix.shape[0] // 4
    first_mp = (lax.axis_index("mp") == 0).astype(jnp.float32)
    loss, hidden_sq, logit_sq, dec_bias, dec_grad, hidden_grad, cell_grad, rec_grad, letter_grad = recurrences(
        step_ids, own_len, h_init, c_init, embed, w_in, w_rec, bias, w_dec, wd_full,
        b_dec, count, lanes,
    )
    embed_wide = embed.astype(jnp.float32)
    in_grad = jnp.einsum("dve,dvc->dec", embed_wide, letter_grad, precision=lax.Precision.HIGHEST)
    bias_grad = jnp.sum(letter_grad, axis=1, keepdims=True)
    embed_part = jnp.einsum(
        "dvc,dec->dve", letter_grad, w_in.astype(jnp.float32), precision=lax.Precision.HIGHEST
    )
    edge = ungrouped_wide(jnp.concatenate([in_grad, bias_grad], axis=1), lanes)
    rec_part = lax.psum_scatter(rec_grad.astype(jnp.bfloat16), "seq", scatter_dimension=1, tiled=True)
    edge_part = lax.psum_scatter(edge.astype(jnp.bfloat16), "seq", scatter_dimension=2, tiled=True)
    dec_part = lax.psum_scatter(dec_grad.astype(jnp.bfloat16), "seq", scatter_dimension=1, tiled=True)
    loss_sum, hidden_all, logit_all, dec_bias_grad, embed_grad = lax.psum(
        (loss * first_mp, hidden_sq, logit_sq * first_mp, dec_bias * first_mp, embed_part), ("seq", "mp")
    )
    rec_out = ungrouped(rec_part, matrix).astype(jnp.float32)
    return (
        loss_sum, hidden_all, logit_all, dec_bias_grad, dec_part.astype(jnp.float32), hidden_grad, cell_grad, rec_out,
        edge_part[:, :-1].astype(jnp.float32), edge_part[:, -1].astype(jnp.float32), embed_grad,
    )


def per_device(ids, lengths, order, h_init, c_init, embed, w_in, w_rec, bias, w_dec, b_dec):
    seq_rank = lax.axis_index("seq")
    streams = ids.shape[1]
    per_dev = h_init.shape[1]
    own_units, all_units = h_init.shape[2], w_rec.shape[1]
    letter_count = embed.shape[1]
    wd_full = lax.all_gather(w_dec, "mp", axis=1, tiled=True)
    whole_ids = lax.all_gather(ids, "seq", axis=0, tiled=True)
    own_order = lax.dynamic_slice_in_dim(order, seq_rank * per_dev, per_dev)
    slot_ids = jnp.take(whole_ids, own_order, axis=1)
    own_len = jnp.take(lengths, own_order)
    live_total = jnp.sum(lengths).astype(jnp.float32)
    count = 2.0 * (jnp.sum(lengths) - streams).astype(jnp.float32)
    step_ids = jnp.stack([slot_ids, jnp.flip(slot_ids, 0)])
    lanes, matrix = column_order(own_units)
    w_rec_grouped = grouped(w_rec, matrix)
    w_in_grouped = grouped(w_in, matrix)
    bias_grouped = jnp.swapaxes(
        bias.reshape(2, own_units // lanes, lanes, 4), -1, -2
    ).reshape(bias.shape)
    operands = (
        step_ids, own_len, h_init, c_init, embed, w_in_grouped, w_rec_grouped, bias_grouped, w_dec, wd_full,
        b_dec, count, matrix,
    )
    fits = own_units % LANES == 0 and per_dev == CHUNK and all_units % (lax.axis_size("seq") * PIECE) == 0
    if lax.axis_size("mp") == 8 and lax.axis_size("seq") == 4 and fits:
        results = kernel_step(*operands)
    else:
        results = plain_step(*operands)
    loss_sum, hidden_all, logit_all, dec_bias_grad, dec_part, hidden_grad, cell_grad, rec_out, in_out, bias_out, embed_grad = results
    embed_wide = embed.astype(jnp.float32)
    rms_embed = jnp.sqrt(jnp.mean(embed_wide * embed_wide, axis=(1, 2)))
    return (
        loss_sum / count,
        hidden_grad,
        cell_grad,
        embed_grad,
        in_out,
        rec_out,
        bias_out,
        dec_part,
        dec_bias_grad,
        rms_embed,
        jnp.sqrt(hidden_all / (all_units * live_total)),
        jnp.sqrt(logit_all / (letter_count * count / 2.0)),
    )


def solution(mesh):
    in_specs = (
        P("seq", None),
        P(),
        P(),
        P(None, "seq", "mp"),
        P(None, "seq", "mp"),
        P(),
        P(None, None, "mp"),
        P(None, None, "mp"),
        P(None, "mp"),
        P(None, "mp", None),
        P(),
    )
    out_specs = (
        P(),
        P(None, "seq", "mp"),
        P(None, "seq", "mp"),
        P(),
        P(None, None, ("mp", "seq")),
        P(None, "seq", "mp"),
        P(None, ("mp", "seq")),
        P(None, ("mp", "seq"), None),
        P(),
        P(),
        P(),
        P(),
    )
    return jax.shard_map(
        per_device, mesh=mesh, in_specs=in_specs, out_specs=out_specs, check_vma=False
    )
```

```python
import functools

import jax
import jax.numpy as jnp
from jax import lax
from jax.experimental import pallas as pl
from jax.experimental.pallas import tpu as pltpu
from jax.sharding import PartitionSpec as P

VMEM_LIMIT = 58 * 2**20


def column_order(own_units):
    lanes = min(128, own_units)
    source = jnp.arange(4 * lanes, dtype=jnp.int32)
    place = (source % 4) * lanes + source // 4
    matrix = (place[:, None] == jnp.arange(4 * lanes, dtype=jnp.int32)[None, :]).astype(jnp.bfloat16)
    return lanes, matrix


def grouped(x, matrix):
    width = matrix.shape[0]
    parts = x.reshape(x.shape[:-1] + (x.shape[-1] // width, width))
    out = jnp.einsum("...gc,cp->...gp", parts, matrix, preferred_element_type=jnp.float32)
    return out.astype(x.dtype).reshape(x.shape)


def ungrouped(x, matrix):
    return grouped(x, matrix.T)


def ungrouped_wide(x, lanes):
    parts = x.reshape(x.shape[:-1] + (x.shape[-1] // (4 * lanes), 4, lanes))
    return jnp.swapaxes(parts, -1, -2).reshape(x.shape)


def gates_of(pre, lanes):
    parts = pre.reshape(pre.shape[:-1] + (pre.shape[-1] // (4 * lanes), 4, lanes))
    flat = pre.shape[:-1] + (pre.shape[-1] // 4,)
    return tuple(parts[..., k, :].reshape(flat) for k in range(4))


def joined_gates(gates, lanes):
    split = [g.reshape(g.shape[:-1] + (g.shape[-1] // lanes, 1, lanes)) for g in gates]
    joined = jnp.concatenate(split, axis=-2)
    return joined.reshape(gates[0].shape[:-1] + (4 * gates[0].shape[-1],))


def recurrences(step_ids, own_len, h_init, c_init, embed, w_in, w_rec, bias, w_dec, wd_full, b_dec, count, lanes):
    length, per_dev = step_ids.shape[1:]
    letter_count = embed.shape[1]
    steps = jnp.arange(length, dtype=jnp.int32)
    live_steps = jnp.stack(
        [steps[:, None] < own_len[None, :], (length - 1 - steps)[:, None] < own_len[None, :]], axis=1
    )[..., None]
    letters = jnp.arange(letter_count, dtype=jnp.int32)
    onehot = (jnp.swapaxes(step_ids, 0, 1)[..., None] == letters).astype(jnp.bfloat16)
    letter_rows = jnp.einsum(
        "sdbv,dve->sdbe", onehot, embed, preferred_element_type=jnp.float32
    ).astype(jnp.bfloat16)
    gates_in = jnp.einsum(
        "sdbe,dec->sdbc", letter_rows, w_in, preferred_element_type=jnp.float32
    ).astype(jnp.bfloat16)

    def forward_step(carry, inputs):
        hidden, cell = carry
        gate_in, live = inputs
        whole = lax.all_gather(hidden, "mp", axis=2, tiled=True)
        recurrent = jnp.einsum("dbh,dhc->dbc", whole, w_rec, preferred_element_type=jnp.float32)
        pre = gate_in.astype(jnp.float32) + recurrent + bias[:, None]
        in_pre, forget_pre, cell_pre, out_pre = gates_of(pre, lanes)
        in_gate, forget, out_gate = (jax.nn.sigmoid(x) for x in (in_pre, forget_pre, out_pre))
        cell_gate = jnp.tanh(cell_pre)
        new_cell = forget * cell + in_gate * cell_gate
        cell_next = jnp.where(live, new_cell, cell)
        hidden_next = jnp.where(
            live, out_gate * jnp.tanh(new_cell), hidden.astype(jnp.float32)
        ).astype(jnp.bfloat16)
        return ((hidden_next, cell_next), (whole, cell, in_gate, forget, cell_gate, out_gate))

    (last_hidden, last_cell), (wholes, cells, *gates) = lax.scan(
        forward_step, (h_init, c_init), (gates_in, live_steps)
    )
    last_whole = lax.all_gather(last_hidden, "mp", axis=2, tiled=True)
    after = jnp.concatenate([wholes[1:], last_whole[None]], axis=0)
    own = h_init.shape[2]
    mine = lax.dynamic_slice_in_dim(after, lax.axis_index("mp") * own, own, axis=3)
    mine_wide = mine.astype(jnp.float32)
    hidden_sq = jnp.sum(jnp.where(live_steps, mine_wide * mine_wide, 0.0), axis=(0, 2, 3))
    logits = (
        jnp.einsum("sdbh,dhv->sdbv", after, wd_full, preferred_element_type=jnp.float32) + b_dec[None, :, None]
    )
    targets = jnp.swapaxes(jnp.concatenate([step_ids[:, 1:], step_ids[:, :1]], axis=1), 0, 1)
    fore_valid = (steps[:, None] + 1 < own_len[None, :])
    back_valid = (steps[:, None] < length - 1) & ((length - 1 - steps)[:, None] < own_len[None, :])
    valid = jnp.stack([fore_valid, back_valid], axis=1).astype(jnp.float32)
    logit_sq = jnp.sum(valid[..., None] * logits * logits, axis=(0, 2, 3))
    top = jnp.max(logits, axis=-1, keepdims=True)
    log_total = top + jnp.log(jnp.sum(jnp.exp(logits - top), axis=-1, keepdims=True))
    target_hot = targets[..., None] == letters
    picked = jnp.sum(jnp.where(target_hot, logits, 0.0), axis=-1)
    loss = jnp.sum(valid * (log_total[..., 0] - picked))
    grad_logits = (
        valid[..., None] * (jnp.exp(logits - log_total) - target_hot.astype(jnp.float32)) / count
    ).astype(jnp.bfloat16)
    dec_bias = jnp.sum(grad_logits.astype(jnp.float32), axis=(0, 2))
    dec_grad = jnp.einsum("sdbh,sdbv->dhv", mine, grad_logits, preferred_element_type=jnp.float32)

    def backward_step(carry, inputs):
        grad_hidden, grad_cell = carry
        live, cell, in_gate, forget, cell_gate, out_gate, grad_logit = inputs
        grad_hidden = grad_hidden + jnp.einsum(
            "dbv,dhv->dbh", grad_logit, w_dec, preferred_element_type=jnp.float32
        )
        squash = jnp.tanh(forget * cell + in_gate * cell_gate)
        grad_new = jnp.where(live, grad_cell + grad_hidden * out_gate * (1.0 - squash * squash), 0.0)
        grad_out = jnp.where(live, grad_hidden * squash, 0.0)
        grad_pre = joined_gates(
            [
                grad_new * cell_gate * in_gate * (1.0 - in_gate),
                grad_new * cell * forget * (1.0 - forget),
                grad_new * in_gate * (1.0 - cell_gate * cell_gate),
                grad_out * out_gate * (1.0 - out_gate),
            ],
            lanes,
        ).astype(jnp.bfloat16)
        grad_cell_prev = grad_new * forget + jnp.where(live, 0.0, grad_cell)
        held = jnp.where(live, 0.0, grad_hidden)
        terms = jnp.einsum("dbc,dhc->dbh", grad_pre, w_rec, preferred_element_type=jnp.float32)
        through = lax.psum_scatter(
            terms.astype(jnp.bfloat16), "mp", scatter_dimension=2, tiled=True
        ).astype(jnp.float32)
        return ((held + through, grad_cell_prev), grad_pre)

    start = jnp.zeros(c_init.shape, jnp.float32)
    (hidden_grad, cell_grad), grad_pres = lax.scan(
        backward_step, (start, start), (live_steps, cells, *gates, grad_logits), reverse=True
    )
    rec_grad = jnp.einsum("sdbh,sdbc->dhc", wholes, grad_pres, preferred_element_type=jnp.float32)
    letter_grad = jnp.einsum("sdbv,sdbc->dvc", onehot, grad_pres, preferred_element_type=jnp.float32)
    return loss, hidden_sq, logit_sq, dec_bias, dec_grad, hidden_grad, cell_grad, rec_grad, letter_grad


MESH = pl.DeviceIdType.MESH
LANES = 128
VOCAB_PAD = 384
SPLIT = 1
NT = (((1,), (1,)), ((), ()))
TN = (((0,), (0,)), ((), ()))


def sigmoid(x):
    return 0.5 * jnp.tanh(0.5 * x) + 0.5


def matmul(left, right, dims=(((1,), (0,)), ((), ()))):
    return lax.dot_general(left, right, dims, preferred_element_type=jnp.float32)


def neighbours():
    me = lax.axis_index("mp")
    row, column, core = me // 4, (me // 2) % 2, me % 2
    sibling = row * 4 + column * 2 + (1 - core)
    across = (1 - row) * 4 + (1 - column) * 2 + core
    side = row * 4 + (1 - column) * 2 + core
    up = (1 - row) * 4 + column * 2 + core
    return me, sibling, (across, side, up)


def greet(peers, seqs=0):
    seq, me = lax.axis_index("seq"), lax.axis_index("mp")
    barrier = pltpu.get_barrier_semaphore()
    for peer in peers:
        pl.semaphore_signal(barrier, inc=1, device_id=(seq, peer), device_id_type=MESH)
    for n in range(1, seqs):
        pl.semaphore_signal(barrier, inc=1, device_id=((seq + n) % seqs, me), device_id_type=MESH)
    pl.semaphore_wait(barrier, len(peers) + max(seqs - 1, 0))


def remote(src, dst, send, recv, peer):
    return pltpu.make_async_remote_copy(
        src_ref=src, dst_ref=dst, send_sem=send, recv_sem=recv,
        device_id=(lax.axis_index("seq"), peer), device_id_type=MESH,
    )


def other_core(peer):
    return (peer // 2) * 2 + (1 - peer % 2)


def folded(x):
    return jnp.sum(x.reshape(x.shape[0] // 8, 8, x.shape[1]), axis=0)


def column_of(table, lane):
    lanes = lax.broadcasted_iota(jnp.int32, table.shape, 1)
    return jnp.sum(jnp.where(lanes == lane, table, 0.0), axis=1, keepdims=True)


def time_of(direction, step, length):
    return step if direction == 0 else length - 1 - step


def stream_order():
    return [d * SPLIT + r for r in range(SPLIT) for d in range(2)]


def forward_kernel(
    length, letters, ids_in, lens, order_row, order_column, inverse, h_in, c_in, embed, w_in_raw, bias, b_dec,
    w_dec, matrix, w_hbm,
    wholes, acts, grads, w_out, loss, logit_sq, hidden_sq, dec_bias, dec_grad, info, ids, w_in,
    w, wd, buf, cell, acc, logit, stage, grad, all_ids, table, load_sem, ids_send, ids_recv, wd_send, wd_recv,
    send_sem, recv_sem, save_sem, act_sem, grad_sem,
):
    me, sibling, peers = neighbours()
    seq, seqs, times = lax.axis_index("seq"), all_ids.shape[0], ids_in.shape[0]
    blocks, rows, units = buf.shape[2:]
    groups, span = units // LANES, matrix.shape[0]
    columns = w.shape[-1]
    load_w = pltpu.make_async_copy(w_hbm, w, load_sem.at[0])
    store_w = pltpu.make_async_copy(w, w_out, load_sem.at[1])
    load_w.start()
    all_ids[seq, :times] = ids_in[...].astype(jnp.float32)
    wd[me] = w_dec[...]
    for s in range(2 * SPLIT):
        buf[s, 0, me] = h_in[s]
    greet((sibling,) + peers, seqs)

    def ids_copy(n):
        to = (seq + n) % seqs
        block = all_ids.at[seq]
        return pltpu.make_async_remote_copy(
            src_ref=block, dst_ref=block, send_sem=ids_send.at[n - 1], recv_sem=ids_recv.at[seq],
            device_id=(to, me), device_id_type=MESH,
        )

    def ids_arrival(n):
        source = (seq + n) % seqs
        block = all_ids.at[source]
        return pltpu.make_async_remote_copy(
            src_ref=block, dst_ref=block, send_sem=ids_send.at[n - 1], recv_sem=ids_recv.at[source],
            device_id=(source, me), device_id_type=MESH,
        )

    def direct(s, step):
        slot, par = step % 3, step % 2
        block = buf.at[s, slot, me]
        return [
            remote(block, block, send_sem.at[s, par, n], recv_sem.at[s, slot, me], peer)
            for n, peer in enumerate(peers + (sibling,))
        ]

    def relay(s, step, n):
        slot, par = step % 3, step % 2
        block = buf.at[s, slot, peers[n]]
        return remote(block, block, send_sem.at[s, par, 4 + n], recv_sem.at[s, slot, peers[n]], sibling)

    def arrival(s, step, source):
        slot = step % 3
        block = buf.at[s, slot, source]
        return remote(block, block, send_sem.at[s, step % 2, 0], recv_sem.at[s, slot, source], sibling)

    def wd_copy(n):
        peer = (peers + (sibling,))[n]
        return remote(wd.at[me], wd.at[me], wd_send.at[n], wd_recv.at[me], peer)

    def wd_relay(n):
        block = wd.at[peers[n]]
        return remote(block, block, wd_send.at[4 + n], wd_recv.at[peers[n]], sibling)

    def wd_arrival(source):
        return remote(wd.at[source], wd.at[source], wd_send.at[0], wd_recv.at[source], sibling)

    def save(s, step):
        return pltpu.make_async_copy(buf.at[s, step % 3], wholes.at[step, s], save_sem.at[s, step % 2])

    def save_acts(s, step):
        return pltpu.make_async_copy(stage.at[s], acts.at[step, s], act_sem.at[s])

    def save_grad(s, step):
        return pltpu.make_async_copy(grad.at[s], grads.at[step, s], grad_sem.at[s])

    def finish_sends(s, step):
        for copy in direct(s, step):
            copy.wait_send()
        for n in range(3):
            relay(s, step, n).wait_send()

    for n in range(1, seqs):
        ids_copy(n).start()
    for s in stream_order():
        for copy in direct(s, 0):
            copy.start()
    for n in range(4):
        wd_copy(n).start()
    for ref in (loss, logit_sq, hidden_sq, dec_bias, dec_grad):
        ref[...] = jnp.zeros(ref.shape, ref.dtype)
    cell[...] = c_in[...]
    for d in range(2):
        for g in range(columns // span):
            part = slice(g * span, (g + 1) * span)
            w_in[d, :, part] = matmul(w_in_raw[d, :, part], matrix[...]).astype(jnp.bfloat16)
    load_w.wait()

    def regroup(b, carry):
        for d in range(2):
            for g in range(columns // span):
                part = slice(g * span, (g + 1) * span)
                w[d, b, :, part] = matmul(w[d, b, :, part], matrix[...]).astype(jnp.bfloat16)
        return carry

    lax.fori_loop(0, blocks, regroup, 0)
    store_w.start()
    for n in range(1, seqs):
        ids_arrival(n).wait_recv()
    streams = order_row.shape[1]
    total_streams = lens.shape[1]
    pick_column = (
        lax.broadcasted_iota(jnp.int32, (streams, total_streams), 1) == order_column[...]
    ).astype(jnp.bfloat16)
    pick_row = (
        lax.broadcasted_iota(jnp.int32, (total_streams, streams), 0) == order_row[...]
    ).astype(jnp.bfloat16)
    table[...] = jnp.zeros(table.shape, table.dtype)
    for d in range(2):
        for t in range(length):
            row = t if d == 0 else length - 1 - t
            table[t:t + 1] = all_ids[row // times, row % times:row % times + 1]
        table[LANES - 1:] = lens[...].astype(jnp.float32)
        high = jnp.floor(table[...] * (1.0 / 16.0))
        low = (table[...] - 16.0 * high).astype(jnp.bfloat16)
        high = high.astype(jnp.bfloat16)
        values = 16.0 * matmul(pick_column, high, NT) + matmul(pick_column, low, NT)
        for r in range(SPLIT):
            info[d * SPLIT + r] = values[r * rows:(r + 1) * rows]
        values = 16.0 * matmul(high[:length], pick_row) + matmul(low[:length], pick_row)
        for r in range(SPLIT):
            ids[d * SPLIT + r] = values[:, r * rows:(r + 1) * rows]

    def gates(s, step):
        slot, later = step % 3, (step + 1) % 3
        d = s // SPLIT
        when = time_of(d, step, length)
        live = info[s, :, LANES - 1:] > when.astype(jnp.float32)
        for g in range(groups):
            lanes = slice(g * LANES, (g + 1) * LANES)
            pre = [acc[:, (4 * g + k) * LANES:(4 * g + k + 1) * LANES] for k in range(4)]
            in_gate, forget, out_gate = sigmoid(pre[0]), sigmoid(pre[1]), sigmoid(pre[3])
            cell_gate = jnp.tanh(pre[2])
            old = cell[s, :, lanes]
            new = forget * old + in_gate * cell_gate
            for k, value in enumerate((in_gate, forget, cell_gate, out_gate, old)):
                stage[s, k, :, lanes] = value
            cell[s, :, lanes] = jnp.where(live, new, old)
            before = buf[s, slot, me, :, lanes].astype(jnp.float32)
            hidden = jnp.where(live, out_gate * jnp.tanh(new), before).astype(jnp.bfloat16)
            buf[s, later, me, :, lanes] = hidden
            wide = hidden.astype(jnp.float32)
            hidden_sq[d] += folded(jnp.where(live, wide * wide, 0.0))

    def decode(s, step):
        slot = step % 3
        d = s // SPLIT
        total = jnp.broadcast_to(b_dec[d], logit.shape)
        for b in range(blocks):
            total += matmul(buf[s, slot, b], wd[b, d])
        logit[...] = total
        when = time_of(d, step - 1, length)
        reach = when + 1 if d == 0 else when
        lookup = info[s]
        valid = (lookup[:, LANES - 1:] > reach.astype(jnp.float32)) & (step < length)
        target = column_of(lookup, step)
        value = logit[...]
        lanes = lax.broadcasted_iota(jnp.int32, value.shape, 1)
        hot = lanes.astype(jnp.float32) == target
        top = jnp.max(value, axis=1, keepdims=True)
        power = jnp.exp(value - top)
        total = jnp.sum(power, axis=1, keepdims=True)
        picked = jnp.sum(jnp.where(hot, value, 0.0), axis=1, keepdims=True)
        loss[d] += folded(jnp.broadcast_to(jnp.where(valid, top + jnp.log(total) - picked, 0.0), (rows, LANES)))
        kept = jnp.where(valid & (lanes < letters), value, 0.0)
        square = kept * kept
        logit_sq[d] += folded(sum(square[:, n * LANES:(n + 1) * LANES] for n in range(VOCAB_PAD // LANES)))
        slope = jnp.where(
            valid, (power * (1.0 / total) - jnp.where(hot, 1.0, 0.0)) * inverse[0, 0], 0.0
        ).astype(jnp.bfloat16)
        grad[s] = slope
        dec_bias[d] += folded(slope.astype(jnp.float32))
        dec_grad[d] += matmul(buf[s, slot, me], grad[s], TN)

    others = tuple(other_core(peer) for peer in peers)

    def half(step, s):
        d = s // SPLIT

        @pl.when(step < length)
        def _():
            now = column_of(info[s], step)
            hot = (lax.broadcasted_iota(jnp.int32, (rows, VOCAB_PAD), 1).astype(jnp.float32) == now)
            row = matmul(hot.astype(jnp.bfloat16), embed[d]).astype(jnp.bfloat16)
            acc[...] = matmul(row, w_in[d]).astype(jnp.bfloat16).astype(jnp.float32) + bias[d]

        for n, peer in enumerate(peers):
            arrival(s, step, peer).wait_recv()
            relay(s, step, n).start()

        if s == 0:
            @pl.when(step == 1)
            def _():
                for n, peer in enumerate(peers):
                    wd_arrival(peer).wait_recv()
                    wd_relay(n).start()

        slot = step % 3

        def advance(block):
            acc[...] += matmul(buf[s, slot, block], w[d, block])

        @pl.when(step < length)
        def _():
            for block in (me,) + peers:
                advance(block)

        for block in (sibling,) + others:
            arrival(s, step, block).wait_recv()

        @pl.when(step < length)
        def _():
            save(s, step).start()
            for block in (sibling,) + others:
                advance(block)

            @pl.when(step > 0)
            def _():
                save_acts(s, step - 1).wait()

            gates(s, step)
            save_acts(s, step).start()

            @pl.when(step > 0)
            def _():
                save(s, step - 1).wait()
                finish_sends(s, step - 1)

            for copy in direct(s, step + 1):
                copy.start()

        if s == 0:
            @pl.when(step == 1)
            def _():
                for block in (sibling,) + others:
                    wd_arrival(block).wait_recv()

        @pl.when(step > 0)
        def _():
            @pl.when(step > 1)
            def _():
                save_grad(s, step - 2).wait()

            decode(s, step)
            save_grad(s, step - 1).start()

    def every(step, carry):
        for s in stream_order():
            half(step, s)
        return carry

    lax.fori_loop(0, length + 1, every, 0)
    store_w.wait()
    for n in range(1, seqs):
        ids_copy(n).wait_send()
    for n in range(4):
        wd_copy(n).wait_send()
    for n in range(3):
        wd_relay(n).wait_send()
    for s in stream_order():
        save(s, length - 1).wait()
        save_acts(s, length - 1).wait()
        save_grad(s, length - 1).wait()
        finish_sends(s, length - 1)
        finish_sends(s, length)


def backward_kernel(
    length, info, ids, w_dec, acts, grads, wholes, w_hbm,
    rec_out, letter_grad, hidden_grad, cell_grad,
    w, rec, stage, grad, whole, pre, held, own, sent, got, passed, taken, load_sem, act_sem, grad_sem, whole_sem,
    core_send, core_recv, chip_send, chip_recv,
):
    me, sibling, peers = neighbours()
    rows, units = held.shape[1:]
    groups = units // LANES
    load_w = pltpu.make_async_copy(w_hbm, w, load_sem)
    load_w.start()

    def load_acts(s, step):
        return pltpu.make_async_copy(acts.at[step, s], stage.at[s], act_sem.at[s])

    def load_grad(s, step):
        return pltpu.make_async_copy(grads.at[step, s], grad.at[s], grad_sem.at[s])

    def load_whole(s, step):
        return pltpu.make_async_copy(wholes.at[step, s], whole.at[s], whole_sem.at[s])

    for s in stream_order():
        load_acts(s, length - 1).start()
        load_grad(s, length - 1).start()
        load_whole(s, length - 1).start()
    greet((sibling,) + peers)
    held[...] = jnp.zeros(held.shape, held.dtype)
    own[...] = jnp.zeros(own.shape, own.dtype)
    cell_grad[...] = jnp.zeros(cell_grad.shape, cell_grad.dtype)
    letter_grad[...] = jnp.zeros(letter_grad.shape, letter_grad.dtype)

    def clear(b, carry):
        for d in range(2):
            rec[d, b] = jnp.zeros(rec.shape[2:], rec.dtype)
        return carry

    lax.fori_loop(0, w.shape[1], clear, 0)
    load_w.wait()

    def to_core(s, turn, n):
        return remote(
            sent.at[s, n], got.at[s, turn % 2, n], core_send.at[s, n], core_recv.at[s, turn % 2, n], sibling
        )

    def to_chip(s, turn, n):
        return remote(
            passed.at[s, n], taken.at[s, turn % 2, n], chip_send.at[s, n], chip_recv.at[s, turn % 2, n], peers[n]
        )

    def half(turn, s):
        step = length - 1 - turn
        d = s // SPLIT
        when = time_of(d, step, length)
        load_acts(s, step).wait()
        load_grad(s, step).wait()
        held[s] += matmul(grad[s], w_dec[d], NT)

        @pl.when(turn > 0)
        def _():
            for n in range(3):
                to_chip(s, turn - 1, n).wait_recv()

        live = info[s, :, LANES - 1:] > when.astype(jnp.float32)
        for g in range(groups):
            lanes = slice(g * LANES, (g + 1) * LANES)
            through = own[s, :, lanes]
            for n in range(3):
                through += jnp.where(turn > 0, taken[s, (turn + 1) % 2, n, :, lanes].astype(jnp.float32), 0.0)
            total = held[s, :, lanes] + through
            in_gate, forget, cell_gate, out_gate, old = (stage[s, k, :, lanes] for k in range(5))
            squash = jnp.tanh(forget * old + in_gate * cell_gate)
            later = cell_grad[s, :, lanes]
            new = jnp.where(live, later + total * out_gate * (1.0 - squash * squash), 0.0)
            out = jnp.where(live, total * squash, 0.0)
            values = (
                new * cell_gate * in_gate * (1.0 - in_gate),
                new * old * forget * (1.0 - forget),
                new * in_gate * (1.0 - cell_gate * cell_gate),
                out * out_gate * (1.0 - out_gate),
            )
            for k, value in enumerate(values):
                pre[s, :, (4 * g + k) * LANES:(4 * g + k + 1) * LANES] = value.astype(jnp.bfloat16)
            cell_grad[s, :, lanes] = new * forget + jnp.where(live, 0.0, later)
            held[s, :, lanes] = jnp.where(live, 0.0, total)

        @pl.when(turn < length - 1)
        def _():
            load_acts(s, step - 1).start()
            load_grad(s, step - 1).start()

        @pl.when(turn > 0)
        def _():
            for n in range(4):
                to_core(s, turn - 1, n).wait_send()
            for n in range(3):
                to_chip(s, turn - 1, n).wait_send()

        for n, block in enumerate(tuple(other_core(peer) for peer in peers) + (sibling,)):
            sent[s, n] = matmul(pre[s], w[d, block], NT).astype(jnp.bfloat16)
            to_core(s, turn, n).start()
        for n, block in enumerate(peers + (me,)):
            part = matmul(pre[s], w[d, block], NT)
            to_core(s, turn, n).wait_recv()
            part += got[s, turn % 2, n].astype(jnp.float32)
            if n < 3:
                passed[s, n] = part.astype(jnp.bfloat16)
                to_chip(s, turn, n).start()
            else:
                own[s] = part

        if s % SPLIT == SPLIT - 1:
            both = range(s - SPLIT + 1, s + 1)
            for i in both:
                load_whole(i, step).wait()
            for b in range(w.shape[1]):
                rec[d, b] += sum(matmul(whole[i, b], pre[i], TN) for i in both)

            @pl.when(turn < length - 1)
            def _():
                for i in both:
                    load_whole(i, step - 1).start()

            letters = lax.broadcasted_iota(jnp.int32, (VOCAB_PAD, rows), 0).astype(jnp.float32)
            terms = []
            for i in both:
                hot = letters == ids[i, pl.ds(step, 1), :]
                terms.append(matmul(hot.astype(jnp.bfloat16), pre[i]))
            letter_grad[d] += sum(terms)

    def every(turn, carry):
        for s in stream_order():
            half(turn, s)
        return carry

    lax.fori_loop(0, length, every, 0)
    for s in stream_order():
        for n in range(3):
            to_chip(s, length - 1, n).wait_recv()
        total = held[s] + own[s]
        for n in range(3):
            total += taken[s, (length - 1) % 2, n].astype(jnp.float32)
        hidden_grad[s] = total
        for n in range(4):
            to_core(s, length - 1, n).wait_send()
        for n in range(3):
            to_chip(s, length - 1, n).wait_send()

    def narrow(b, carry):
        for d in range(2):
            w[d, b] = rec[d, b].astype(jnp.bfloat16)
        return carry

    lax.fori_loop(0, w.shape[1], narrow, 0)
    store = pltpu.make_async_copy(w, rec_out, load_sem)
    store.start()
    store.wait()


def kernel_step(ids, lengths, order, count, h_init, c_init, embed, w_in, w_rec, bias, w_dec, b_dec, matrix):
    seqs = lax.axis_size("seq")
    local_times, all_streams = ids.shape
    length = local_times * seqs
    per_dev, units = h_init.shape[1:]
    streams, rows = 2 * SPLIT, per_dev // SPLIT
    letters, width = embed.shape[1:]
    columns = w_rec.shape[2]
    blocks = w_rec.shape[1] // units
    any_space, vmem = pl.BlockSpec(memory_space=pl.ANY), pl.BlockSpec(memory_space=pltpu.VMEM)
    own_order = lax.dynamic_slice_in_dim(order, lax.axis_index("seq") * per_dev, per_dev)
    pad_letters = VOCAB_PAD - letters
    embed_pad = jnp.pad(embed, ((0, 0), (0, pad_letters), (0, LANES - width)))
    w_in_pad = jnp.pad(w_in, ((0, 0), (0, LANES - width), (0, 0)))
    w_dec_pad = jnp.pad(w_dec, ((0, 0), (0, 0), (0, pad_letters)))
    b_dec_pad = jnp.pad(b_dec, ((0, 0), (0, pad_letters)), constant_values=-1e30)[:, None]
    bias_grouped = jnp.swapaxes(bias.reshape(2, units // LANES, LANES, 4), -1, -2).reshape(2, 1, columns)
    f32, bf16 = jnp.float32, jnp.bfloat16
    dma = pltpu.SemaphoreType.DMA
    shape = jax.ShapeDtypeStruct
    wholes, acts, grads, w_grouped, loss, logit_sq, hidden_sq, dec_bias, dec_grad, info, slot_ids, w_in_grouped = pl.pallas_call(
        functools.partial(forward_kernel, length, letters),
        out_shape=(
            shape((length, streams, blocks, rows, units), bf16),
            shape((length, streams, 5, rows, units), f32),
            shape((length, streams, rows, VOCAB_PAD), bf16),
            shape((2, blocks, units, columns), bf16),
            shape((2, 8, LANES), f32),
            shape((2, 8, LANES), f32),
            shape((2, 8, LANES), f32),
            shape((2, 8, VOCAB_PAD), f32),
            shape((2, units, VOCAB_PAD), f32),
            shape((streams, rows, LANES), f32),
            shape((streams, length, rows), f32),
            shape((2, LANES, columns), bf16),
        ),
        in_specs=[vmem] * 4 + [pl.BlockSpec(memory_space=pltpu.SMEM)] + [vmem] * 8 + [any_space],
        out_specs=(any_space,) * 4 + (vmem,) * 8,
        scratch_shapes=[
            pltpu.VMEM((2, blocks, units, columns), bf16),
            pltpu.VMEM((blocks, 2, units, VOCAB_PAD), bf16),
            pltpu.VMEM((streams, 3, blocks, rows, units), bf16),
            pltpu.VMEM((streams, rows, units), f32),
            pltpu.VMEM((rows, columns), f32),
            pltpu.VMEM((rows, VOCAB_PAD), f32),
            pltpu.VMEM((streams, 5, rows, units), f32),
            pltpu.VMEM((streams, rows, VOCAB_PAD), bf16),
            pltpu.VMEM((seqs, 8, all_streams), f32),
            pltpu.VMEM((LANES, all_streams), f32),
            dma((2,)),
            dma((seqs - 1,)),
            dma((seqs,)),
            dma((7,)),
            dma((blocks,)),
            dma((streams, 2, 7)),
            dma((streams, 3, blocks)),
            dma((streams, 2)),
            dma((streams,)),
            dma((streams,)),
        ],
        compiler_params=pltpu.CompilerParams(
            collective_id=0, has_side_effects=True, vmem_limit_bytes=VMEM_LIMIT
        ),
        name="forward_visits",
    )(
        ids, lengths[None], own_order[None], own_order[:, None], (1.0 / count).reshape(1, 1),
        h_init.reshape(streams, rows, units), c_init.reshape(streams, rows, units), embed_pad, w_in_pad,
        bias_grouped, b_dec_pad, w_dec_pad, matrix, w_rec.reshape(2, blocks, units, columns),
    )
    rec_grad, letter_grad, hidden_grad, cell_grad = pl.pallas_call(
        functools.partial(backward_kernel, length),
        out_shape=(
            shape((2, blocks, units, columns), bf16),
            shape((2, VOCAB_PAD, columns), f32),
            shape((streams, rows, units), f32),
            shape((streams, rows, units), f32),
        ),
        in_specs=[vmem] * 3 + [any_space] * 4,
        out_specs=(any_space, vmem, vmem, vmem),
        scratch_shapes=[
            pltpu.VMEM((2, blocks, units, columns), bf16),
            pltpu.VMEM((2, blocks, units, columns), f32),
            pltpu.VMEM((streams, 5, rows, units), f32),
            pltpu.VMEM((streams, rows, VOCAB_PAD), bf16),
            pltpu.VMEM((streams, blocks, rows, units), bf16),
            pltpu.VMEM((streams, rows, columns), bf16),
            pltpu.VMEM((streams, rows, units), f32),
            pltpu.VMEM((streams, rows, units), f32),
            pltpu.VMEM((streams, 4, rows, units), bf16),
            pltpu.VMEM((streams, 2, 4, rows, units), bf16),
            pltpu.VMEM((streams, 3, rows, units), bf16),
            pltpu.VMEM((streams, 2, 3, rows, units), bf16),
            dma,
            dma((streams,)),
            dma((streams,)),
            dma((streams,)),
            dma((streams, 4)),
            dma((streams, 2, 4)),
            dma((streams, 3)),
            dma((streams, 2, 3)),
        ],
        compiler_params=pltpu.CompilerParams(
            collective_id=1, has_side_effects=True, vmem_limit_bytes=VMEM_LIMIT
        ),
        name="backward_visits",
    )(info, slot_ids, w_dec_pad, acts, grads, wholes, w_grouped)
    rec_part, edge_part, dec_part, small = kernel_sums(
        rec_grad, letter_grad, embed_pad, w_in_grouped, matrix, width, letters, dec_grad,
        (loss, logit_sq, hidden_sq, dec_bias),
    )
    at = 2 * TABLE
    return (
        small[at, 0],
        jnp.sum(small[at + 3:at + 5], axis=1),
        jnp.sum(small[at + 1:at + 3], axis=1),
        small[at + 5:at + 5 + 2 * (VOCAB_PAD // LANES)].reshape(2, VOCAB_PAD)[:, :letters],
        dec_part[:, :, :letters],
        hidden_grad.reshape(h_init.shape),
        cell_grad.reshape(h_init.shape),
        rec_part.reshape(2, -1, columns),
        edge_part[:, :width],
        edge_part[:, width],
        small[:at].reshape(2, TABLE, LANES)[:, :letters, :width],
    )


PIECE = 128
LAG = 3
WINDOW = 3
TABLE = 280


def spread(letter_grad, other, dims):
    high = letter_grad.astype(jnp.bfloat16)
    low = (letter_grad - high.astype(jnp.float32)).astype(jnp.bfloat16)
    return matmul(high, other, dims) + matmul(low, other, dims)


def reduce_kernel(
    width, rec_hbm, letter_grad, embed, w_in, matrix, dec_grad, loss, logit_sq, hidden_sq, dec_bias,
    rec_out, edge_out, dec_out, small_out,
    own, ahead, behind, edge, edge_in, dec, dec_in, small, part, small_in, part_in, summed,
    load_sem, line_send, line_recv, back_send, back_recv, edge_send, edge_recv, dec_send, dec_recv,
    scatter_send, scatter_recv, seq_send, seq_recv, gather_send, gather_recv,
):
    seq, me = lax.axis_index("seq"), lax.axis_index("mp")
    count, parts = own.shape[1], own.shape[2]
    peers = lax.axis_size("mp")
    share = small.shape[0] // peers
    half = seq // (count // 2)
    place = seq + half * (count - 1 - 2 * seq)
    onward = 1 - 2 * half
    inner = count // 2 - 1
    lag = LAG + (inner - place) * 5
    load = pltpu.make_async_copy(rec_hbm, own, load_sem)
    load.start()

    def other_seq(n):
        return (seq + n) % count

    def other_mp(n):
        return (me + n) % peers

    barrier = pltpu.get_barrier_semaphore()
    for n in range(1, count):
        pl.semaphore_signal(barrier, inc=1, device_id=(other_seq(n), me), device_id_type=MESH)
    for n in range(1, peers):
        pl.semaphore_signal(barrier, inc=1, device_id=(seq, other_mp(n)), device_id_type=MESH)
    pl.semaphore_wait(barrier, count + peers - 2)
    load.wait()

    def send(src, dst, send_sem, recv_sem, seq_to, mp_to):
        return pltpu.make_async_remote_copy(
            src_ref=src, dst_ref=dst, send_sem=send_sem, recv_sem=recv_sem,
            device_id=(seq_to, mp_to), device_id_type=MESH,
        )

    def actual(chunk):
        return chunk + half * (count - 1 - 2 * chunk)

    pieces = 2 * parts

    def slot(k):
        return k // pieces, (k % pieces) // parts, k % parts

    def piece(chunk, d, r):
        return own.at[d, actual(chunk), r]

    def line_copy(k, crossing):
        i, d, r = slot(k)
        target = behind.at[i, d, r] if crossing else ahead.at[i, d, r]
        sem = back_recv.at[i, d, r] if crossing else line_recv.at[i, d, r]
        return send(piece(count - 1 - i, d, r), target, line_send.at[i, d, r], sem, seq + onward, me)

    def back_copy(k):
        i, d, r = slot(k)
        return send(
            piece(i, d, r), behind.at[i, d, r], back_send.at[i, d, r], back_recv.at[i, d, r], seq - onward, me
        )

    def add(chunk, d, r, term):
        ref = piece(chunk, d, r)
        ref[...] = (ref[...].astype(jnp.float32) + term[...].astype(jnp.float32)).astype(jnp.bfloat16)

    def line(k):
        i, d, r = slot(k)

        @pl.when((place > 0) & (i <= count - 1 - place))
        def _():
            line_copy(k, False).wait_recv()
            add(count - 1 - i, d, r, ahead.at[i, d, r])

        @pl.when((place == 0) & (k >= WINDOW))
        def _():
            line_copy(k - WINDOW, False).wait_send()

        @pl.when((i <= count - 2 - place) & (place < inner))
        def _():
            line_copy(k, False).start()

        @pl.when((i <= count - 2 - place) & (place == inner))
        def _():
            line_copy(k, True).start()

    def back(k):
        i, d, r = slot(k)

        @pl.when(i <= place)
        def _():
            back_copy(k).wait_recv()
            add(i, d, r, behind.at[i, d, r])

        @pl.when(i < place)
        def _():
            back_copy(k).start()

    def advance(k, carry):
        @pl.when(k < (count - 1) * pieces)
        def _():
            line(k)

        @pl.when((k >= lag) & (k - lag < (count // 2) * pieces))
        def _():
            back(k - lag)

        return carry

    def edge_copy(n):
        to = other_seq(n)
        return send(edge.at[to], edge_in.at[n - 1], edge_send.at[n - 1], edge_recv.at[n - 1], to, me)

    def dec_copy(n):
        to = other_seq(n)
        return send(dec.at[to], dec_in.at[n - 1], dec_send.at[n - 1], dec_recv.at[n - 1], to, me)

    def scatter_copy(n):
        to = other_mp(n)
        rows = pl.ds(pl.multiple_of(to * share, 8), share)
        return send(small.at[rows], small_in.at[n - 1], scatter_send.at[n - 1], scatter_recv.at[n - 1], seq, to)

    def seq_copy(n):
        return send(part, part_in.at[n - 1], seq_send.at[n - 1], seq_recv.at[n - 1], other_seq(n), me)

    own_rows = pl.ds(pl.multiple_of(me * share, 8), share)

    def gather_copy(n):
        return send(
            summed.at[own_rows], summed.at[own_rows], gather_send.at[n - 1], gather_recv.at[me], seq, other_mp(n)
        )

    def gather_arrival(n):
        source = other_mp(n)
        rows = pl.ds(pl.multiple_of(source * share, 8), share)
        return send(summed.at[rows], summed.at[rows], gather_send.at[n - 1], gather_recv.at[source], seq, source)

    start = 6
    lax.fori_loop(0, 2, advance, 0)
    first = jnp.where(me == 0, 1.0, 0.0)
    for d in range(2):
        small[d * TABLE:(d + 1) * TABLE] = spread(letter_grad[d], w_in[d], NT)[:TABLE]
    small[2 * TABLE:] = jnp.zeros((small.shape[0] - 2 * TABLE, LANES), jnp.float32)
    at = 2 * TABLE
    small[at:at + 1] = jnp.sum(loss[0] + loss[1], axis=0, keepdims=True) * first
    for d in range(2):
        small[at + 1 + d:at + 2 + d] = jnp.sum(logit_sq[d], axis=0, keepdims=True) * first
        small[at + 3 + d:at + 4 + d] = jnp.sum(hidden_sq[d], axis=0, keepdims=True)
        row = jnp.sum(dec_bias[d], axis=0, keepdims=True) * first
        for n in range(VOCAB_PAD // LANES):
            line_at = at + 5 + d * (VOCAB_PAD // LANES) + n
            small[line_at:line_at + 1] = row[:, n * LANES:(n + 1) * LANES]
    for n in range(1, peers):
        scatter_copy(n).start()
    rows = edge.shape[2]
    span = matrix.shape[0]
    wide = own.shape[-1] // count
    for d in range(2):
        full = spread_left(embed[d], letter_grad[d]).astype(jnp.bfloat16)
        flat = [
            matmul(full[:, g * span:(g + 1) * span], matrix[...], NT).astype(jnp.bfloat16)
            for g in range(own.shape[-1] // span)
        ]
        for q in range(count):
            group, offset = (q * wide) // span, (q * wide) % span
            edge[q, d] = flat[group][:rows, offset:offset + wide]
            depth = dec.shape[2]
            dec[q, d] = dec_grad[d, q * depth:(q + 1) * depth].astype(jnp.bfloat16)
    for n in range(1, count):
        edge_copy(n).start()
        dec_copy(n).start()
    lax.fori_loop(2, start, advance, 0)
    for n in range(1, peers):
        scatter_copy(n).wait()
    total = small[own_rows, :]
    for n in range(1, peers):
        total += small_in[n - 1]
    part[...] = total
    for n in range(1, count):
        seq_copy(n).start()
    lax.fori_loop(start, 2 * start, advance, 0)
    for n in range(1, count):
        seq_copy(n).wait()
        total += part_in[n - 1]
    summed[own_rows, :] = total
    for n in range(1, peers):
        gather_copy(n).start()
    lax.fori_loop(2 * start, (count - 1) * pieces + LAG, advance, 0)
    for n in range(1, peers):
        gather_copy(n).wait_send()
        gather_arrival(n).wait_recv()
    small_out[...] = summed[...]
    for n in range(1, count):
        edge_copy(n).wait()
        dec_copy(n).wait()
    for d in range(2):
        edge_out[d] = edge[seq, d].astype(jnp.float32) + sum(
            edge_in[n, d].astype(jnp.float32) for n in range(count - 1)
        )
        dec_out[d] = dec[seq, d].astype(jnp.float32) + sum(
            dec_in[n, d].astype(jnp.float32) for n in range(count - 1)
        )
        for r in range(parts):
            for g in range(own.shape[-1] // span):
                columns = slice(g * span, (g + 1) * span)
                rec_out[d, r, :, columns] = matmul(own[d, seq, r, :, columns], matrix[...], NT)

    def finish(k, carry):
        i, d, r = slot(k)

        @pl.when((i <= count - 2 - place) & ((place > 0) | (k >= (count - 1) * pieces - WINDOW)))
        def _():
            line_copy(k, False).wait_send()

        @pl.when((i < place) & (k < (count // 2) * pieces))
        def _():
            back_copy(k).wait_send()

        return carry

    lax.fori_loop(0, (count - 1) * pieces, finish, 0)


def spread_left(other, letter_grad):
    high = letter_grad.astype(jnp.bfloat16)
    low = (letter_grad - high.astype(jnp.float32)).astype(jnp.bfloat16)
    return matmul(other, high, TN) + matmul(other, low, TN)


def kernel_sums(rec_grad, letter_grad, embed_pad, w_in_pad, matrix, width, letters, dec_grad, stats):
    count = lax.axis_size("seq")
    peers = lax.axis_size("mp")
    columns = rec_grad.shape[-1]
    all_rows = rec_grad.shape[1] * rec_grad.shape[2]
    parts = all_rows // count // PIECE
    units = dec_grad.shape[1]
    edge_rows = -(-(width + 1) // 8) * 8
    small_rows = -(-(2 * TABLE + 16) // (8 * peers)) * 8 * peers
    share = small_rows // peers
    f32, bf16 = jnp.float32, jnp.bfloat16
    dma = pltpu.SemaphoreType.DMA
    shape = jax.ShapeDtypeStruct
    vmem = pl.BlockSpec(memory_space=pltpu.VMEM)
    ones = (jnp.arange(VOCAB_PAD) < letters).astype(bf16)
    embed_one = embed_pad.at[:, :, width].set(ones[None])
    return pl.pallas_call(
        functools.partial(reduce_kernel, width),
        out_shape=(
            shape((2, parts, PIECE, columns), f32),
            shape((2, edge_rows, columns // count), f32),
            shape((2, units // count, VOCAB_PAD), f32),
            shape((small_rows, LANES), f32),
        ),
        in_specs=[pl.BlockSpec(memory_space=pl.ANY)] + [vmem] * 9,
        out_specs=(vmem,) * 4,
        scratch_shapes=[
            pltpu.VMEM((2, count, parts, PIECE, columns), bf16),
            pltpu.VMEM((count - 1, 2, parts, PIECE, columns), bf16),
            pltpu.VMEM((count // 2, 2, parts, PIECE, columns), bf16),
            pltpu.VMEM((count, 2, edge_rows, columns // count), bf16),
            pltpu.VMEM((count - 1, 2, edge_rows, columns // count), bf16),
            pltpu.VMEM((count, 2, units // count, VOCAB_PAD), bf16),
            pltpu.VMEM((count - 1, 2, units // count, VOCAB_PAD), bf16),
            pltpu.VMEM((small_rows, LANES), f32),
            pltpu.VMEM((share, LANES), f32),
            pltpu.VMEM((peers - 1, share, LANES), f32),
            pltpu.VMEM((count - 1, share, LANES), f32),
            pltpu.VMEM((small_rows, LANES), f32),
            dma,
            dma((count - 1, 2, parts)),
            dma((count - 1, 2, parts)),
            dma((count // 2, 2, parts)),
            dma((count // 2, 2, parts)),
            dma((count - 1,)),
            dma((count - 1,)),
            dma((count - 1,)),
            dma((count - 1,)),
            dma((peers - 1,)),
            dma((peers - 1,)),
            dma((count - 1,)),
            dma((count - 1,)),
            dma((peers - 1,)),
            dma((peers,)),
        ],
        compiler_params=pltpu.CompilerParams(
            collective_id=2, has_side_effects=True, vmem_limit_bytes=VMEM_LIMIT
        ),
        name="gradient_sums",
    )(
        rec_grad.reshape(2, count, parts, PIECE, columns), letter_grad, embed_one, w_in_pad, matrix, dec_grad,
        *stats,
    )


def plain_step(ids, lengths, order, count, h_init, c_init, embed, w_in, w_rec, bias, w_dec, b_dec, matrix):
    first_mp = (lax.axis_index("mp") == 0).astype(jnp.float32)
    per_dev, own_units = h_init.shape[1:]
    lanes = matrix.shape[0] // 4
    wd_full = lax.all_gather(w_dec, "mp", axis=1, tiled=True)
    whole_ids = lax.all_gather(ids, "seq", axis=0, tiled=True)
    own_order = lax.dynamic_slice_in_dim(order, lax.axis_index("seq") * per_dev, per_dev)
    slot_ids = jnp.take(whole_ids, own_order, axis=1)
    own_len = jnp.take(lengths, own_order)
    step_ids = jnp.stack([slot_ids, jnp.flip(slot_ids, 0)])
    w_rec_grouped = grouped(w_rec, matrix)
    w_in_grouped = grouped(w_in, matrix)
    bias_grouped = jnp.swapaxes(
        bias.reshape(2, own_units // lanes, lanes, 4), -1, -2
    ).reshape(bias.shape)
    loss, hidden_sq, logit_sq, dec_bias, dec_grad, hidden_grad, cell_grad, rec_grad, letter_grad = recurrences(
        step_ids, own_len, h_init, c_init, embed, w_in_grouped, w_rec_grouped, bias_grouped, w_dec, wd_full,
        b_dec, count, lanes,
    )
    embed_wide = embed.astype(jnp.float32)
    in_grad = jnp.einsum("dve,dvc->dec", embed_wide, letter_grad, precision=lax.Precision.HIGHEST)
    bias_grad = jnp.sum(letter_grad, axis=1, keepdims=True)
    embed_part = jnp.einsum(
        "dvc,dec->dve", letter_grad, w_in_grouped.astype(jnp.float32), precision=lax.Precision.HIGHEST
    )
    edge = ungrouped_wide(jnp.concatenate([in_grad, bias_grad], axis=1), lanes)
    rec_part = lax.psum_scatter(rec_grad.astype(jnp.bfloat16), "seq", scatter_dimension=1, tiled=True)
    edge_part = lax.psum_scatter(edge.astype(jnp.bfloat16), "seq", scatter_dimension=2, tiled=True)
    dec_part = lax.psum_scatter(dec_grad.astype(jnp.bfloat16), "seq", scatter_dimension=1, tiled=True)
    loss_sum, hidden_all, logit_all, dec_bias_grad, embed_grad = lax.psum(
        (loss * first_mp, hidden_sq, logit_sq * first_mp, dec_bias * first_mp, embed_part), ("seq", "mp")
    )
    rec_out = ungrouped(rec_part, matrix).astype(jnp.float32)
    return (
        loss_sum, hidden_all, logit_all, dec_bias_grad, dec_part.astype(jnp.float32), hidden_grad, cell_grad, rec_out,
        edge_part[:, :-1].astype(jnp.float32), edge_part[:, -1].astype(jnp.float32), embed_grad,
    )


def per_device(ids, lengths, order, h_init, c_init, embed, w_in, w_rec, bias, w_dec, b_dec):
    streams = ids.shape[1]
    per_dev, own_units = h_init.shape[1:]
    all_units, letter_count = w_rec.shape[1], embed.shape[1]
    live_total = jnp.sum(lengths).astype(jnp.float32)
    count = 2.0 * (jnp.sum(lengths) - streams).astype(jnp.float32)
    _, matrix = column_order(own_units)
    operands = (ids, lengths, order, count, h_init, c_init, embed, w_in, w_rec, bias, w_dec, b_dec, matrix)
    fits = own_units % LANES == 0 and per_dev % (SPLIT * LANES) == 0 and per_dev <= 256
    fits = fits and all_units % (lax.axis_size("seq") * PIECE) == 0 and letter_count <= TABLE
    if lax.axis_size("mp") == 8 and lax.axis_size("seq") == 4 and fits:
        results = kernel_step(*operands)
    else:
        results = plain_step(*operands)
    (
        loss_sum, hidden_all, logit_all, dec_bias_grad, dec_part, hidden_grad, cell_grad, rec_out, in_out, bias_out,
        embed_grad,
    ) = results
    embed_wide = embed.astype(jnp.float32)
    rms_embed = jnp.sqrt(jnp.mean(embed_wide * embed_wide, axis=(1, 2)))
    return (
        loss_sum / count,
        hidden_grad,
        cell_grad,
        embed_grad,
        in_out,
        rec_out,
        bias_out,
        dec_part,
        dec_bias_grad,
        rms_embed,
        jnp.sqrt(hidden_all / (all_units * live_total)),
        jnp.sqrt(logit_all / (letter_count * count / 2.0)),
    )


def solution(mesh):
    in_specs = (
        P("seq", None),
        P(),
        P(),
        P(None, "seq", "mp"),
        P(None, "seq", "mp"),
        P(),
        P(None, None, "mp"),
        P(None, None, "mp"),
        P(None, "mp"),
        P(None, "mp", None),
        P(),
    )
    out_specs = (
        P(),
        P(None, "seq", "mp"),
        P(None, "seq", "mp"),
        P(),
        P(None, None, ("mp", "seq")),
        P(None, "seq", "mp"),
        P(None, ("mp", "seq")),
        P(None, ("mp", "seq"), None),
        P(),
        P(),
        P(),
        P(),
    )
    return jax.shard_map(
        per_device, mesh=mesh, in_specs=in_specs, out_specs=out_specs, check_vma=False
    )
```

```python
import functools

import jax
import jax.numpy as jnp
from jax import lax
from jax.experimental import pallas as pl
from jax.experimental.pallas import tpu as pltpu
from jax.sharding import PartitionSpec as P

VMEM_LIMIT = 58 * 2**20


def column_order(own_units):
    lanes = min(128, own_units)
    source = jnp.arange(4 * lanes, dtype=jnp.int32)
    place = (source % 4) * lanes + source // 4
    matrix = (place[:, None] == jnp.arange(4 * lanes, dtype=jnp.int32)[None, :]).astype(jnp.bfloat16)
    return lanes, matrix


def grouped(x, matrix):
    width = matrix.shape[0]
    parts = x.reshape(x.shape[:-1] + (x.shape[-1] // width, width))
    out = jnp.einsum("...gc,cp->...gp", parts, matrix, preferred_element_type=jnp.float32)
    return out.astype(x.dtype).reshape(x.shape)


def ungrouped(x, matrix):
    return grouped(x, matrix.T)


def ungrouped_wide(x, lanes):
    parts = x.reshape(x.shape[:-1] + (x.shape[-1] // (4 * lanes), 4, lanes))
    return jnp.swapaxes(parts, -1, -2).reshape(x.shape)


def gates_of(pre, lanes):
    parts = pre.reshape(pre.shape[:-1] + (pre.shape[-1] // (4 * lanes), 4, lanes))
    flat = pre.shape[:-1] + (pre.shape[-1] // 4,)
    return tuple(parts[..., k, :].reshape(flat) for k in range(4))


def joined_gates(gates, lanes):
    split = [g.reshape(g.shape[:-1] + (g.shape[-1] // lanes, 1, lanes)) for g in gates]
    joined = jnp.concatenate(split, axis=-2)
    return joined.reshape(gates[0].shape[:-1] + (4 * gates[0].shape[-1],))


def recurrences(step_ids, own_len, h_init, c_init, embed, w_in, w_rec, bias, w_dec, wd_full, b_dec, count, lanes):
    length, per_dev = step_ids.shape[1:]
    letter_count = embed.shape[1]
    steps = jnp.arange(length, dtype=jnp.int32)
    live_steps = jnp.stack(
        [steps[:, None] < own_len[None, :], (length - 1 - steps)[:, None] < own_len[None, :]], axis=1
    )[..., None]
    letters = jnp.arange(letter_count, dtype=jnp.int32)
    onehot = (jnp.swapaxes(step_ids, 0, 1)[..., None] == letters).astype(jnp.bfloat16)
    letter_rows = jnp.einsum(
        "sdbv,dve->sdbe", onehot, embed, preferred_element_type=jnp.float32
    ).astype(jnp.bfloat16)
    gates_in = jnp.einsum(
        "sdbe,dec->sdbc", letter_rows, w_in, preferred_element_type=jnp.float32
    ).astype(jnp.bfloat16)

    def forward_step(carry, inputs):
        hidden, cell = carry
        gate_in, live = inputs
        whole = lax.all_gather(hidden, "mp", axis=2, tiled=True)
        recurrent = jnp.einsum("dbh,dhc->dbc", whole, w_rec, preferred_element_type=jnp.float32)
        pre = gate_in.astype(jnp.float32) + recurrent + bias[:, None]
        in_pre, forget_pre, cell_pre, out_pre = gates_of(pre, lanes)
        in_gate, forget, out_gate = (jax.nn.sigmoid(x) for x in (in_pre, forget_pre, out_pre))
        cell_gate = jnp.tanh(cell_pre)
        new_cell = forget * cell + in_gate * cell_gate
        cell_next = jnp.where(live, new_cell, cell)
        hidden_next = jnp.where(
            live, out_gate * jnp.tanh(new_cell), hidden.astype(jnp.float32)
        ).astype(jnp.bfloat16)
        return ((hidden_next, cell_next), (whole, cell, in_gate, forget, cell_gate, out_gate))

    (last_hidden, last_cell), (wholes, cells, *gates) = lax.scan(
        forward_step, (h_init, c_init), (gates_in, live_steps)
    )
    last_whole = lax.all_gather(last_hidden, "mp", axis=2, tiled=True)
    after = jnp.concatenate([wholes[1:], last_whole[None]], axis=0)
    own = h_init.shape[2]
    mine = lax.dynamic_slice_in_dim(after, lax.axis_index("mp") * own, own, axis=3)
    mine_wide = mine.astype(jnp.float32)
    hidden_sq = jnp.sum(jnp.where(live_steps, mine_wide * mine_wide, 0.0), axis=(0, 2, 3))
    logits = (
        jnp.einsum("sdbh,dhv->sdbv", after, wd_full, preferred_element_type=jnp.float32) + b_dec[None, :, None]
    )
    targets = jnp.swapaxes(jnp.concatenate([step_ids[:, 1:], step_ids[:, :1]], axis=1), 0, 1)
    fore_valid = (steps[:, None] + 1 < own_len[None, :])
    back_valid = (steps[:, None] < length - 1) & ((length - 1 - steps)[:, None] < own_len[None, :])
    valid = jnp.stack([fore_valid, back_valid], axis=1).astype(jnp.float32)
    logit_sq = jnp.sum(valid[..., None] * logits * logits, axis=(0, 2, 3))
    top = jnp.max(logits, axis=-1, keepdims=True)
    log_total = top + jnp.log(jnp.sum(jnp.exp(logits - top), axis=-1, keepdims=True))
    target_hot = targets[..., None] == letters
    picked = jnp.sum(jnp.where(target_hot, logits, 0.0), axis=-1)
    loss = jnp.sum(valid * (log_total[..., 0] - picked))
    grad_logits = (
        valid[..., None] * (jnp.exp(logits - log_total) - target_hot.astype(jnp.float32)) / count
    ).astype(jnp.bfloat16)
    dec_bias = jnp.sum(grad_logits.astype(jnp.float32), axis=(0, 2))
    dec_grad = jnp.einsum("sdbh,sdbv->dhv", mine, grad_logits, preferred_element_type=jnp.float32)

    def backward_step(carry, inputs):
        grad_hidden, grad_cell = carry
        live, cell, in_gate, forget, cell_gate, out_gate, grad_logit = inputs
        grad_hidden = grad_hidden + jnp.einsum(
            "dbv,dhv->dbh", grad_logit, w_dec, preferred_element_type=jnp.float32
        )
        squash = jnp.tanh(forget * cell + in_gate * cell_gate)
        grad_new = jnp.where(live, grad_cell + grad_hidden * out_gate * (1.0 - squash * squash), 0.0)
        grad_out = jnp.where(live, grad_hidden * squash, 0.0)
        grad_pre = joined_gates(
            [
                grad_new * cell_gate * in_gate * (1.0 - in_gate),
                grad_new * cell * forget * (1.0 - forget),
                grad_new * in_gate * (1.0 - cell_gate * cell_gate),
                grad_out * out_gate * (1.0 - out_gate),
            ],
            lanes,
        ).astype(jnp.bfloat16)
        grad_cell_prev = grad_new * forget + jnp.where(live, 0.0, grad_cell)
        held = jnp.where(live, 0.0, grad_hidden)
        terms = jnp.einsum("dbc,dhc->dbh", grad_pre, w_rec, preferred_element_type=jnp.float32)
        through = lax.psum_scatter(
            terms.astype(jnp.bfloat16), "mp", scatter_dimension=2, tiled=True
        ).astype(jnp.float32)
        return ((held + through, grad_cell_prev), grad_pre)

    start = jnp.zeros(c_init.shape, jnp.float32)
    (hidden_grad, cell_grad), grad_pres = lax.scan(
        backward_step, (start, start), (live_steps, cells, *gates, grad_logits), reverse=True
    )
    rec_grad = jnp.einsum("sdbh,sdbc->dhc", wholes, grad_pres, preferred_element_type=jnp.float32)
    letter_grad = jnp.einsum("sdbv,sdbc->dvc", onehot, grad_pres, preferred_element_type=jnp.float32)
    return loss, hidden_sq, logit_sq, dec_bias, dec_grad, hidden_grad, cell_grad, rec_grad, letter_grad


MESH = pl.DeviceIdType.MESH
LANES = 128
VOCAB_PAD = 384
NT = (((1,), (1,)), ((), ()))
TN = (((0,), (0,)), ((), ()))


def sigmoid(x):
    return 0.5 * jnp.tanh(0.5 * x) + 0.5


def matmul(left, right, dims=(((1,), (0,)), ((), ()))):
    return lax.dot_general(left, right, dims, preferred_element_type=jnp.float32)


def neighbours():
    me = lax.axis_index("mp")
    row, column, core = me // 4, (me // 2) % 2, me % 2
    sibling = row * 4 + column * 2 + (1 - core)
    across = (1 - row) * 4 + (1 - column) * 2 + core
    side = row * 4 + (1 - column) * 2 + core
    up = (1 - row) * 4 + column * 2 + core
    return me, sibling, (across, side, up)


def greet(peers, seqs=0):
    seq, me = lax.axis_index("seq"), lax.axis_index("mp")
    barrier = pltpu.get_barrier_semaphore()
    for peer in peers:
        pl.semaphore_signal(barrier, inc=1, device_id=(seq, peer), device_id_type=MESH)
    for n in range(1, seqs):
        pl.semaphore_signal(barrier, inc=1, device_id=((seq + n) % seqs, me), device_id_type=MESH)
    pl.semaphore_wait(barrier, len(peers) + max(seqs - 1, 0))


def remote(src, dst, send, recv, peer):
    return pltpu.make_async_remote_copy(
        src_ref=src, dst_ref=dst, send_sem=send, recv_sem=recv,
        device_id=(lax.axis_index("seq"), peer), device_id_type=MESH,
    )


def other_core(peer):
    return (peer // 2) * 2 + (1 - peer % 2)


def folded(x):
    return jnp.sum(x.reshape(x.shape[0] // 8, 8, x.shape[1]), axis=0)


def regroup_matrix(span):
    source = lax.broadcasted_iota(jnp.int32, (span, span), 0)
    place = (source & 3) * (span // 4) + (source >> 2)
    return (place == lax.broadcasted_iota(jnp.int32, (span, span), 1)).astype(jnp.bfloat16)


def padded(ref, value):
    ref[...] = jnp.zeros(ref.shape, ref.dtype)
    for d in range(2):
        ref[d, :value.shape[1], :value.shape[2]] = value[d]


def column_of(table, lane):
    lanes = lax.broadcasted_iota(jnp.int32, table.shape, 1)
    return jnp.sum(jnp.where(lanes == lane, table, 0.0), axis=1, keepdims=True)


def time_of(direction, step, length):
    return step if direction == 0 else length - 1 - step


def forward_kernel(
    length, letters, ids_in, lens, order, h_in, c_in, embed_in, w_in_raw, bias, b_dec_in, w_dec_in, w_hbm,
    wholes, acts, grads, w_out, loss, logit_sq, hidden_sq, dec_bias, dec_grad, info, ids, w_in,
    w, wd, buf, cell, acc, logit, stage, grad, all_ids, table, matrix, embed, b_dec, inverse, load_sem, ids_send, ids_recv, wd_send, wd_recv,
    send_sem, recv_sem, save_sem, act_sem, grad_sem,
):
    me, sibling, peers = neighbours()
    seq, seqs, times = lax.axis_index("seq"), all_ids.shape[0], ids_in.shape[0]
    blocks, rows, units = buf.shape[2:]
    groups, span = units // LANES, matrix.shape[0]
    columns = w.shape[-1]
    load_w = pltpu.make_async_copy(w_hbm, w, load_sem.at[0])
    store_w = pltpu.make_async_copy(w, w_out, load_sem.at[1])
    load_w.start()
    all_ids[seq, :times] = ids_in[...].astype(jnp.float32)
    matrix[...] = regroup_matrix(span)
    for s in range(2):
        buf[s, 0, me] = h_in[s]
    greet((sibling,) + peers, seqs)

    def ids_copy(n):
        to = (seq + n) % seqs
        block = all_ids.at[seq]
        return pltpu.make_async_remote_copy(
            src_ref=block, dst_ref=block, send_sem=ids_send.at[n - 1], recv_sem=ids_recv.at[seq],
            device_id=(to, me), device_id_type=MESH,
        )

    def ids_arrival(n):
        source = (seq + n) % seqs
        block = all_ids.at[source]
        return pltpu.make_async_remote_copy(
            src_ref=block, dst_ref=block, send_sem=ids_send.at[n - 1], recv_sem=ids_recv.at[source],
            device_id=(source, me), device_id_type=MESH,
        )

    across, side, up = peers
    depth = rows // 2

    def transfer(s, step, block, h, index, peer):
        slot, par = step % 3, step % 2
        ref = buf.at[s, slot, block, h * depth:(h + 1) * depth]
        return remote(ref, ref, send_sem.at[s, par, index], recv_sem.at[s, slot, block, h], peer)

    def transfer_whole(s, step, block, index):
        slot, par = step % 3, step % 2
        ref = buf.at[s, slot, block]
        return remote(ref, ref, send_sem.at[s, par, index], recv_sem.at[s, slot, block, 0], sibling)

    def direct(s, step):
        plan = ((0, side), (1, up), (1, side), (0, up))
        return [transfer(s, step, me, h, n, peer) for n, (h, peer) in enumerate(plan)]

    def pass_on(s, step):
        for n, (block, h, peer) in enumerate(((side, 0, up), (up, 1, side))):
            transfer(s, step, block, h, 0, sibling).wait_recv()
            transfer(s, step, block, h, 4 + n, peer).start()

    def core_copies(s, step):
        return [transfer_whole(s, step, block, 6 + n) for n, block in enumerate((me, side, up, across))]

    def wd_copy(n):
        peer = (peers + (sibling,))[n]
        return remote(wd.at[me], wd.at[me], wd_send.at[n], wd_recv.at[me], peer)

    def wd_relay(n):
        block = wd.at[peers[n]]
        return remote(block, block, wd_send.at[4 + n], wd_recv.at[peers[n]], sibling)

    def wd_arrival(source):
        return remote(wd.at[source], wd.at[source], wd_send.at[0], wd_recv.at[source], sibling)

    def save(s, step):
        return pltpu.make_async_copy(buf.at[s, step % 3], wholes.at[step, s], save_sem.at[s, step % 2])

    def save_acts(s, step):
        return pltpu.make_async_copy(stage.at[s], acts.at[step, s], act_sem.at[s])

    def save_grad(s, step):
        return pltpu.make_async_copy(grad.at[s], grads.at[step, s], grad_sem.at[s])

    def finish_sends(s, step):
        for copy in direct(s, step) + core_copies(s, step):
            copy.wait_send()
        for n, (block, h, peer) in enumerate(((side, 0, up), (up, 1, side))):
            transfer(s, step, block, h, 4 + n, peer).wait_send()

    for n in range(1, seqs):
        ids_copy(n).start()
    for s in range(2):
        for copy in direct(s, 0):
            copy.start()
        transfer_whole(s, 0, me, 6).start()
    padded(wd.at[me], w_dec_in)
    for n in range(4):
        wd_copy(n).start()
    padded(embed, embed_in)
    padded(w_in, w_in_raw)
    b_dec[...] = jnp.full(b_dec.shape, -1e30, jnp.float32)
    for d in range(2):
        b_dec[d, :, :letters] = b_dec_in[d:d + 1]
    lengths = lens[...].astype(jnp.float32)
    inverse[...] = 0.5 / (jnp.sum(lengths, axis=1, keepdims=True) - lens.shape[1])
    for ref in (loss, logit_sq, hidden_sq, dec_bias, dec_grad):
        ref[...] = jnp.zeros(ref.shape, ref.dtype)
    cell[...] = c_in[...]
    for d in range(2):
        for g in range(columns // span):
            part = slice(g * span, (g + 1) * span)
            w_in[d, :, part] = matmul(w_in[d, :, part], matrix[...]).astype(jnp.bfloat16)
    load_w.wait()

    def regroup(b, carry):
        for d in range(2):
            for g in range(columns // span):
                part = slice(g * span, (g + 1) * span)
                w[d, b, :, part] = matmul(w[d, b, :, part], matrix[...]).astype(jnp.bfloat16)
        return carry

    lax.fori_loop(0, blocks, regroup, 0)
    store_w.start()
    for n in range(1, seqs):
        ids_arrival(n).wait_recv()
    streams = rows
    order_row = order[:, pl.ds(pl.multiple_of(seq * rows, LANES), rows)]
    square = (rows, rows)
    diagonal = lax.broadcasted_iota(jnp.int32, square, 0) == lax.broadcasted_iota(jnp.int32, square, 1)
    order_column = jnp.sum(
        jnp.where(diagonal, jnp.broadcast_to(order_row.astype(jnp.float32), square), 0.0), axis=1, keepdims=True
    ).astype(jnp.int32)
    total_streams = lens.shape[1]
    pick_column = (
        lax.broadcasted_iota(jnp.int32, (streams, total_streams), 1) == order_column
    ).astype(jnp.bfloat16)
    pick_row = (
        lax.broadcasted_iota(jnp.int32, (total_streams, streams), 0) == order_row
    ).astype(jnp.bfloat16)
    table[...] = jnp.zeros(table.shape, table.dtype)
    for d in range(2):
        for t in range(length):
            row = t if d == 0 else length - 1 - t
            table[t:t + 1] = all_ids[row // times, row % times:row % times + 1]
        table[LANES - 1:] = lengths
        high = jnp.floor(table[...] * (1.0 / 16.0))
        low = (table[...] - 16.0 * high).astype(jnp.bfloat16)
        high = high.astype(jnp.bfloat16)
        values = 16.0 * matmul(pick_column, high, NT) + matmul(pick_column, low, NT)
        info[d] = values
        values = 16.0 * matmul(high[:length], pick_row) + matmul(low[:length], pick_row)
        ids[d] = values

    def gates(s, step):
        slot, later = step % 3, (step + 1) % 3
        d = s
        when = time_of(d, step, length)
        live = info[s, :, LANES - 1:] > when.astype(jnp.float32)
        for g in range(groups):
            lanes = slice(g * LANES, (g + 1) * LANES)
            pre = [acc[:, (4 * g + k) * LANES:(4 * g + k + 1) * LANES] for k in range(4)]
            in_gate, forget, out_gate = sigmoid(pre[0]), sigmoid(pre[1]), sigmoid(pre[3])
            cell_gate = jnp.tanh(pre[2])
            old = cell[s, :, lanes]
            new = forget * old + in_gate * cell_gate
            for k, value in enumerate((in_gate, forget, cell_gate, out_gate, old)):
                stage[s, k, :, lanes] = value
            cell[s, :, lanes] = jnp.where(live, new, old)
            before = buf[s, slot, me, :, lanes].astype(jnp.float32)
            hidden = jnp.where(live, out_gate * jnp.tanh(new), before).astype(jnp.bfloat16)
            buf[s, later, me, :, lanes] = hidden
            wide = hidden.astype(jnp.float32)
            hidden_sq[d] += folded(jnp.where(live, wide * wide, 0.0))

    def decode(s, step):
        slot = step % 3
        d = s
        total = jnp.broadcast_to(b_dec[d], logit.shape)
        for b in range(blocks):
            total += matmul(buf[s, slot, b], wd[b, d])
        logit[...] = total
        when = time_of(d, step - 1, length)
        reach = when + 1 if d == 0 else when
        lookup = info[s]
        valid = (lookup[:, LANES - 1:] > reach.astype(jnp.float32)) & (step < length)
        target = column_of(lookup, step)
        value = logit[...]
        lanes = lax.broadcasted_iota(jnp.int32, value.shape, 1)
        hot = lanes.astype(jnp.float32) == target
        top = jnp.max(value, axis=1, keepdims=True)
        power = jnp.exp(value - top)
        total = jnp.sum(power, axis=1, keepdims=True)
        picked = jnp.sum(jnp.where(hot, value, 0.0), axis=1, keepdims=True)
        loss[d] += folded(jnp.broadcast_to(jnp.where(valid, top + jnp.log(total) - picked, 0.0), (rows, LANES)))
        kept = jnp.where(valid & (lanes < letters), value, 0.0)
        square = kept * kept
        logit_sq[d] += folded(sum(square[:, n * LANES:(n + 1) * LANES] for n in range(VOCAB_PAD // LANES)))
        slope = jnp.where(
            valid, (power * (1.0 / total) - jnp.where(hot, 1.0, 0.0)) * inverse[...], 0.0
        ).astype(jnp.bfloat16)
        grad[s] = slope
        dec_bias[d] += folded(slope.astype(jnp.float32))
        dec_grad[d] += matmul(buf[s, slot, me], grad[s], TN)

    others = tuple(other_core(peer) for peer in peers)

    def half(step, s):
        d = s

        @pl.when(step < length)
        def _():
            now = column_of(info[s], step)
            hot = (lax.broadcasted_iota(jnp.int32, (rows, VOCAB_PAD), 1).astype(jnp.float32) == now)
            row = matmul(hot.astype(jnp.bfloat16), embed[d]).astype(jnp.bfloat16)
            acc[...] = matmul(row, w_in[d]).astype(jnp.bfloat16).astype(jnp.float32) + bias[d]

        for n, (block, halves) in enumerate(((side, (1,)), (up, (0,)), (across, (0, 1)))):
            for h in halves:
                transfer(s, step, block, h, 0, sibling).wait_recv()
            transfer_whole(s, step, block, 7 + n).start()

        if s == 0:
            @pl.when(step == 1)
            def _():
                for n, peer in enumerate(peers):
                    wd_arrival(peer).wait_recv()
                    wd_relay(n).start()

        slot = step % 3

        def advance(block):
            acc[...] += matmul(buf[s, slot, block], w[d, block])

        @pl.when(step < length)
        def _():
            for block in (me,) + peers:
                advance(block)

        for block in (sibling,) + others:
            transfer_whole(s, step, block, 6).wait_recv()

        @pl.when(step < length)
        def _():
            for block in (sibling,) + others:
                advance(block)

        if s == 0:
            pass_on(1, step)
        else:
            @pl.when(step < length)
            def _():
                pass_on(0, step + 1)

        @pl.when(step < length)
        def _():

            @pl.when(step > 0)
            def _():
                save_acts(s, step - 1).wait()

            gates(s, step)

            @pl.when(step > 0)
            def _():
                save(s, step - 1).wait()
                finish_sends(s, step - 1)

            for copy in direct(s, step + 1):
                copy.start()
            transfer_whole(s, step + 1, me, 6).start()
            save_acts(s, step).start()
            save(s, step).start()

        if s == 0:
            @pl.when(step == 1)
            def _():
                for block in (sibling,) + others:
                    wd_arrival(block).wait_recv()

        @pl.when(step > 0)
        def _():
            @pl.when(step > 1)
            def _():
                save_grad(s, step - 2).wait()

            decode(s, step)
            save_grad(s, step - 1).start()

    def every(step, carry):
        for s in range(2):
            half(step, s)
        return carry

    pass_on(0, 0)
    lax.fori_loop(0, length + 1, every, 0)
    store_w.wait()
    for n in range(1, seqs):
        ids_copy(n).wait_send()
    for n in range(4):
        wd_copy(n).wait_send()
    for n in range(3):
        wd_relay(n).wait_send()
    for s in range(2):
        save(s, length - 1).wait()
        save_acts(s, length - 1).wait()
        save_grad(s, length - 1).wait()
        finish_sends(s, length - 1)
        finish_sends(s, length)


def backward_kernel(
    length, info, ids, w_dec_in, dec_grad, acts, grads, wholes, w_hbm,
    rec_out, letter_grad, hidden_grad, cell_grad, dec_out,
    w, rec, stage, grad, whole, pre, held, own, sent, got, passed, taken, kept, middle, w_dec, dec, dec_in, load_sem, act_sem,
    grad_sem, whole_sem, core_send, core_recv, chip_send, chip_recv, middle_send, middle_recv, dec_send, dec_recv,
):
    me, sibling, peers = neighbours()
    rows, units = held.shape[1:]
    groups = units // LANES
    load_w = pltpu.make_async_copy(w_hbm, w, load_sem)
    load_w.start()

    def load_acts(s, step):
        return pltpu.make_async_copy(acts.at[step, s], stage.at[s], act_sem.at[s])

    def load_grad(s, step):
        return pltpu.make_async_copy(grads.at[step, s], grad.at[s], grad_sem.at[s])

    def load_whole(s, step):
        return pltpu.make_async_copy(wholes.at[step, s], whole.at[s], whole_sem.at[s])

    for s in range(2):
        load_acts(s, length - 1).start()
        load_grad(s, length - 1).start()
        load_whole(s, length - 1).start()
    seq, seqs, tall = lax.axis_index("seq"), dec.shape[0], dec.shape[2]
    for q in range(seqs):
        for d in range(2):
            dec[q, d] = dec_grad[d, q * tall:(q + 1) * tall].astype(jnp.bfloat16)
    greet((sibling,) + peers, seqs)

    def dec_copy(n):
        to = (seq + n) % seqs
        return pltpu.make_async_remote_copy(
            src_ref=dec.at[to], dst_ref=dec_in.at[n - 1], send_sem=dec_send.at[n - 1], recv_sem=dec_recv.at[n - 1],
            device_id=(to, me), device_id_type=MESH,
        )

    for n in range(1, seqs):
        dec_copy(n).start()
    padded(w_dec, w_dec_in)
    held[...] = jnp.zeros(held.shape, held.dtype)
    own[...] = jnp.zeros(own.shape, own.dtype)
    cell_grad[...] = jnp.zeros(cell_grad.shape, cell_grad.dtype)
    letter_grad[...] = jnp.zeros(letter_grad.shape, letter_grad.dtype)

    def clear(b, carry):
        for d in range(2):
            rec[d, b] = jnp.zeros(rec.shape[2:], rec.dtype)
        return carry

    lax.fori_loop(0, w.shape[1], clear, 0)
    load_w.wait()

    def to_core(s, turn, n):
        return remote(
            sent.at[s, n], got.at[s, turn % 2, n], core_send.at[s, n], core_recv.at[s, turn % 2, n], sibling
        )

    across, side, up = peers
    depth = rows // 2

    def to_chip(s, turn, n, h):
        part = slice(h * depth, (h + 1) * depth)
        return remote(
            passed.at[s, n, part], taken.at[s, turn % 2, n - 1, part],
            chip_send.at[s, n - 1, h], chip_recv.at[s, turn % 2, n - 1, h], peers[n],
        )

    def to_middle(s, turn, h):
        return remote(
            passed.at[s, 0, h * depth:(h + 1) * depth], middle.at[s, turn % 2, h],
            middle_send.at[s, h], middle_recv.at[s, turn % 2, h], peers[1 + h],
        )

    def chip_copies(s, turn):
        return [to_chip(s, turn, n, h) for n in (1, 2) for h in range(2)]

    def pass_on(s, turn):
        for h in range(2):
            to_middle(s, turn, h).wait_recv()
            total = kept[s, h] + middle[s, turn % 2, h].astype(jnp.float32)
            passed[s, 2 - h, h * depth:(h + 1) * depth] = total.astype(jnp.bfloat16)
            to_chip(s, turn, 2 - h, h).start()

    def half(turn, s):
        step = length - 1 - turn
        d = s
        when = time_of(d, step, length)
        load_acts(s, step).wait()
        load_grad(s, step).wait()
        held[s] += matmul(grad[s], w_dec[d], NT)

        @pl.when(turn > 0)
        def _():
            for copy in chip_copies(s, turn - 1):
                copy.wait_recv()

        live = info[s, :, LANES - 1:] > when.astype(jnp.float32)
        for g in range(groups):
            lanes = slice(g * LANES, (g + 1) * LANES)
            through = own[s, :, lanes]
            for n in range(2):
                through += jnp.where(turn > 0, taken[s, (turn + 1) % 2, n, :, lanes].astype(jnp.float32), 0.0)
            total = held[s, :, lanes] + through
            in_gate, forget, cell_gate, out_gate, old = (stage[s, k, :, lanes] for k in range(5))
            squash = jnp.tanh(forget * old + in_gate * cell_gate)
            later = cell_grad[s, :, lanes]
            new = jnp.where(live, later + total * out_gate * (1.0 - squash * squash), 0.0)
            out = jnp.where(live, total * squash, 0.0)
            values = (
                new * cell_gate * in_gate * (1.0 - in_gate),
                new * old * forget * (1.0 - forget),
                new * in_gate * (1.0 - cell_gate * cell_gate),
                out * out_gate * (1.0 - out_gate),
            )
            for k, value in enumerate(values):
                pre[s, :, (4 * g + k) * LANES:(4 * g + k + 1) * LANES] = value.astype(jnp.bfloat16)
            cell_grad[s, :, lanes] = new * forget + jnp.where(live, 0.0, later)
            held[s, :, lanes] = jnp.where(live, 0.0, total)

        if s == 0:
            @pl.when(turn > 0)
            def _():
                pass_on(1, turn - 1)
        else:
            pass_on(0, turn)

        @pl.when(turn > 0)
        def _():
            for n in range(4):
                to_core(s, turn - 1, n).wait_send()
            for h in range(2):
                to_middle(s, turn - 1, h).wait_send()
            for copy in chip_copies(s, turn - 1):
                copy.wait_send()

        for n, block in enumerate(tuple(other_core(peer) for peer in peers) + (sibling,)):
            sent[s, n] = matmul(pre[s], w[d, block], NT).astype(jnp.bfloat16)
            to_core(s, turn, n).start()
        for n, block in enumerate(peers + (me,)):
            part = matmul(pre[s], w[d, block], NT)
            to_core(s, turn, n).wait_recv()
            part += got[s, turn % 2, n].astype(jnp.float32)
            if n == 0:
                passed[s, 0] = part.astype(jnp.bfloat16)
                for h in range(2):
                    to_middle(s, turn, h).start()
            elif n < 3:
                now, later = n - 1, 2 - n
                kept[s, later] = part[later * depth:(later + 1) * depth]
                passed[s, n, now * depth:(now + 1) * depth] = (
                    part[now * depth:(now + 1) * depth].astype(jnp.bfloat16)
                )
                to_chip(s, turn, n, now).start()
            else:
                own[s] = part

        @pl.when(turn < length - 1)
        def _():
            load_acts(s, step - 1).start()
            load_grad(s, step - 1).start()

        load_whole(s, step).wait()
        for b in range(w.shape[1]):
            rec[s, b] += matmul(whole[s, b], pre[s], TN)

        @pl.when(turn < length - 1)
        def _():
            load_whole(s, step - 1).start()

        letters = lax.broadcasted_iota(jnp.int32, (VOCAB_PAD, rows), 0).astype(jnp.float32)
        hot = letters == ids[s, pl.ds(step, 1), :]
        letter_grad[s] += matmul(hot.astype(jnp.bfloat16), pre[s])

    def every(turn, carry):
        for s in range(2):
            half(turn, s)
        return carry

    lax.fori_loop(0, length, every, 0)
    pass_on(1, length - 1)
    for n in range(1, seqs):
        dec_copy(n).wait()
    for d in range(2):
        dec_out[d] = dec[seq, d].astype(jnp.float32) + sum(
            dec_in[n, d].astype(jnp.float32) for n in range(seqs - 1)
        )
    for s in range(2):
        for copy in chip_copies(s, length - 1):
            copy.wait_recv()
        total = held[s] + own[s]
        for n in range(2):
            total += taken[s, (length - 1) % 2, n].astype(jnp.float32)
        hidden_grad[s] = total
        for n in range(4):
            to_core(s, length - 1, n).wait_send()
        for h in range(2):
            to_middle(s, length - 1, h).wait_send()
        for copy in chip_copies(s, length - 1):
            copy.wait_send()

    def narrow(b, carry):
        for d in range(2):
            w[d, b] = rec[d, b].astype(jnp.bfloat16)
        return carry

    lax.fori_loop(0, w.shape[1], narrow, 0)
    store = pltpu.make_async_copy(w, rec_out, load_sem)
    store.start()
    store.wait()


def kernel_step(ids, lengths, order, h_init, c_init, embed, w_in, w_rec, bias, w_dec, b_dec):
    seqs = lax.axis_size("seq")
    local_times, all_streams = ids.shape
    length = local_times * seqs
    rows, units = h_init.shape[1:]
    streams = 2
    letters, width = embed.shape[1:]
    columns = w_rec.shape[2]
    blocks = w_rec.shape[1] // units
    any_space, vmem = pl.BlockSpec(memory_space=pl.ANY), pl.BlockSpec(memory_space=pltpu.VMEM)
    bias_grouped = jnp.swapaxes(bias.reshape(2, units // LANES, LANES, 4), -1, -2).reshape(2, 1, columns)
    f32, bf16 = jnp.float32, jnp.bfloat16
    dma = pltpu.SemaphoreType.DMA
    shape = jax.ShapeDtypeStruct
    wholes, acts, grads, w_grouped, loss, logit_sq, hidden_sq, dec_bias, dec_grad, info, slot_ids, w_in_grouped = pl.pallas_call(
        functools.partial(forward_kernel, length, letters),
        out_shape=(
            shape((length, streams, blocks, rows, units), bf16),
            shape((length, streams, 5, rows, units), f32),
            shape((length, streams, rows, VOCAB_PAD), bf16),
            shape((2, blocks, units, columns), bf16),
            shape((2, 8, LANES), f32),
            shape((2, 8, LANES), f32),
            shape((2, 8, LANES), f32),
            shape((2, 8, VOCAB_PAD), f32),
            shape((2, units, VOCAB_PAD), f32),
            shape((streams, rows, LANES), f32),
            shape((streams, length, rows), f32),
            shape((2, LANES, columns), bf16),
        ),
        in_specs=[vmem] * 10 + [any_space],
        out_specs=(any_space,) * 4 + (vmem,) * 8,
        scratch_shapes=[
            pltpu.VMEM((2, blocks, units, columns), bf16),
            pltpu.VMEM((blocks, 2, units, VOCAB_PAD), bf16),
            pltpu.VMEM((streams, 3, blocks, rows, units), bf16),
            pltpu.VMEM((streams, rows, units), f32),
            pltpu.VMEM((rows, columns), f32),
            pltpu.VMEM((rows, VOCAB_PAD), f32),
            pltpu.VMEM((streams, 5, rows, units), f32),
            pltpu.VMEM((streams, rows, VOCAB_PAD), bf16),
            pltpu.VMEM((seqs, 8, all_streams), f32),
            pltpu.VMEM((LANES, all_streams), f32),
            pltpu.VMEM((4 * LANES, 4 * LANES), bf16),
            pltpu.VMEM((2, VOCAB_PAD, LANES), bf16),
            pltpu.VMEM((2, 1, VOCAB_PAD), f32),
            pltpu.VMEM((1, 1), f32),
            dma((2,)),
            dma((seqs - 1,)),
            dma((seqs,)),
            dma((7,)),
            dma((blocks,)),
            dma((streams, 2, 10)),
            dma((streams, 3, blocks, 2)),
            dma((streams, 2)),
            dma((streams,)),
            dma((streams,)),
        ],
        compiler_params=pltpu.CompilerParams(
            collective_id=0, has_side_effects=True, vmem_limit_bytes=VMEM_LIMIT
        ),
        name="forward_visits",
    )(
        ids, lengths[None], order[None], h_init, c_init, embed, w_in, bias_grouped, b_dec, w_dec,
        w_rec.reshape(2, blocks, units, columns),
    )
    rec_grad, letter_grad, hidden_grad, cell_grad, dec_part = pl.pallas_call(
        functools.partial(backward_kernel, length),
        out_shape=(
            shape((2, blocks, units, columns), bf16),
            shape((2, VOCAB_PAD, columns), f32),
            shape((streams, rows, units), f32),
            shape((streams, rows, units), f32),
            shape((2, units // seqs, VOCAB_PAD), f32),
        ),
        in_specs=[vmem] * 4 + [any_space] * 4,
        out_specs=(any_space,) + (vmem,) * 4,
        scratch_shapes=[
            pltpu.VMEM((2, blocks, units, columns), bf16),
            pltpu.VMEM((2, blocks, units, columns), f32),
            pltpu.VMEM((streams, 5, rows, units), f32),
            pltpu.VMEM((streams, rows, VOCAB_PAD), bf16),
            pltpu.VMEM((streams, blocks, rows, units), bf16),
            pltpu.VMEM((streams, rows, columns), bf16),
            pltpu.VMEM((streams, rows, units), f32),
            pltpu.VMEM((streams, rows, units), f32),
            pltpu.VMEM((streams, 4, rows, units), bf16),
            pltpu.VMEM((streams, 2, 4, rows, units), bf16),
            pltpu.VMEM((streams, 3, rows, units), bf16),
            pltpu.VMEM((streams, 2, 2, rows, units), bf16),
            pltpu.VMEM((streams, 2, rows // 2, units), f32),
            pltpu.VMEM((streams, 2, 2, rows // 2, units), bf16),
            pltpu.VMEM((2, units, VOCAB_PAD), bf16),
            pltpu.VMEM((seqs, 2, units // seqs, VOCAB_PAD), bf16),
            pltpu.VMEM((seqs - 1, 2, units // seqs, VOCAB_PAD), bf16),
            dma,
            dma((streams,)),
            dma((streams,)),
            dma((streams,)),
            dma((streams, 4)),
            dma((streams, 2, 4)),
            dma((streams, 2, 2)),
            dma((streams, 2, 2, 2)),
            dma((streams, 2)),
            dma((streams, 2, 2)),
            dma((seqs - 1,)),
            dma((seqs - 1,)),
        ],
        compiler_params=pltpu.CompilerParams(
            collective_id=1, has_side_effects=True, vmem_limit_bytes=VMEM_LIMIT
        ),
        name="backward_visits",
    )(info, slot_ids, w_dec, dec_grad, acts, grads, wholes, w_grouped)
    rec_part, edge_part, small = kernel_sums(
        rec_grad, letter_grad, embed, w_in_grouped, (loss, logit_sq, hidden_sq, dec_bias)
    )
    outs = (
        shape((1, 1), f32),
        shape(h_init.shape, f32),
        shape(h_init.shape, f32),
        shape(embed.shape, f32),
        shape((2, width, columns // seqs), f32),
        shape((2, w_rec.shape[1] // seqs, columns), f32),
        shape((2, columns // seqs), f32),
        shape((2, units // seqs, letters), f32),
        shape((2, letters), f32),
        shape((1, 2), f32),
        shape((1, 2), f32),
        shape((1, 2), f32),
    )
    tile = rec_part.shape[2]
    parts = rec_part.shape[1]
    results = pl.pallas_call(
        functools.partial(finish_kernel, w_rec.shape[1]),
        grid=(2, parts),
        out_shape=outs,
        in_specs=[vmem] * 7 + [pl.BlockSpec((1, 1, tile, columns), lambda d, r: (d, r, 0, 0))],
        out_specs=tuple(
            pl.BlockSpec((1, tile, columns), lambda d, r: (d, r, 0)) if n == 5 else vmem for n in range(len(outs))
        ),
        scratch_shapes=[pltpu.VMEM((4 * LANES, 4 * LANES), bf16)],
        compiler_params=pltpu.CompilerParams(
            dimension_semantics=("arbitrary", "arbitrary"), vmem_limit_bytes=VMEM_LIMIT
        ),
        name="results",
    )(lengths[None], embed, edge_part, dec_part, small, hidden_grad, cell_grad, rec_part)
    scalar = (0, 9, 10, 11)
    return tuple(
        x.reshape(()) if n == 0 else x.reshape(2) if n in scalar else x for n, x in enumerate(results)
    )


def finish_kernel(
    all_units, lens, embed, edge, dec, small, hidden_in, cell_in, rec,
    loss, hidden_grad, cell_grad, embed_grad, in_grad, rec_grad, bias_grad, dec_grad, dec_bias, rms_embed, rms_hidden,
    rms_logits, matrix,
):
    first = (pl.program_id(0) == 0) & (pl.program_id(1) == 0)
    letters, width = embed.shape[1:]
    span = matrix.shape[0]

    @pl.when(first)
    def _():
        matrix[...] = regroup_matrix(span)
        hidden_grad[...] = hidden_in[...]
        cell_grad[...] = cell_in[...]
        live = jnp.sum(lens[...].astype(jnp.float32), axis=1, keepdims=True)
        count = 2.0 * (live - lens.shape[1])
        at = 2 * TABLE
        loss[...] = small[at:at + 1, :1] / count
        for d in range(2):
            embed_grad[d] = small[d * TABLE:d * TABLE + letters, :width]
            in_grad[d] = edge[d, :width]
            bias_grad[d:d + 1] = edge[d, width:width + 1]
            dec_grad[d] = dec[d, :, :letters]
            for n in range(VOCAB_PAD // LANES):
                row = at + 5 + d * (VOCAB_PAD // LANES) + n
                last = min(LANES, letters - n * LANES)
                dec_bias[d:d + 1, n * LANES:n * LANES + last] = small[row:row + 1, :last]
            table = embed[d].astype(jnp.float32)
            square = jnp.sum(jnp.sum(table * table, axis=1, keepdims=True), axis=0, keepdims=True)
            rms_embed[:, d:d + 1] = jnp.sqrt(square / (letters * width))
            logit_sq = jnp.sum(small[at + 1 + d:at + 2 + d], axis=1, keepdims=True)
            hidden_sq = jnp.sum(small[at + 3 + d:at + 4 + d], axis=1, keepdims=True)
            rms_hidden[:, d:d + 1] = jnp.sqrt(hidden_sq / (all_units * live))
            rms_logits[:, d:d + 1] = jnp.sqrt(logit_sq / (letters * count / 2.0))

    for g in range(rec.shape[-1] // span):
        columns = slice(g * span, (g + 1) * span)
        rec_grad[0, :, columns] = matmul(rec[0, 0, :, columns], matrix[...], NT)


PIECE = 128
LAG = 3
WINDOW = 3
TABLE = 280


def spread(letter_grad, other, dims):
    high = letter_grad.astype(jnp.bfloat16)
    low = (letter_grad - high.astype(jnp.float32)).astype(jnp.bfloat16)
    return matmul(high, other, dims) + matmul(low, other, dims)


def reduce_kernel(
    rec_hbm, letter_grad, embed_in, w_in, loss, logit_sq, hidden_sq, dec_bias,
    rec_out, edge_out, small_out,
    own, ahead, behind, edge, edge_in, small, part, small_in, part_in, summed, matrix, embed,
    load_sem, line_send, line_recv, back_send, back_recv, edge_send, edge_recv,
    scatter_send, scatter_recv, seq_send, seq_recv, gather_send, gather_recv,
):
    seq, me = lax.axis_index("seq"), lax.axis_index("mp")
    count, parts = own.shape[1], own.shape[2]
    peers = lax.axis_size("mp")
    share = small.shape[0] // peers
    half = seq // (count // 2)
    place = seq + half * (count - 1 - 2 * seq)
    onward = 1 - 2 * half
    inner = count // 2 - 1
    lag = LAG + (inner - place) * 5
    load = pltpu.make_async_copy(rec_hbm, own, load_sem)
    load.start()

    def other_seq(n):
        return (seq + n) % count

    def other_mp(n):
        return (me + n) % peers

    barrier = pltpu.get_barrier_semaphore()
    for n in range(1, count):
        pl.semaphore_signal(barrier, inc=1, device_id=(other_seq(n), me), device_id_type=MESH)
    for n in range(1, peers):
        pl.semaphore_signal(barrier, inc=1, device_id=(seq, other_mp(n)), device_id_type=MESH)
    pl.semaphore_wait(barrier, count + peers - 2)
    load.wait()

    def send(src, dst, send_sem, recv_sem, seq_to, mp_to):
        return pltpu.make_async_remote_copy(
            src_ref=src, dst_ref=dst, send_sem=send_sem, recv_sem=recv_sem,
            device_id=(seq_to, mp_to), device_id_type=MESH,
        )

    def actual(chunk):
        return chunk + half * (count - 1 - 2 * chunk)

    pieces = 2 * parts

    def slot(k):
        return k // pieces, (k % pieces) // parts, k % parts

    def piece(chunk, d, r):
        return own.at[d, actual(chunk), r]

    def line_copy(k, crossing):
        i, d, r = slot(k)
        target = behind.at[i, d, r] if crossing else ahead.at[i, d, r]
        sem = back_recv.at[i, d, r] if crossing else line_recv.at[i, d, r]
        return send(piece(count - 1 - i, d, r), target, line_send.at[i, d, r], sem, seq + onward, me)

    def back_copy(k):
        i, d, r = slot(k)
        return send(
            piece(i, d, r), behind.at[i, d, r], back_send.at[i, d, r], back_recv.at[i, d, r], seq - onward, me
        )

    def add(chunk, d, r, term):
        ref = piece(chunk, d, r)
        ref[...] = (ref[...].astype(jnp.float32) + term[...].astype(jnp.float32)).astype(jnp.bfloat16)

    def line(k):
        i, d, r = slot(k)

        @pl.when((place > 0) & (i <= count - 1 - place))
        def _():
            line_copy(k, False).wait_recv()
            add(count - 1 - i, d, r, ahead.at[i, d, r])

        @pl.when((place == 0) & (k >= WINDOW))
        def _():
            line_copy(k - WINDOW, False).wait_send()

        @pl.when((i <= count - 2 - place) & (place < inner))
        def _():
            line_copy(k, False).start()

        @pl.when((i <= count - 2 - place) & (place == inner))
        def _():
            line_copy(k, True).start()

    def back(k):
        i, d, r = slot(k)

        @pl.when(i <= place)
        def _():
            back_copy(k).wait_recv()
            add(i, d, r, behind.at[i, d, r])

        @pl.when(i < place)
        def _():
            back_copy(k).start()

    def advance(k, carry):
        @pl.when(k < (count - 1) * pieces)
        def _():
            line(k)

        @pl.when((k >= lag) & (k - lag < (count // 2) * pieces))
        def _():
            back(k - lag)

        return carry

    def edge_copy(n):
        to = other_seq(n)
        return send(edge.at[to], edge_in.at[n - 1], edge_send.at[n - 1], edge_recv.at[n - 1], to, me)

    def scatter_copy(n):
        to = other_mp(n)
        rows = pl.ds(pl.multiple_of(to * share, 8), share)
        return send(small.at[rows], small_in.at[n - 1], scatter_send.at[n - 1], scatter_recv.at[n - 1], seq, to)

    def seq_copy(n):
        return send(part, part_in.at[n - 1], seq_send.at[n - 1], seq_recv.at[n - 1], other_seq(n), me)

    own_rows = pl.ds(pl.multiple_of(me * share, 8), share)

    def gather_copy(n):
        return send(
            summed.at[own_rows], summed.at[own_rows], gather_send.at[n - 1], gather_recv.at[me], seq, other_mp(n)
        )

    def gather_arrival(n):
        source = other_mp(n)
        rows = pl.ds(pl.multiple_of(source * share, 8), share)
        return send(summed.at[rows], summed.at[rows], gather_send.at[n - 1], gather_recv.at[source], seq, source)

    start = 6
    lax.fori_loop(0, 2, advance, 0)
    matrix[...] = regroup_matrix(matrix.shape[0])
    letters, width = embed_in.shape[1:]
    lanes = lax.broadcasted_iota(jnp.int32, (letters, LANES), 1)
    padded(embed, embed_in)
    for d in range(2):
        embed[d, :letters] = jnp.where(lanes == width, 1.0, embed[d, :letters].astype(jnp.float32)).astype(jnp.bfloat16)
    first = jnp.where(me == 0, 1.0, 0.0)
    for d in range(2):
        small[d * TABLE:(d + 1) * TABLE] = spread(letter_grad[d], w_in[d], NT)[:TABLE]
    small[2 * TABLE:] = jnp.zeros((small.shape[0] - 2 * TABLE, LANES), jnp.float32)
    at = 2 * TABLE
    small[at:at + 1] = jnp.sum(loss[0] + loss[1], axis=0, keepdims=True) * first
    for d in range(2):
        small[at + 1 + d:at + 2 + d] = jnp.sum(logit_sq[d], axis=0, keepdims=True) * first
        small[at + 3 + d:at + 4 + d] = jnp.sum(hidden_sq[d], axis=0, keepdims=True)
        row = jnp.sum(dec_bias[d], axis=0, keepdims=True) * first
        for n in range(VOCAB_PAD // LANES):
            line_at = at + 5 + d * (VOCAB_PAD // LANES) + n
            small[line_at:line_at + 1] = row[:, n * LANES:(n + 1) * LANES]
    for n in range(1, peers):
        scatter_copy(n).start()
    rows = edge.shape[2]
    span = matrix.shape[0]
    wide = own.shape[-1] // count
    for d in range(2):
        full = spread_left(embed[d], letter_grad[d]).astype(jnp.bfloat16)
        flat = [
            matmul(full[:, g * span:(g + 1) * span], matrix[...], NT).astype(jnp.bfloat16)
            for g in range(own.shape[-1] // span)
        ]
        for q in range(count):
            group, offset = (q * wide) // span, (q * wide) % span
            edge[q, d] = flat[group][:rows, offset:offset + wide]
    for n in range(1, count):
        edge_copy(n).start()
    lax.fori_loop(2, start, advance, 0)
    for n in range(1, peers):
        scatter_copy(n).wait()
    total = small[own_rows, :]
    for n in range(1, peers):
        total += small_in[n - 1]
    part[...] = total
    for n in range(1, count):
        seq_copy(n).start()
    lax.fori_loop(start, 2 * start, advance, 0)
    for n in range(1, count):
        seq_copy(n).wait()
        total += part_in[n - 1]
    summed[own_rows, :] = total
    for n in range(1, peers):
        gather_copy(n).start()
    lax.fori_loop(2 * start, (count - 1) * pieces + LAG, advance, 0)
    for n in range(1, peers):
        gather_copy(n).wait_send()
        gather_arrival(n).wait_recv()
    small_out[...] = summed[...]
    for n in range(1, count):
        edge_copy(n).wait()
    for d in range(2):
        edge_out[d] = edge[seq, d].astype(jnp.float32) + sum(
            edge_in[n, d].astype(jnp.float32) for n in range(count - 1)
        )
        rec_out[d] = own[d, seq]

    def finish(k, carry):
        i, d, r = slot(k)

        @pl.when((i <= count - 2 - place) & ((place > 0) | (k >= (count - 1) * pieces - WINDOW)))
        def _():
            line_copy(k, False).wait_send()

        @pl.when((i < place) & (k < (count // 2) * pieces))
        def _():
            back_copy(k).wait_send()

        return carry

    lax.fori_loop(0, (count - 1) * pieces, finish, 0)


def spread_left(other, letter_grad):
    high = letter_grad.astype(jnp.bfloat16)
    low = (letter_grad - high.astype(jnp.float32)).astype(jnp.bfloat16)
    return matmul(other, high, TN) + matmul(other, low, TN)


def kernel_sums(rec_grad, letter_grad, embed, w_in_grouped, stats):
    count = lax.axis_size("seq")
    peers = lax.axis_size("mp")
    columns = rec_grad.shape[-1]
    all_rows = rec_grad.shape[1] * rec_grad.shape[2]
    parts = all_rows // count // PIECE
    width = embed.shape[2]
    edge_rows = -(-(width + 1) // 8) * 8
    small_rows = -(-(2 * TABLE + 16) // (8 * peers)) * 8 * peers
    share = small_rows // peers
    f32, bf16 = jnp.float32, jnp.bfloat16
    dma = pltpu.SemaphoreType.DMA
    shape = jax.ShapeDtypeStruct
    vmem = pl.BlockSpec(memory_space=pltpu.VMEM)
    return pl.pallas_call(
        reduce_kernel,
        out_shape=(
            shape((2, parts, PIECE, columns), bf16),
            shape((2, edge_rows, columns // count), f32),
            shape((small_rows, LANES), f32),
        ),
        in_specs=[pl.BlockSpec(memory_space=pl.ANY)] + [vmem] * 7,
        out_specs=(vmem,) * 3,
        scratch_shapes=[
            pltpu.VMEM((2, count, parts, PIECE, columns), bf16),
            pltpu.VMEM((count - 1, 2, parts, PIECE, columns), bf16),
            pltpu.VMEM((count // 2, 2, parts, PIECE, columns), bf16),
            pltpu.VMEM((count, 2, edge_rows, columns // count), bf16),
            pltpu.VMEM((count - 1, 2, edge_rows, columns // count), bf16),
            pltpu.VMEM((small_rows, LANES), f32),
            pltpu.VMEM((share, LANES), f32),
            pltpu.VMEM((peers - 1, share, LANES), f32),
            pltpu.VMEM((count - 1, share, LANES), f32),
            pltpu.VMEM((small_rows, LANES), f32),
            pltpu.VMEM((4 * LANES, 4 * LANES), bf16),
            pltpu.VMEM((2, VOCAB_PAD, LANES), bf16),
            dma,
            dma((count - 1, 2, parts)),
            dma((count - 1, 2, parts)),
            dma((count // 2, 2, parts)),
            dma((count // 2, 2, parts)),
            dma((count - 1,)),
            dma((count - 1,)),
            dma((peers - 1,)),
            dma((peers - 1,)),
            dma((count - 1,)),
            dma((count - 1,)),
            dma((peers - 1,)),
            dma((peers,)),
        ],
        compiler_params=pltpu.CompilerParams(
            collective_id=2, has_side_effects=True, vmem_limit_bytes=VMEM_LIMIT
        ),
        name="gradient_sums",
    )(
        rec_grad.reshape(2, count, parts, PIECE, columns), letter_grad, embed, w_in_grouped, *stats,
    )


def plain_step(ids, lengths, order, count, h_init, c_init, embed, w_in, w_rec, bias, w_dec, b_dec, matrix):
    first_mp = (lax.axis_index("mp") == 0).astype(jnp.float32)
    per_dev, own_units = h_init.shape[1:]
    lanes = matrix.shape[0] // 4
    wd_full = lax.all_gather(w_dec, "mp", axis=1, tiled=True)
    whole_ids = lax.all_gather(ids, "seq", axis=0, tiled=True)
    own_order = lax.dynamic_slice_in_dim(order, lax.axis_index("seq") * per_dev, per_dev)
    slot_ids = jnp.take(whole_ids, own_order, axis=1)
    own_len = jnp.take(lengths, own_order)
    step_ids = jnp.stack([slot_ids, jnp.flip(slot_ids, 0)])
    w_rec_grouped = grouped(w_rec, matrix)
    w_in_grouped = grouped(w_in, matrix)
    bias_grouped = jnp.swapaxes(
        bias.reshape(2, own_units // lanes, lanes, 4), -1, -2
    ).reshape(bias.shape)
    loss, hidden_sq, logit_sq, dec_bias, dec_grad, hidden_grad, cell_grad, rec_grad, letter_grad = recurrences(
        step_ids, own_len, h_init, c_init, embed, w_in_grouped, w_rec_grouped, bias_grouped, w_dec, wd_full,
        b_dec, count, lanes,
    )
    embed_wide = embed.astype(jnp.float32)
    in_grad = jnp.einsum("dve,dvc->dec", embed_wide, letter_grad, precision=lax.Precision.HIGHEST)
    bias_grad = jnp.sum(letter_grad, axis=1, keepdims=True)
    embed_part = jnp.einsum(
        "dvc,dec->dve", letter_grad, w_in_grouped.astype(jnp.float32), precision=lax.Precision.HIGHEST
    )
    edge = ungrouped_wide(jnp.concatenate([in_grad, bias_grad], axis=1), lanes)
    rec_part = lax.psum_scatter(rec_grad.astype(jnp.bfloat16), "seq", scatter_dimension=1, tiled=True)
    edge_part = lax.psum_scatter(edge.astype(jnp.bfloat16), "seq", scatter_dimension=2, tiled=True)
    dec_part = lax.psum_scatter(dec_grad.astype(jnp.bfloat16), "seq", scatter_dimension=1, tiled=True)
    loss_sum, hidden_all, logit_all, dec_bias_grad, embed_grad = lax.psum(
        (loss * first_mp, hidden_sq, logit_sq * first_mp, dec_bias * first_mp, embed_part), ("seq", "mp")
    )
    rec_out = ungrouped(rec_part, matrix).astype(jnp.float32)
    return (
        loss_sum, hidden_all, logit_all, dec_bias_grad, dec_part.astype(jnp.float32), hidden_grad, cell_grad, rec_out,
        edge_part[:, :-1].astype(jnp.float32), edge_part[:, -1].astype(jnp.float32), embed_grad,
    )


def per_device(ids, lengths, order, h_init, c_init, embed, w_in, w_rec, bias, w_dec, b_dec):
    streams = ids.shape[1]
    per_dev, own_units = h_init.shape[1:]
    all_units, letter_count = w_rec.shape[1], embed.shape[1]
    fits = own_units % LANES == 0 and per_dev % LANES == 0 and per_dev <= 256 and own_units <= 256
    fits = fits and all_units % (lax.axis_size("seq") * PIECE) == 0 and letter_count <= TABLE
    if lax.axis_size("mp") == 8 and lax.axis_size("seq") == 4 and fits and embed.shape[2] < LANES:
        return kernel_step(ids, lengths, order, h_init, c_init, embed, w_in, w_rec, bias, w_dec, b_dec)
    live_total = jnp.sum(lengths).astype(jnp.float32)
    count = 2.0 * (jnp.sum(lengths) - streams).astype(jnp.float32)
    _, matrix = column_order(own_units)
    (
        loss_sum, hidden_all, logit_all, dec_bias_grad, dec_part, hidden_grad, cell_grad, rec_out, in_out, bias_out,
        embed_grad,
    ) = plain_step(ids, lengths, order, count, h_init, c_init, embed, w_in, w_rec, bias, w_dec, b_dec, matrix)
    embed_wide = embed.astype(jnp.float32)
    rms_embed = jnp.sqrt(jnp.mean(embed_wide * embed_wide, axis=(1, 2)))
    return (
        loss_sum / count,
        hidden_grad,
        cell_grad,
        embed_grad,
        in_out,
        rec_out,
        bias_out,
        dec_part,
        dec_bias_grad,
        rms_embed,
        jnp.sqrt(hidden_all / (all_units * live_total)),
        jnp.sqrt(logit_all / (letter_count * count / 2.0)),
    )


def solution(mesh):
    in_specs = (
        P("seq", None),
        P(),
        P(),
        P(None, "seq", "mp"),
        P(None, "seq", "mp"),
        P(),
        P(None, None, "mp"),
        P(None, None, "mp"),
        P(None, "mp"),
        P(None, "mp", None),
        P(),
    )
    out_specs = (
        P(),
        P(None, "seq", "mp"),
        P(None, "seq", "mp"),
        P(),
        P(None, None, ("mp", "seq")),
        P(None, "seq", "mp"),
        P(None, ("mp", "seq")),
        P(None, ("mp", "seq"), None),
        P(),
        P(),
        P(),
        P(),
    )
    return jax.shard_map(
        per_device, mesh=mesh, in_specs=in_specs, out_specs=out_specs, check_vma=False
    )
```

```python
import functools

import jax
import jax.numpy as jnp
from jax import lax
from jax.experimental import pallas as pl
from jax.experimental.pallas import tpu as pltpu
from jax.sharding import PartitionSpec as P

VMEM_LIMIT = 58 * 2**20


def column_order(own_units):
    lanes = min(128, own_units)
    source = jnp.arange(4 * lanes, dtype=jnp.int32)
    place = (source % 4) * lanes + source // 4
    matrix = (place[:, None] == jnp.arange(4 * lanes, dtype=jnp.int32)[None, :]).astype(jnp.bfloat16)
    return lanes, matrix


def grouped(x, matrix):
    width = matrix.shape[0]
    parts = x.reshape(x.shape[:-1] + (x.shape[-1] // width, width))
    out = jnp.einsum("...gc,cp->...gp", parts, matrix, preferred_element_type=jnp.float32)
    return out.astype(x.dtype).reshape(x.shape)


def ungrouped(x, matrix):
    return grouped(x, matrix.T)


def ungrouped_wide(x, lanes):
    parts = x.reshape(x.shape[:-1] + (x.shape[-1] // (4 * lanes), 4, lanes))
    return jnp.swapaxes(parts, -1, -2).reshape(x.shape)


def gates_of(pre, lanes):
    parts = pre.reshape(pre.shape[:-1] + (pre.shape[-1] // (4 * lanes), 4, lanes))
    flat = pre.shape[:-1] + (pre.shape[-1] // 4,)
    return tuple(parts[..., k, :].reshape(flat) for k in range(4))


def joined_gates(gates, lanes):
    split = [g.reshape(g.shape[:-1] + (g.shape[-1] // lanes, 1, lanes)) for g in gates]
    joined = jnp.concatenate(split, axis=-2)
    return joined.reshape(gates[0].shape[:-1] + (4 * gates[0].shape[-1],))


def recurrences(step_ids, own_len, h_init, c_init, embed, w_in, w_rec, bias, w_dec, wd_full, b_dec, count, lanes):
    length, per_dev = step_ids.shape[1:]
    letter_count = embed.shape[1]
    steps = jnp.arange(length, dtype=jnp.int32)
    live_steps = jnp.stack(
        [steps[:, None] < own_len[None, :], (length - 1 - steps)[:, None] < own_len[None, :]], axis=1
    )[..., None]
    letters = jnp.arange(letter_count, dtype=jnp.int32)
    onehot = (jnp.swapaxes(step_ids, 0, 1)[..., None] == letters).astype(jnp.bfloat16)
    letter_rows = jnp.einsum(
        "sdbv,dve->sdbe", onehot, embed, preferred_element_type=jnp.float32
    ).astype(jnp.bfloat16)
    gates_in = jnp.einsum(
        "sdbe,dec->sdbc", letter_rows, w_in, preferred_element_type=jnp.float32
    ).astype(jnp.bfloat16)

    def forward_step(carry, inputs):
        hidden, cell = carry
        gate_in, live = inputs
        whole = lax.all_gather(hidden, "mp", axis=2, tiled=True)
        recurrent = jnp.einsum("dbh,dhc->dbc", whole, w_rec, preferred_element_type=jnp.float32)
        pre = gate_in.astype(jnp.float32) + recurrent + bias[:, None]
        in_pre, forget_pre, cell_pre, out_pre = gates_of(pre, lanes)
        in_gate, forget, out_gate = (jax.nn.sigmoid(x) for x in (in_pre, forget_pre, out_pre))
        cell_gate = jnp.tanh(cell_pre)
        new_cell = forget * cell + in_gate * cell_gate
        cell_next = jnp.where(live, new_cell, cell)
        hidden_next = jnp.where(
            live, out_gate * jnp.tanh(new_cell), hidden.astype(jnp.float32)
        ).astype(jnp.bfloat16)
        return ((hidden_next, cell_next), (whole, cell, in_gate, forget, cell_gate, out_gate))

    (last_hidden, last_cell), (wholes, cells, *gates) = lax.scan(
        forward_step, (h_init, c_init), (gates_in, live_steps)
    )
    last_whole = lax.all_gather(last_hidden, "mp", axis=2, tiled=True)
    after = jnp.concatenate([wholes[1:], last_whole[None]], axis=0)
    own = h_init.shape[2]
    mine = lax.dynamic_slice_in_dim(after, lax.axis_index("mp") * own, own, axis=3)
    mine_wide = mine.astype(jnp.float32)
    hidden_sq = jnp.sum(jnp.where(live_steps, mine_wide * mine_wide, 0.0), axis=(0, 2, 3))
    logits = (
        jnp.einsum("sdbh,dhv->sdbv", after, wd_full, preferred_element_type=jnp.float32) + b_dec[None, :, None]
    )
    targets = jnp.swapaxes(jnp.concatenate([step_ids[:, 1:], step_ids[:, :1]], axis=1), 0, 1)
    fore_valid = (steps[:, None] + 1 < own_len[None, :])
    back_valid = (steps[:, None] < length - 1) & ((length - 1 - steps)[:, None] < own_len[None, :])
    valid = jnp.stack([fore_valid, back_valid], axis=1).astype(jnp.float32)
    logit_sq = jnp.sum(valid[..., None] * logits * logits, axis=(0, 2, 3))
    top = jnp.max(logits, axis=-1, keepdims=True)
    log_total = top + jnp.log(jnp.sum(jnp.exp(logits - top), axis=-1, keepdims=True))
    target_hot = targets[..., None] == letters
    picked = jnp.sum(jnp.where(target_hot, logits, 0.0), axis=-1)
    loss = jnp.sum(valid * (log_total[..., 0] - picked))
    grad_logits = (
        valid[..., None] * (jnp.exp(logits - log_total) - target_hot.astype(jnp.float32)) / count
    ).astype(jnp.bfloat16)
    dec_bias = jnp.sum(grad_logits.astype(jnp.float32), axis=(0, 2))
    dec_grad = jnp.einsum("sdbh,sdbv->dhv", mine, grad_logits, preferred_element_type=jnp.float32)

    def backward_step(carry, inputs):
        grad_hidden, grad_cell = carry
        live, cell, in_gate, forget, cell_gate, out_gate, grad_logit = inputs
        grad_hidden = grad_hidden + jnp.einsum(
            "dbv,dhv->dbh", grad_logit, w_dec, preferred_element_type=jnp.float32
        )
        squash = jnp.tanh(forget * cell + in_gate * cell_gate)
        grad_new = jnp.where(live, grad_cell + grad_hidden * out_gate * (1.0 - squash * squash), 0.0)
        grad_out = jnp.where(live, grad_hidden * squash, 0.0)
        grad_pre = joined_gates(
            [
                grad_new * cell_gate * in_gate * (1.0 - in_gate),
                grad_new * cell * forget * (1.0 - forget),
                grad_new * in_gate * (1.0 - cell_gate * cell_gate),
                grad_out * out_gate * (1.0 - out_gate),
            ],
            lanes,
        ).astype(jnp.bfloat16)
        grad_cell_prev = grad_new * forget + jnp.where(live, 0.0, grad_cell)
        held = jnp.where(live, 0.0, grad_hidden)
        terms = jnp.einsum("dbc,dhc->dbh", grad_pre, w_rec, preferred_element_type=jnp.float32)
        through = lax.psum_scatter(
            terms.astype(jnp.bfloat16), "mp", scatter_dimension=2, tiled=True
        ).astype(jnp.float32)
        return ((held + through, grad_cell_prev), grad_pre)

    start = jnp.zeros(c_init.shape, jnp.float32)
    (hidden_grad, cell_grad), grad_pres = lax.scan(
        backward_step, (start, start), (live_steps, cells, *gates, grad_logits), reverse=True
    )
    rec_grad = jnp.einsum("sdbh,sdbc->dhc", wholes, grad_pres, preferred_element_type=jnp.float32)
    letter_grad = jnp.einsum("sdbv,sdbc->dvc", onehot, grad_pres, preferred_element_type=jnp.float32)
    return loss, hidden_sq, logit_sq, dec_bias, dec_grad, hidden_grad, cell_grad, rec_grad, letter_grad


MESH = pl.DeviceIdType.MESH
LANES = 128
VOCAB_PAD = 384
NT = (((1,), (1,)), ((), ()))
TN = (((0,), (0,)), ((), ()))


def sigmoid(x):
    return 0.5 * jnp.tanh(0.5 * x) + 0.5


def matmul(left, right, dims=(((1,), (0,)), ((), ()))):
    return lax.dot_general(left, right, dims, preferred_element_type=jnp.float32)


def neighbours():
    me = lax.axis_index("mp")
    row, column, core = me // 4, (me // 2) % 2, me % 2
    sibling = row * 4 + column * 2 + (1 - core)
    across = (1 - row) * 4 + (1 - column) * 2 + core
    side = row * 4 + (1 - column) * 2 + core
    up = (1 - row) * 4 + column * 2 + core
    return me, sibling, (across, side, up)


def greet(peers, seqs=0):
    seq, me = lax.axis_index("seq"), lax.axis_index("mp")
    barrier = pltpu.get_barrier_semaphore()
    for peer in peers:
        pl.semaphore_signal(barrier, inc=1, device_id=(seq, peer), device_id_type=MESH)
    for n in range(1, seqs):
        pl.semaphore_signal(barrier, inc=1, device_id=((seq + n) % seqs, me), device_id_type=MESH)
    pl.semaphore_wait(barrier, len(peers) + max(seqs - 1, 0))


def remote(src, dst, send, recv, peer):
    return pltpu.make_async_remote_copy(
        src_ref=src, dst_ref=dst, send_sem=send, recv_sem=recv,
        device_id=(lax.axis_index("seq"), peer), device_id_type=MESH,
    )


def other_core(peer):
    return (peer // 2) * 2 + (1 - peer % 2)


def folded(x):
    return jnp.sum(x.reshape(x.shape[0] // 8, 8, x.shape[1]), axis=0)


def regroup_matrix(span):
    source = lax.broadcasted_iota(jnp.int32, (span, span), 0)
    place = (source & 3) * (span // 4) + (source >> 2)
    return (place == lax.broadcasted_iota(jnp.int32, (span, span), 1)).astype(jnp.bfloat16)


def padded(ref, value):
    ref[...] = jnp.zeros(ref.shape, ref.dtype)
    for d in range(2):
        ref[d, :value.shape[1], :value.shape[2]] = value[d]


def column_of(table, lane):
    lanes = lax.broadcasted_iota(jnp.int32, table.shape, 1)
    return jnp.sum(jnp.where(lanes == lane, table, 0.0), axis=1, keepdims=True)


def time_of(direction, step, length):
    return step if direction == 0 else length - 1 - step


def forward_kernel(
    length, letters, ids_in, lens, order, h_in, c_in, embed_in, w_in_raw, bias, b_dec_in, w_dec_in, w_hbm,
    wholes, acts, grads, w_out, loss, logit_sq, hidden_sq, dec_bias, dec_grad, info, ids, w_in,
    w, wd, buf, cell, acc, logit, stage, grad, all_ids, table, matrix, embed, b_dec, inverse, load_sem, ids_send, ids_recv, wd_send, wd_recv,
    send_sem, recv_sem, save_sem, act_sem, grad_sem,
):
    me, sibling, peers = neighbours()
    seq, seqs, times = lax.axis_index("seq"), all_ids.shape[0], ids_in.shape[0]
    blocks, rows, units = buf.shape[2:]
    groups, span = units // LANES, matrix.shape[0]
    columns = w.shape[-1]
    load_w = pltpu.make_async_copy(w_hbm, w, load_sem.at[0])
    store_w = pltpu.make_async_copy(w, w_out, load_sem.at[1])
    load_w.start()
    all_ids[seq, :times] = ids_in[...].astype(jnp.float32)
    matrix[...] = regroup_matrix(span)
    for s in range(2):
        buf[s, 0, me] = h_in[s]
    greet((sibling,) + peers, seqs)

    def ids_copy(n):
        to = (seq + n) % seqs
        block = all_ids.at[seq]
        return pltpu.make_async_remote_copy(
            src_ref=block, dst_ref=block, send_sem=ids_send.at[n - 1], recv_sem=ids_recv.at[seq],
            device_id=(to, me), device_id_type=MESH,
        )

    def ids_arrival(n):
        source = (seq + n) % seqs
        block = all_ids.at[source]
        return pltpu.make_async_remote_copy(
            src_ref=block, dst_ref=block, send_sem=ids_send.at[n - 1], recv_sem=ids_recv.at[source],
            device_id=(source, me), device_id_type=MESH,
        )

    across, side, up = peers
    depth = rows // 2

    def transfer(s, step, block, h, index, peer):
        slot, par = step % 3, step % 2
        ref = buf.at[s, slot, block, h * depth:(h + 1) * depth]
        return remote(ref, ref, send_sem.at[s, par, index], recv_sem.at[s, slot, block, h], peer)

    def transfer_whole(s, step, block, index):
        slot, par = step % 3, step % 2
        ref = buf.at[s, slot, block]
        return remote(ref, ref, send_sem.at[s, par, index], recv_sem.at[s, slot, block, 0], sibling)

    def direct(s, step):
        plan = ((0, side), (1, up), (1, side), (0, up))
        return [transfer(s, step, me, h, n, peer) for n, (h, peer) in enumerate(plan)]

    def pass_on(s, step):
        for n, (block, h, peer) in enumerate(((side, 0, up), (up, 1, side))):
            transfer(s, step, block, h, 0, sibling).wait_recv()
            transfer(s, step, block, h, 4 + n, peer).start()

    def core_copies(s, step):
        return [transfer_whole(s, step, block, 6 + n) for n, block in enumerate((me, side, up, across))]

    def wd_copy(n):
        peer = (peers + (sibling,))[n]
        return remote(wd.at[me], wd.at[me], wd_send.at[n], wd_recv.at[me], peer)

    def wd_relay(n):
        block = wd.at[peers[n]]
        return remote(block, block, wd_send.at[4 + n], wd_recv.at[peers[n]], sibling)

    def wd_arrival(source):
        return remote(wd.at[source], wd.at[source], wd_send.at[0], wd_recv.at[source], sibling)

    def save(s, step):
        return pltpu.make_async_copy(buf.at[s, step % 3], wholes.at[step, s], save_sem.at[s, step % 2])

    def save_acts(s, step):
        return pltpu.make_async_copy(stage.at[s], acts.at[step, s], act_sem.at[s])

    def save_grad(s, step):
        return pltpu.make_async_copy(grad.at[s], grads.at[step, s], grad_sem.at[s])

    def finish_sends(s, step):
        for copy in direct(s, step) + core_copies(s, step):
            copy.wait_send()
        for n, (block, h, peer) in enumerate(((side, 0, up), (up, 1, side))):
            transfer(s, step, block, h, 4 + n, peer).wait_send()

    for n in range(1, seqs):
        ids_copy(n).start()
    for s in range(2):
        for copy in direct(s, 0):
            copy.start()
        transfer_whole(s, 0, me, 6).start()
    padded(wd.at[me], w_dec_in)
    for n in range(4):
        wd_copy(n).start()
    padded(embed, embed_in)
    padded(w_in, w_in_raw)
    b_dec[...] = jnp.full(b_dec.shape, -1e30, jnp.float32)
    for d in range(2):
        b_dec[d, :, :letters] = b_dec_in[d:d + 1]
    lengths = lens[...].astype(jnp.float32)
    inverse[...] = 0.5 / (jnp.sum(lengths, axis=1, keepdims=True) - lens.shape[1])
    for ref in (loss, logit_sq, hidden_sq, dec_bias, dec_grad):
        ref[...] = jnp.zeros(ref.shape, ref.dtype)
    cell[...] = c_in[...]
    for d in range(2):
        for g in range(columns // span):
            part = slice(g * span, (g + 1) * span)
            w_in[d, :, part] = matmul(w_in[d, :, part], matrix[...]).astype(jnp.bfloat16)
    load_w.wait()

    def regroup(b, carry):
        for d in range(2):
            for g in range(columns // span):
                part = slice(g * span, (g + 1) * span)
                w[d, b, :, part] = matmul(w[d, b, :, part], matrix[...]).astype(jnp.bfloat16)
        return carry

    for b in range(blocks):
        regroup(b, 0)
    store_w.start()
    for n in range(1, seqs):
        ids_arrival(n).wait_recv()
    streams = rows
    order_row = order[:, pl.ds(pl.multiple_of(seq * rows, LANES), rows)]
    square = (rows, rows)
    diagonal = lax.broadcasted_iota(jnp.int32, square, 0) == lax.broadcasted_iota(jnp.int32, square, 1)
    order_column = jnp.sum(
        jnp.where(diagonal, jnp.broadcast_to(order_row.astype(jnp.float32), square), 0.0), axis=1, keepdims=True
    ).astype(jnp.int32)
    total_streams = lens.shape[1]
    pick_column = (
        lax.broadcasted_iota(jnp.int32, (streams, total_streams), 1) == order_column
    ).astype(jnp.bfloat16)
    pick_row = (
        lax.broadcasted_iota(jnp.int32, (total_streams, streams), 0) == order_row
    ).astype(jnp.bfloat16)
    table[...] = jnp.zeros(table.shape, table.dtype)
    for d in range(2):
        for t in range(length):
            row = t if d == 0 else length - 1 - t
            table[t:t + 1] = all_ids[row // times, row % times:row % times + 1]
        table[LANES - 1:] = lengths
        high = jnp.floor(table[...] * (1.0 / 16.0))
        low = (table[...] - 16.0 * high).astype(jnp.bfloat16)
        high = high.astype(jnp.bfloat16)
        values = 16.0 * matmul(pick_column, high, NT) + matmul(pick_column, low, NT)
        info[d] = values
        values = 16.0 * matmul(high[:length], pick_row) + matmul(low[:length], pick_row)
        ids[d] = values

    def gates(s, step):
        slot, later = step % 3, (step + 1) % 3
        d = s
        when = time_of(d, step, length)
        live = info[s, :, LANES - 1:] > when.astype(jnp.float32)
        for g in range(groups):
            lanes = slice(g * LANES, (g + 1) * LANES)
            pre = [acc[:, (4 * g + k) * LANES:(4 * g + k + 1) * LANES] for k in range(4)]
            in_gate, forget, out_gate = sigmoid(pre[0]), sigmoid(pre[1]), sigmoid(pre[3])
            cell_gate = jnp.tanh(pre[2])
            old = cell[s, :, lanes]
            new = forget * old + in_gate * cell_gate
            for k, value in enumerate((in_gate, forget, cell_gate, out_gate, old)):
                stage[s, k, :, lanes] = value
            cell[s, :, lanes] = jnp.where(live, new, old)
            before = buf[s, slot, me, :, lanes].astype(jnp.float32)
            hidden = jnp.where(live, out_gate * jnp.tanh(new), before).astype(jnp.bfloat16)
            buf[s, later, me, :, lanes] = hidden
            wide = hidden.astype(jnp.float32)
            hidden_sq[d] += folded(jnp.where(live, wide * wide, 0.0))

    def decode(s, step):
        slot = step % 3
        d = s
        total = jnp.broadcast_to(b_dec[d], logit.shape)
        for b in range(blocks):
            total += matmul(buf[s, slot, b], wd[b, d])
        logit[...] = total
        when = time_of(d, step - 1, length)
        reach = when + 1 if d == 0 else when
        lookup = info[s]
        valid = (lookup[:, LANES - 1:] > reach.astype(jnp.float32)) & (step < length)
        target = column_of(lookup, step)
        value = logit[...]
        lanes = lax.broadcasted_iota(jnp.int32, value.shape, 1)
        hot = lanes.astype(jnp.float32) == target
        top = jnp.max(value, axis=1, keepdims=True)
        power = jnp.exp(value - top)
        total = jnp.sum(power, axis=1, keepdims=True)
        picked = jnp.sum(jnp.where(hot, value, 0.0), axis=1, keepdims=True)
        loss[d] += folded(jnp.broadcast_to(jnp.where(valid, top + jnp.log(total) - picked, 0.0), (rows, LANES)))
        kept = jnp.where(valid & (lanes < letters), value, 0.0)
        square = kept * kept
        logit_sq[d] += folded(sum(square[:, n * LANES:(n + 1) * LANES] for n in range(VOCAB_PAD // LANES)))
        slope = jnp.where(
            valid, (power * (1.0 / total) - jnp.where(hot, 1.0, 0.0)) * inverse[...], 0.0
        ).astype(jnp.bfloat16)
        grad[s] = slope
        dec_bias[d] += folded(slope.astype(jnp.float32))
        dec_grad[d] += matmul(buf[s, slot, me], grad[s], TN)

    others = tuple(other_core(peer) for peer in peers)

    def half(step, s):
        d = s

        @pl.when(step < length)
        def _():
            now = column_of(info[s], step)
            hot = (lax.broadcasted_iota(jnp.int32, (rows, VOCAB_PAD), 1).astype(jnp.float32) == now)
            row = matmul(hot.astype(jnp.bfloat16), embed[d]).astype(jnp.bfloat16)
            acc[...] = matmul(row, w_in[d]).astype(jnp.bfloat16).astype(jnp.float32) + bias[d]

        for n, (block, halves) in enumerate(((side, (1,)), (up, (0,)), (across, (0, 1)))):
            for h in halves:
                transfer(s, step, block, h, 0, sibling).wait_recv()
            transfer_whole(s, step, block, 7 + n).start()

        if s == 0:
            @pl.when(step == 1)
            def _():
                for n, peer in enumerate(peers):
                    wd_arrival(peer).wait_recv()
                    wd_relay(n).start()

        slot = step % 3

        def advance(block):
            acc[...] += matmul(buf[s, slot, block], w[d, block])

        @pl.when(step < length)
        def _():
            for block in (me,) + peers:
                advance(block)

        if s == 0:
            pass_on(1, step)
        else:
            @pl.when(step < length)
            def _():
                pass_on(0, step + 1)

        for block in (sibling,) + others:
            transfer_whole(s, step, block, 6).wait_recv()

        @pl.when(step < length)
        def _():
            for block in (sibling,) + others:
                advance(block)

        @pl.when(step < length)
        def _():

            @pl.when(step > 0)
            def _():
                save_acts(s, step - 1).wait()

            gates(s, step)

            @pl.when(step > 0)
            def _():
                save(s, step - 1).wait()
                finish_sends(s, step - 1)

            for copy in direct(s, step + 1):
                copy.start()
            transfer_whole(s, step + 1, me, 6).start()
            save_acts(s, step).start()
            save(s, step).start()

        if s == 0:
            @pl.when(step == 1)
            def _():
                for block in (sibling,) + others:
                    wd_arrival(block).wait_recv()

        @pl.when(step > 0)
        def _():
            @pl.when(step > 1)
            def _():
                save_grad(s, step - 2).wait()

            decode(s, step)
            save_grad(s, step - 1).start()

    def every(step, carry):
        for s in range(2):
            half(step, s)
        return carry

    pass_on(0, 0)
    lax.fori_loop(0, length + 1, every, 0)
    store_w.wait()
    for n in range(1, seqs):
        ids_copy(n).wait_send()
    for n in range(4):
        wd_copy(n).wait_send()
    for n in range(3):
        wd_relay(n).wait_send()
    for s in range(2):
        save(s, length - 1).wait()
        save_acts(s, length - 1).wait()
        save_grad(s, length - 1).wait()
        finish_sends(s, length - 1)
        finish_sends(s, length)


def backward_kernel(
    length, info, ids, w_dec_in, dec_grad, acts, grads, wholes, w_hbm,
    rec_out, letter_grad, hidden_grad, cell_grad, dec_out,
    w, rec, stage, grad, whole, pre, held, own, sent, got, passed, taken, kept, middle, w_dec, dec, dec_in, load_sem, act_sem,
    grad_sem, whole_sem, core_send, core_recv, chip_send, chip_recv, middle_send, middle_recv, dec_send, dec_recv, store_sem,
):
    me, sibling, peers = neighbours()
    rows, units = held.shape[1:]
    groups = units // LANES
    load_w = pltpu.make_async_copy(w_hbm, w, load_sem)
    load_w.start()

    def load_acts(s, step):
        return pltpu.make_async_copy(acts.at[step, s], stage.at[s], act_sem.at[s])

    def load_grad(s, step):
        return pltpu.make_async_copy(grads.at[step, s], grad.at[s], grad_sem.at[s])

    def load_whole(s, step):
        return pltpu.make_async_copy(wholes.at[step, s], whole.at[s], whole_sem.at[s])

    for s in range(2):
        load_acts(s, length - 1).start()
        load_grad(s, length - 1).start()
        load_whole(s, length - 1).start()
    seq, seqs, tall = lax.axis_index("seq"), dec.shape[0], dec.shape[2]
    for q in range(seqs):
        for d in range(2):
            dec[q, d] = dec_grad[d, q * tall:(q + 1) * tall].astype(jnp.bfloat16)
    greet((sibling,) + peers, seqs)

    def dec_copy(n):
        to = (seq + n) % seqs
        return pltpu.make_async_remote_copy(
            src_ref=dec.at[to], dst_ref=dec_in.at[n - 1], send_sem=dec_send.at[n - 1], recv_sem=dec_recv.at[n - 1],
            device_id=(to, me), device_id_type=MESH,
        )

    for n in range(1, seqs):
        dec_copy(n).start()
    padded(w_dec, w_dec_in)
    held[...] = jnp.zeros(held.shape, held.dtype)
    own[...] = jnp.zeros(own.shape, own.dtype)
    cell_grad[...] = jnp.zeros(cell_grad.shape, cell_grad.dtype)
    letter_grad[...] = jnp.zeros(letter_grad.shape, letter_grad.dtype)

    def clear(b, carry):
        for d in range(2):
            rec[d, b] = jnp.zeros(rec.shape[2:], rec.dtype)
        return carry

    lax.fori_loop(0, w.shape[1], clear, 0)
    load_w.wait()

    def to_core(s, turn, n):
        return remote(
            sent.at[s, n], got.at[s, turn % 2, n], core_send.at[s, n], core_recv.at[s, turn % 2, n], sibling
        )

    across, side, up = peers
    depth = rows // 2

    def to_chip(s, turn, n, h):
        part = slice(h * depth, (h + 1) * depth)
        return remote(
            passed.at[s, n, part], taken.at[s, turn % 2, n - 1, part],
            chip_send.at[s, n - 1, h], chip_recv.at[s, turn % 2, n - 1, h], peers[n],
        )

    def to_middle(s, turn, h):
        return remote(
            passed.at[s, 0, h * depth:(h + 1) * depth], middle.at[s, turn % 2, h],
            middle_send.at[s, h], middle_recv.at[s, turn % 2, h], peers[1 + h],
        )

    def chip_copies(s, turn):
        return [to_chip(s, turn, n, h) for n in (1, 2) for h in range(2)]

    def pass_on(s, turn):
        for h in range(2):
            to_middle(s, turn, h).wait_recv()
            total = kept[s, h] + middle[s, turn % 2, h].astype(jnp.float32)
            passed[s, 2 - h, h * depth:(h + 1) * depth] = total.astype(jnp.bfloat16)
            to_chip(s, turn, 2 - h, h).start()

    def half(turn, s):
        step = length - 1 - turn
        d = s
        when = time_of(d, step, length)
        load_acts(s, step).wait()
        load_grad(s, step).wait()
        held[s] += matmul(grad[s], w_dec[d], NT)

        @pl.when(turn > 0)
        def _():
            for copy in chip_copies(s, turn - 1):
                copy.wait_recv()

        live = info[s, :, LANES - 1:] > when.astype(jnp.float32)
        for g in range(groups):
            lanes = slice(g * LANES, (g + 1) * LANES)
            through = own[s, :, lanes]
            for n in range(2):
                through += jnp.where(turn > 0, taken[s, (turn + 1) % 2, n, :, lanes].astype(jnp.float32), 0.0)
            total = held[s, :, lanes] + through
            in_gate, forget, cell_gate, out_gate, old = (stage[s, k, :, lanes] for k in range(5))
            squash = jnp.tanh(forget * old + in_gate * cell_gate)
            later = cell_grad[s, :, lanes]
            new = jnp.where(live, later + total * out_gate * (1.0 - squash * squash), 0.0)
            out = jnp.where(live, total * squash, 0.0)
            values = (
                new * cell_gate * in_gate * (1.0 - in_gate),
                new * old * forget * (1.0 - forget),
                new * in_gate * (1.0 - cell_gate * cell_gate),
                out * out_gate * (1.0 - out_gate),
            )
            for k, value in enumerate(values):
                pre[s, :, (4 * g + k) * LANES:(4 * g + k + 1) * LANES] = value.astype(jnp.bfloat16)
            cell_grad[s, :, lanes] = new * forget + jnp.where(live, 0.0, later)
            held[s, :, lanes] = jnp.where(live, 0.0, total)

        @pl.when(turn > 0)
        def _():
            for n in range(4):
                to_core(s, turn - 1, n).wait_send()
            for h in range(2):
                to_middle(s, turn - 1, h).wait_send()
            for copy in chip_copies(s, turn - 1):
                copy.wait_send()

        for n, block in enumerate(tuple(other_core(peer) for peer in peers) + (sibling,)):
            sent[s, n] = matmul(pre[s], w[d, block], NT).astype(jnp.bfloat16)
            to_core(s, turn, n).start()
        if s == 0:
            @pl.when(turn > 0)
            def _():
                pass_on(1, turn - 1)
        else:
            pass_on(0, turn)

        for n, block in enumerate(peers + (me,)):
            part = matmul(pre[s], w[d, block], NT)
            to_core(s, turn, n).wait_recv()
            part += got[s, turn % 2, n].astype(jnp.float32)
            if n == 0:
                passed[s, 0] = part.astype(jnp.bfloat16)
                for h in range(2):
                    to_middle(s, turn, h).start()
            elif n < 3:
                now, later = n - 1, 2 - n
                kept[s, later] = part[later * depth:(later + 1) * depth]
                passed[s, n, now * depth:(now + 1) * depth] = (
                    part[now * depth:(now + 1) * depth].astype(jnp.bfloat16)
                )
                to_chip(s, turn, n, now).start()
            else:
                own[s] = part

        @pl.when(turn < length - 1)
        def _():
            load_acts(s, step - 1).start()
            load_grad(s, step - 1).start()

        load_whole(s, step).wait()
        for b in range(w.shape[1]):
            rec[s, b] += matmul(whole[s, b], pre[s], TN)

        @pl.when(turn < length - 1)
        def _():
            load_whole(s, step - 1).start()

        letters = lax.broadcasted_iota(jnp.int32, (VOCAB_PAD, rows), 0).astype(jnp.float32)
        hot = letters == ids[s, pl.ds(step, 1), :]
        letter_grad[s] += matmul(hot.astype(jnp.bfloat16), pre[s])

    def every(turn, carry):
        for s in range(2):
            half(turn, s)
        return carry

    lax.fori_loop(0, length, every, 0)
    pass_on(1, length - 1)
    for n in range(1, seqs):
        dec_copy(n).wait()
    for d in range(2):
        dec_out[d] = dec[seq, d].astype(jnp.float32) + sum(
            dec_in[n, d].astype(jnp.float32) for n in range(seqs - 1)
        )
    for s in range(2):
        for copy in chip_copies(s, length - 1):
            copy.wait_recv()
        total = held[s] + own[s]
        for n in range(2):
            total += taken[s, (length - 1) % 2, n].astype(jnp.float32)
        hidden_grad[s] = total
        for n in range(4):
            to_core(s, length - 1, n).wait_send()
        for h in range(2):
            to_middle(s, length - 1, h).wait_send()
        for copy in chip_copies(s, length - 1):
            copy.wait_send()

    def narrow(b, carry):
        for d in range(2):
            w[d, b] = rec[d, b].astype(jnp.bfloat16)
        store(b).start()
        return carry

    def store(b):
        return pltpu.make_async_copy(w.at[:, b], rec_out.at[:, b], store_sem.at[b])

    for b in range(w.shape[1]):
        narrow(b, 0)
    for b in range(w.shape[1]):
        store(b).wait()


def kernel_step(ids, lengths, order, h_init, c_init, embed, w_in, w_rec, bias, w_dec, b_dec):
    seqs = lax.axis_size("seq")
    local_times, all_streams = ids.shape
    length = local_times * seqs
    rows, units = h_init.shape[1:]
    streams = 2
    letters, width = embed.shape[1:]
    columns = w_rec.shape[2]
    blocks = w_rec.shape[1] // units
    any_space, vmem = pl.BlockSpec(memory_space=pl.ANY), pl.BlockSpec(memory_space=pltpu.VMEM)
    bias_grouped = jnp.swapaxes(bias.reshape(2, units // LANES, LANES, 4), -1, -2).reshape(2, 1, columns)
    f32, bf16 = jnp.float32, jnp.bfloat16
    dma = pltpu.SemaphoreType.DMA
    shape = jax.ShapeDtypeStruct
    wholes, acts, grads, w_grouped, loss, logit_sq, hidden_sq, dec_bias, dec_grad, info, slot_ids, w_in_grouped = pl.pallas_call(
        functools.partial(forward_kernel, length, letters),
        out_shape=(
            shape((length, streams, blocks, rows, units), bf16),
            shape((length, streams, 5, rows, units), f32),
            shape((length, streams, rows, VOCAB_PAD), bf16),
            shape((2, blocks, units, columns), bf16),
            shape((2, 8, LANES), f32),
            shape((2, 8, LANES), f32),
            shape((2, 8, LANES), f32),
            shape((2, 8, VOCAB_PAD), f32),
            shape((2, units, VOCAB_PAD), f32),
            shape((streams, rows, LANES), f32),
            shape((streams, length, rows), f32),
            shape((2, LANES, columns), bf16),
        ),
        in_specs=[vmem] * 10 + [any_space],
        out_specs=(any_space,) * 4 + (vmem,) * 8,
        scratch_shapes=[
            pltpu.VMEM((2, blocks, units, columns), bf16),
            pltpu.VMEM((blocks, 2, units, VOCAB_PAD), bf16),
            pltpu.VMEM((streams, 3, blocks, rows, units), bf16),
            pltpu.VMEM((streams, rows, units), f32),
            pltpu.VMEM((rows, columns), f32),
            pltpu.VMEM((rows, VOCAB_PAD), f32),
            pltpu.VMEM((streams, 5, rows, units), f32),
            pltpu.VMEM((streams, rows, VOCAB_PAD), bf16),
            pltpu.VMEM((seqs, 8, all_streams), f32),
            pltpu.VMEM((LANES, all_streams), f32),
            pltpu.VMEM((4 * LANES, 4 * LANES), bf16),
            pltpu.VMEM((2, VOCAB_PAD, LANES), bf16),
            pltpu.VMEM((2, 1, VOCAB_PAD), f32),
            pltpu.VMEM((1, 1), f32),
            dma((2,)),
            dma((seqs - 1,)),
            dma((seqs,)),
            dma((7,)),
            dma((blocks,)),
            dma((streams, 2, 10)),
            dma((streams, 3, blocks, 2)),
            dma((streams, 2)),
            dma((streams,)),
            dma((streams,)),
        ],
        compiler_params=pltpu.CompilerParams(
            collective_id=0, has_side_effects=True, vmem_limit_bytes=VMEM_LIMIT
        ),
        name="forward_visits",
    )(
        ids, lengths[None], order[None], h_init, c_init, embed, w_in, bias_grouped, b_dec, w_dec,
        w_rec.reshape(2, blocks, units, columns),
    )
    rec_grad, letter_grad, hidden_grad, cell_grad, dec_part = pl.pallas_call(
        functools.partial(backward_kernel, length),
        out_shape=(
            shape((2, blocks, units, columns), bf16),
            shape((2, VOCAB_PAD, columns), f32),
            shape((streams, rows, units), f32),
            shape((streams, rows, units), f32),
            shape((2, units // seqs, VOCAB_PAD), f32),
        ),
        in_specs=[vmem] * 4 + [any_space] * 4,
        out_specs=(any_space,) + (vmem,) * 4,
        scratch_shapes=[
            pltpu.VMEM((2, blocks, units, columns), bf16),
            pltpu.VMEM((2, blocks, units, columns), f32),
            pltpu.VMEM((streams, 5, rows, units), f32),
            pltpu.VMEM((streams, rows, VOCAB_PAD), bf16),
            pltpu.VMEM((streams, blocks, rows, units), bf16),
            pltpu.VMEM((streams, rows, columns), bf16),
            pltpu.VMEM((streams, rows, units), f32),
            pltpu.VMEM((streams, rows, units), f32),
            pltpu.VMEM((streams, 4, rows, units), bf16),
            pltpu.VMEM((streams, 2, 4, rows, units), bf16),
            pltpu.VMEM((streams, 3, rows, units), bf16),
            pltpu.VMEM((streams, 2, 2, rows, units), bf16),
            pltpu.VMEM((streams, 2, rows // 2, units), f32),
            pltpu.VMEM((streams, 2, 2, rows // 2, units), bf16),
            pltpu.VMEM((2, units, VOCAB_PAD), bf16),
            pltpu.VMEM((seqs, 2, units // seqs, VOCAB_PAD), bf16),
            pltpu.VMEM((seqs - 1, 2, units // seqs, VOCAB_PAD), bf16),
            dma,
            dma((streams,)),
            dma((streams,)),
            dma((streams,)),
            dma((streams, 4)),
            dma((streams, 2, 4)),
            dma((streams, 2, 2)),
            dma((streams, 2, 2, 2)),
            dma((streams, 2)),
            dma((streams, 2, 2)),
            dma((seqs - 1,)),
            dma((seqs - 1,)),
            dma((blocks,)),
        ],
        compiler_params=pltpu.CompilerParams(
            collective_id=1, has_side_effects=True, vmem_limit_bytes=VMEM_LIMIT
        ),
        name="backward_visits",
    )(info, slot_ids, w_dec, dec_grad, acts, grads, wholes, w_grouped)
    rec_part, edge_part, small = kernel_sums(
        rec_grad, letter_grad, embed, w_in_grouped, (loss, logit_sq, hidden_sq, dec_bias)
    )
    outs = (
        shape((1, 1), f32),
        shape(h_init.shape, f32),
        shape(h_init.shape, f32),
        shape(embed.shape, f32),
        shape((2, width, columns // seqs), f32),
        shape((2, w_rec.shape[1] // seqs, columns), f32),
        shape((2, columns // seqs), f32),
        shape((2, units // seqs, letters), f32),
        shape((2, letters), f32),
        shape((1, 2), f32),
        shape((1, 2), f32),
        shape((1, 2), f32),
    )
    tile = rec_part.shape[2]
    parts = rec_part.shape[1]
    results = pl.pallas_call(
        functools.partial(finish_kernel, w_rec.shape[1]),
        grid=(2, parts),
        out_shape=outs,
        in_specs=[vmem] * 7 + [pl.BlockSpec((1, 1, tile, columns), lambda d, r: (d, r, 0, 0))],
        out_specs=tuple(
            pl.BlockSpec((1, tile, columns), lambda d, r: (d, r, 0)) if n == 5 else vmem for n in range(len(outs))
        ),
        scratch_shapes=[pltpu.VMEM((4 * LANES, 4 * LANES), bf16)],
        compiler_params=pltpu.CompilerParams(
            dimension_semantics=("arbitrary", "arbitrary"), vmem_limit_bytes=VMEM_LIMIT
        ),
        name="results",
    )(lengths[None], embed, edge_part, dec_part, small, hidden_grad, cell_grad, rec_part)
    scalar = (0, 9, 10, 11)
    return tuple(
        x.reshape(()) if n == 0 else x.reshape(2) if n in scalar else x for n, x in enumerate(results)
    )


def finish_kernel(
    all_units, lens, embed, edge, dec, small, hidden_in, cell_in, rec,
    loss, hidden_grad, cell_grad, embed_grad, in_grad, rec_grad, bias_grad, dec_grad, dec_bias, rms_embed, rms_hidden,
    rms_logits, matrix,
):
    first = (pl.program_id(0) == 0) & (pl.program_id(1) == 0)
    letters, width = embed.shape[1:]
    span = matrix.shape[0]

    @pl.when(first)
    def _():
        matrix[...] = regroup_matrix(span)
        hidden_grad[...] = hidden_in[...]
        cell_grad[...] = cell_in[...]
        live = jnp.sum(lens[...].astype(jnp.float32), axis=1, keepdims=True)
        count = 2.0 * (live - lens.shape[1])
        at = 2 * TABLE
        loss[...] = small[at:at + 1, :1] / count
        for d in range(2):
            embed_grad[d] = small[d * TABLE:d * TABLE + letters, :width]
            in_grad[d] = edge[d, :width]
            bias_grad[d:d + 1] = edge[d, width:width + 1]
            dec_grad[d] = dec[d, :, :letters]
            for n in range(VOCAB_PAD // LANES):
                row = at + 5 + d * (VOCAB_PAD // LANES) + n
                last = min(LANES, letters - n * LANES)
                dec_bias[d:d + 1, n * LANES:n * LANES + last] = small[row:row + 1, :last]
            table = embed[d].astype(jnp.float32)
            square = jnp.sum(jnp.sum(table * table, axis=1, keepdims=True), axis=0, keepdims=True)
            rms_embed[:, d:d + 1] = jnp.sqrt(square / (letters * width))
            logit_sq = jnp.sum(small[at + 1 + d:at + 2 + d], axis=1, keepdims=True)
            hidden_sq = jnp.sum(small[at + 3 + d:at + 4 + d], axis=1, keepdims=True)
            rms_hidden[:, d:d + 1] = jnp.sqrt(hidden_sq / (all_units * live))
            rms_logits[:, d:d + 1] = jnp.sqrt(logit_sq / (letters * count / 2.0))

    for g in range(rec.shape[-1] // span):
        columns = slice(g * span, (g + 1) * span)
        rec_grad[0, :, columns] = matmul(rec[0, 0, :, columns], matrix[...], NT)


PIECE = 128
LAG = 3
WINDOW = 3
TABLE = 280


def spread(letter_grad, other, dims):
    high = letter_grad.astype(jnp.bfloat16)
    low = (letter_grad - high.astype(jnp.float32)).astype(jnp.bfloat16)
    return matmul(high, other, dims) + matmul(low, other, dims)


def reduce_kernel(
    rec_hbm, letter_grad, embed_in, w_in, loss, logit_sq, hidden_sq, dec_bias,
    rec_out, edge_out, small_out,
    own, ahead, behind, edge, edge_in, small, part, small_in, part_in, summed, matrix, embed,
    load_sem, line_send, line_recv, back_send, back_recv, edge_send, edge_recv,
    scatter_send, scatter_recv, seq_send, seq_recv, gather_send, gather_recv,
):
    seq, me = lax.axis_index("seq"), lax.axis_index("mp")
    count, parts = own.shape[1], own.shape[2]
    peers = lax.axis_size("mp")
    share = small.shape[0] // peers
    half = seq // (count // 2)
    place = seq + half * (count - 1 - 2 * seq)
    onward = 1 - 2 * half
    inner = count // 2 - 1
    lag = LAG + (inner - place) * 5
    load = pltpu.make_async_copy(rec_hbm, own, load_sem)
    load.start()

    def other_seq(n):
        return (seq + n) % count

    def other_mp(n):
        return (me + n) % peers

    barrier = pltpu.get_barrier_semaphore()
    for n in range(1, count):
        pl.semaphore_signal(barrier, inc=1, device_id=(other_seq(n), me), device_id_type=MESH)
    for n in range(1, peers):
        pl.semaphore_signal(barrier, inc=1, device_id=(seq, other_mp(n)), device_id_type=MESH)
    pl.semaphore_wait(barrier, count + peers - 2)
    load.wait()

    def send(src, dst, send_sem, recv_sem, seq_to, mp_to):
        return pltpu.make_async_remote_copy(
            src_ref=src, dst_ref=dst, send_sem=send_sem, recv_sem=recv_sem,
            device_id=(seq_to, mp_to), device_id_type=MESH,
        )

    def actual(chunk):
        return chunk + half * (count - 1 - 2 * chunk)

    pieces = 2 * parts

    def slot(k):
        return k // pieces, (k % pieces) // parts, k % parts

    def piece(chunk, d, r):
        return own.at[d, actual(chunk), r]

    def line_copy(k, crossing):
        i, d, r = slot(k)
        target = behind.at[i, d, r] if crossing else ahead.at[i, d, r]
        sem = back_recv.at[i, d, r] if crossing else line_recv.at[i, d, r]
        return send(piece(count - 1 - i, d, r), target, line_send.at[i, d, r], sem, seq + onward, me)

    def back_copy(k):
        i, d, r = slot(k)
        return send(
            piece(i, d, r), behind.at[i, d, r], back_send.at[i, d, r], back_recv.at[i, d, r], seq - onward, me
        )

    def add(chunk, d, r, term):
        ref = piece(chunk, d, r)
        ref[...] = (ref[...].astype(jnp.float32) + term[...].astype(jnp.float32)).astype(jnp.bfloat16)

    def line(k):
        i, d, r = slot(k)

        @pl.when((place > 0) & (i <= count - 1 - place))
        def _():
            line_copy(k, False).wait_recv()
            add(count - 1 - i, d, r, ahead.at[i, d, r])

        @pl.when((place == 0) & (k >= WINDOW))
        def _():
            line_copy(k - WINDOW, False).wait_send()

        @pl.when((i <= count - 2 - place) & (place < inner))
        def _():
            line_copy(k, False).start()

        @pl.when((i <= count - 2 - place) & (place == inner))
        def _():
            line_copy(k, True).start()

    def back(k):
        i, d, r = slot(k)

        @pl.when(i <= place)
        def _():
            back_copy(k).wait_recv()
            add(i, d, r, behind.at[i, d, r])

        @pl.when(i < place)
        def _():
            back_copy(k).start()

    def advance(k, carry):
        @pl.when(k < (count - 1) * pieces)
        def _():
            line(k)

        @pl.when((k >= lag) & (k - lag < (count // 2) * pieces))
        def _():
            back(k - lag)

        return carry

    def edge_copy(n):
        to = other_seq(n)
        return send(edge.at[to], edge_in.at[n - 1], edge_send.at[n - 1], edge_recv.at[n - 1], to, me)

    def scatter_copy(n):
        to = other_mp(n)
        rows = pl.ds(pl.multiple_of(to * share, 8), share)
        return send(small.at[rows], small_in.at[n - 1], scatter_send.at[n - 1], scatter_recv.at[n - 1], seq, to)

    def seq_copy(n):
        return send(part, part_in.at[n - 1], seq_send.at[n - 1], seq_recv.at[n - 1], other_seq(n), me)

    own_rows = pl.ds(pl.multiple_of(me * share, 8), share)

    def gather_copy(n):
        return send(
            summed.at[own_rows], summed.at[own_rows], gather_send.at[n - 1], gather_recv.at[me], seq, other_mp(n)
        )

    def gather_arrival(n):
        source = other_mp(n)
        rows = pl.ds(pl.multiple_of(source * share, 8), share)
        return send(summed.at[rows], summed.at[rows], gather_send.at[n - 1], gather_recv.at[source], seq, source)

    start = 6
    lax.fori_loop(0, 2, advance, 0)
    matrix[...] = regroup_matrix(matrix.shape[0])
    letters, width = embed_in.shape[1:]
    lanes = lax.broadcasted_iota(jnp.int32, (letters, LANES), 1)
    padded(embed, embed_in)
    for d in range(2):
        embed[d, :letters] = jnp.where(lanes == width, 1.0, embed[d, :letters].astype(jnp.float32)).astype(jnp.bfloat16)
    first = jnp.where(me == 0, 1.0, 0.0)
    for d in range(2):
        small[d * TABLE:(d + 1) * TABLE] = spread(letter_grad[d], w_in[d], NT)[:TABLE]
    small[2 * TABLE:] = jnp.zeros((small.shape[0] - 2 * TABLE, LANES), jnp.float32)
    at = 2 * TABLE
    small[at:at + 1] = jnp.sum(loss[0] + loss[1], axis=0, keepdims=True) * first
    for d in range(2):
        small[at + 1 + d:at + 2 + d] = jnp.sum(logit_sq[d], axis=0, keepdims=True) * first
        small[at + 3 + d:at + 4 + d] = jnp.sum(hidden_sq[d], axis=0, keepdims=True)
        row = jnp.sum(dec_bias[d], axis=0, keepdims=True) * first
        for n in range(VOCAB_PAD // LANES):
            line_at = at + 5 + d * (VOCAB_PAD // LANES) + n
            small[line_at:line_at + 1] = row[:, n * LANES:(n + 1) * LANES]
    for n in range(1, peers):
        scatter_copy(n).start()
    rows = edge.shape[2]
    span = matrix.shape[0]
    wide = own.shape[-1] // count
    for d in range(2):
        full = spread_left(embed[d], letter_grad[d]).astype(jnp.bfloat16)
        flat = [
            matmul(full[:, g * span:(g + 1) * span], matrix[...], NT).astype(jnp.bfloat16)
            for g in range(own.shape[-1] // span)
        ]
        for q in range(count):
            group, offset = (q * wide) // span, (q * wide) % span
            edge[q, d] = flat[group][:rows, offset:offset + wide]
    for n in range(1, count):
        edge_copy(n).start()
    lax.fori_loop(2, start, advance, 0)
    for n in range(1, peers):
        scatter_copy(n).wait()
    total = small[own_rows, :]
    for n in range(1, peers):
        total += small_in[n - 1]
    part[...] = total
    for n in range(1, count):
        seq_copy(n).start()
    lax.fori_loop(start, 2 * start, advance, 0)
    for n in range(1, count):
        seq_copy(n).wait()
        total += part_in[n - 1]
    summed[own_rows, :] = total
    for n in range(1, peers):
        gather_copy(n).start()
    lax.fori_loop(2 * start, (count - 1) * pieces + LAG, advance, 0)
    for n in range(1, peers):
        gather_copy(n).wait_send()
        gather_arrival(n).wait_recv()
    small_out[...] = summed[...]
    for n in range(1, count):
        edge_copy(n).wait()
    for d in range(2):
        edge_out[d] = edge[seq, d].astype(jnp.float32) + sum(
            edge_in[n, d].astype(jnp.float32) for n in range(count - 1)
        )
        rec_out[d] = own[d, seq]

    def finish(k, carry):
        i, d, r = slot(k)

        @pl.when((i <= count - 2 - place) & ((place > 0) | (k >= (count - 1) * pieces - WINDOW)))
        def _():
            line_copy(k, False).wait_send()

        @pl.when((i < place) & (k < (count // 2) * pieces))
        def _():
            back_copy(k).wait_send()

        return carry

    lax.fori_loop(0, (count - 1) * pieces, finish, 0)


def spread_left(other, letter_grad):
    high = letter_grad.astype(jnp.bfloat16)
    low = (letter_grad - high.astype(jnp.float32)).astype(jnp.bfloat16)
    return matmul(other, high, TN) + matmul(other, low, TN)


def kernel_sums(rec_grad, letter_grad, embed, w_in_grouped, stats):
    count = lax.axis_size("seq")
    peers = lax.axis_size("mp")
    columns = rec_grad.shape[-1]
    all_rows = rec_grad.shape[1] * rec_grad.shape[2]
    parts = all_rows // count // PIECE
    width = embed.shape[2]
    edge_rows = -(-(width + 1) // 8) * 8
    small_rows = -(-(2 * TABLE + 16) // (8 * peers)) * 8 * peers
    share = small_rows // peers
    f32, bf16 = jnp.float32, jnp.bfloat16
    dma = pltpu.SemaphoreType.DMA
    shape = jax.ShapeDtypeStruct
    vmem = pl.BlockSpec(memory_space=pltpu.VMEM)
    return pl.pallas_call(
        reduce_kernel,
        out_shape=(
            shape((2, parts, PIECE, columns), bf16),
            shape((2, edge_rows, columns // count), f32),
            shape((small_rows, LANES), f32),
        ),
        in_specs=[pl.BlockSpec(memory_space=pl.ANY)] + [vmem] * 7,
        out_specs=(vmem,) * 3,
        scratch_shapes=[
            pltpu.VMEM((2, count, parts, PIECE, columns), bf16),
            pltpu.VMEM((count - 1, 2, parts, PIECE, columns), bf16),
            pltpu.VMEM((count // 2, 2, parts, PIECE, columns), bf16),
            pltpu.VMEM((count, 2, edge_rows, columns // count), bf16),
            pltpu.VMEM((count - 1, 2, edge_rows, columns // count), bf16),
            pltpu.VMEM((small_rows, LANES), f32),
            pltpu.VMEM((share, LANES), f32),
            pltpu.VMEM((peers - 1, share, LANES), f32),
            pltpu.VMEM((count - 1, share, LANES), f32),
            pltpu.VMEM((small_rows, LANES), f32),
            pltpu.VMEM((4 * LANES, 4 * LANES), bf16),
            pltpu.VMEM((2, VOCAB_PAD, LANES), bf16),
            dma,
            dma((count - 1, 2, parts)),
            dma((count - 1, 2, parts)),
            dma((count // 2, 2, parts)),
            dma((count // 2, 2, parts)),
            dma((count - 1,)),
            dma((count - 1,)),
            dma((peers - 1,)),
            dma((peers - 1,)),
            dma((count - 1,)),
            dma((count - 1,)),
            dma((peers - 1,)),
            dma((peers,)),
        ],
        compiler_params=pltpu.CompilerParams(
            collective_id=2, has_side_effects=True, vmem_limit_bytes=VMEM_LIMIT
        ),
        name="gradient_sums",
    )(
        rec_grad.reshape(2, count, parts, PIECE, columns), letter_grad, embed, w_in_grouped, *stats,
    )


def plain_step(ids, lengths, order, count, h_init, c_init, embed, w_in, w_rec, bias, w_dec, b_dec, matrix):
    first_mp = (lax.axis_index("mp") == 0).astype(jnp.float32)
    per_dev, own_units = h_init.shape[1:]
    lanes = matrix.shape[0] // 4
    wd_full = lax.all_gather(w_dec, "mp", axis=1, tiled=True)
    whole_ids = lax.all_gather(ids, "seq", axis=0, tiled=True)
    own_order = lax.dynamic_slice_in_dim(order, lax.axis_index("seq") * per_dev, per_dev)
    slot_ids = jnp.take(whole_ids, own_order, axis=1)
    own_len = jnp.take(lengths, own_order)
    step_ids = jnp.stack([slot_ids, jnp.flip(slot_ids, 0)])
    w_rec_grouped = grouped(w_rec, matrix)
    w_in_grouped = grouped(w_in, matrix)
    bias_grouped = jnp.swapaxes(
        bias.reshape(2, own_units // lanes, lanes, 4), -1, -2
    ).reshape(bias.shape)
    loss, hidden_sq, logit_sq, dec_bias, dec_grad, hidden_grad, cell_grad, rec_grad, letter_grad = recurrences(
        step_ids, own_len, h_init, c_init, embed, w_in_grouped, w_rec_grouped, bias_grouped, w_dec, wd_full,
        b_dec, count, lanes,
    )
    embed_wide = embed.astype(jnp.float32)
    in_grad = jnp.einsum("dve,dvc->dec", embed_wide, letter_grad, precision=lax.Precision.HIGHEST)
    bias_grad = jnp.sum(letter_grad, axis=1, keepdims=True)
    embed_part = jnp.einsum(
        "dvc,dec->dve", letter_grad, w_in_grouped.astype(jnp.float32), precision=lax.Precision.HIGHEST
    )
    edge = ungrouped_wide(jnp.concatenate([in_grad, bias_grad], axis=1), lanes)
    rec_part = lax.psum_scatter(rec_grad.astype(jnp.bfloat16), "seq", scatter_dimension=1, tiled=True)
    edge_part = lax.psum_scatter(edge.astype(jnp.bfloat16), "seq", scatter_dimension=2, tiled=True)
    dec_part = lax.psum_scatter(dec_grad.astype(jnp.bfloat16), "seq", scatter_dimension=1, tiled=True)
    loss_sum, hidden_all, logit_all, dec_bias_grad, embed_grad = lax.psum(
        (loss * first_mp, hidden_sq, logit_sq * first_mp, dec_bias * first_mp, embed_part), ("seq", "mp")
    )
    rec_out = ungrouped(rec_part, matrix).astype(jnp.float32)
    return (
        loss_sum, hidden_all, logit_all, dec_bias_grad, dec_part.astype(jnp.float32), hidden_grad, cell_grad, rec_out,
        edge_part[:, :-1].astype(jnp.float32), edge_part[:, -1].astype(jnp.float32), embed_grad,
    )


def per_device(ids, lengths, order, h_init, c_init, embed, w_in, w_rec, bias, w_dec, b_dec):
    streams = ids.shape[1]
    per_dev, own_units = h_init.shape[1:]
    all_units, letter_count = w_rec.shape[1], embed.shape[1]
    fits = own_units % LANES == 0 and per_dev % LANES == 0 and per_dev <= 256 and own_units <= 256
    fits = fits and all_units % (lax.axis_size("seq") * PIECE) == 0 and letter_count <= TABLE
    if lax.axis_size("mp") == 8 and lax.axis_size("seq") == 4 and fits and embed.shape[2] < LANES:
        return kernel_step(ids, lengths, order, h_init, c_init, embed, w_in, w_rec, bias, w_dec, b_dec)
    live_total = jnp.sum(lengths).astype(jnp.float32)
    count = 2.0 * (jnp.sum(lengths) - streams).astype(jnp.float32)
    _, matrix = column_order(own_units)
    (
        loss_sum, hidden_all, logit_all, dec_bias_grad, dec_part, hidden_grad, cell_grad, rec_out, in_out, bias_out,
        embed_grad,
    ) = plain_step(ids, lengths, order, count, h_init, c_init, embed, w_in, w_rec, bias, w_dec, b_dec, matrix)
    embed_wide = embed.astype(jnp.float32)
    rms_embed = jnp.sqrt(jnp.mean(embed_wide * embed_wide, axis=(1, 2)))
    return (
        loss_sum / count,
        hidden_grad,
        cell_grad,
        embed_grad,
        in_out,
        rec_out,
        bias_out,
        dec_part,
        dec_bias_grad,
        rms_embed,
        jnp.sqrt(hidden_all / (all_units * live_total)),
        jnp.sqrt(logit_all / (letter_count * count / 2.0)),
    )


def solution(mesh):
    in_specs = (
        P("seq", None),
        P(),
        P(),
        P(None, "seq", "mp"),
        P(None, "seq", "mp"),
        P(),
        P(None, None, "mp"),
        P(None, None, "mp"),
        P(None, "mp"),
        P(None, "mp", None),
        P(),
    )
    out_specs = (
        P(),
        P(None, "seq", "mp"),
        P(None, "seq", "mp"),
        P(),
        P(None, None, ("mp", "seq")),
        P(None, "seq", "mp"),
        P(None, ("mp", "seq")),
        P(None, ("mp", "seq"), None),
        P(),
        P(),
        P(),
        P(),
    )
    return jax.shard_map(
        per_device, mesh=mesh, in_specs=in_specs, out_specs=out_specs, check_vma=False
    )
```

```python
import functools

import jax
import jax.numpy as jnp
from jax import lax
from jax.experimental import pallas as pl
from jax.experimental.pallas import tpu as pltpu
from jax.sharding import PartitionSpec as P

VMEM_LIMIT = 58 * 2**20


def column_order(own_units):
    lanes = min(128, own_units)
    source = jnp.arange(4 * lanes, dtype=jnp.int32)
    place = (source % 4) * lanes + source // 4
    matrix = (place[:, None] == jnp.arange(4 * lanes, dtype=jnp.int32)[None, :]).astype(jnp.bfloat16)
    return lanes, matrix


def grouped(x, matrix):
    width = matrix.shape[0]
    parts = x.reshape(x.shape[:-1] + (x.shape[-1] // width, width))
    out = jnp.einsum("...gc,cp->...gp", parts, matrix, preferred_element_type=jnp.float32)
    return out.astype(x.dtype).reshape(x.shape)


def ungrouped(x, matrix):
    return grouped(x, matrix.T)


def ungrouped_wide(x, lanes):
    parts = x.reshape(x.shape[:-1] + (x.shape[-1] // (4 * lanes), 4, lanes))
    return jnp.swapaxes(parts, -1, -2).reshape(x.shape)


def gates_of(pre, lanes):
    parts = pre.reshape(pre.shape[:-1] + (pre.shape[-1] // (4 * lanes), 4, lanes))
    flat = pre.shape[:-1] + (pre.shape[-1] // 4,)
    return tuple(parts[..., k, :].reshape(flat) for k in range(4))


def joined_gates(gates, lanes):
    split = [g.reshape(g.shape[:-1] + (g.shape[-1] // lanes, 1, lanes)) for g in gates]
    joined = jnp.concatenate(split, axis=-2)
    return joined.reshape(gates[0].shape[:-1] + (4 * gates[0].shape[-1],))


def recurrences(step_ids, own_len, h_init, c_init, embed, w_in, w_rec, bias, w_dec, wd_full, b_dec, count, lanes):
    length, per_dev = step_ids.shape[1:]
    letter_count = embed.shape[1]
    steps = jnp.arange(length, dtype=jnp.int32)
    live_steps = jnp.stack(
        [steps[:, None] < own_len[None, :], (length - 1 - steps)[:, None] < own_len[None, :]], axis=1
    )[..., None]
    letters = jnp.arange(letter_count, dtype=jnp.int32)
    onehot = (jnp.swapaxes(step_ids, 0, 1)[..., None] == letters).astype(jnp.bfloat16)
    letter_rows = jnp.einsum(
        "sdbv,dve->sdbe", onehot, embed, preferred_element_type=jnp.float32
    ).astype(jnp.bfloat16)
    gates_in = jnp.einsum(
        "sdbe,dec->sdbc", letter_rows, w_in, preferred_element_type=jnp.float32
    ).astype(jnp.bfloat16)

    def forward_step(carry, inputs):
        hidden, cell = carry
        gate_in, live = inputs
        whole = lax.all_gather(hidden, "mp", axis=2, tiled=True)
        recurrent = jnp.einsum("dbh,dhc->dbc", whole, w_rec, preferred_element_type=jnp.float32)
        pre = gate_in.astype(jnp.float32) + recurrent + bias[:, None]
        in_pre, forget_pre, cell_pre, out_pre = gates_of(pre, lanes)
        in_gate, forget, out_gate = (jax.nn.sigmoid(x) for x in (in_pre, forget_pre, out_pre))
        cell_gate = jnp.tanh(cell_pre)
        new_cell = forget * cell + in_gate * cell_gate
        cell_next = jnp.where(live, new_cell, cell)
        hidden_next = jnp.where(
            live, out_gate * jnp.tanh(new_cell), hidden.astype(jnp.float32)
        ).astype(jnp.bfloat16)
        return ((hidden_next, cell_next), (whole, cell, in_gate, forget, cell_gate, out_gate))

    (last_hidden, last_cell), (wholes, cells, *gates) = lax.scan(
        forward_step, (h_init, c_init), (gates_in, live_steps)
    )
    last_whole = lax.all_gather(last_hidden, "mp", axis=2, tiled=True)
    after = jnp.concatenate([wholes[1:], last_whole[None]], axis=0)
    own = h_init.shape[2]
    mine = lax.dynamic_slice_in_dim(after, lax.axis_index("mp") * own, own, axis=3)
    mine_wide = mine.astype(jnp.float32)
    hidden_sq = jnp.sum(jnp.where(live_steps, mine_wide * mine_wide, 0.0), axis=(0, 2, 3))
    logits = (
        jnp.einsum("sdbh,dhv->sdbv", after, wd_full, preferred_element_type=jnp.float32) + b_dec[None, :, None]
    )
    targets = jnp.swapaxes(jnp.concatenate([step_ids[:, 1:], step_ids[:, :1]], axis=1), 0, 1)
    fore_valid = (steps[:, None] + 1 < own_len[None, :])
    back_valid = (steps[:, None] < length - 1) & ((length - 1 - steps)[:, None] < own_len[None, :])
    valid = jnp.stack([fore_valid, back_valid], axis=1).astype(jnp.float32)
    logit_sq = jnp.sum(valid[..., None] * logits * logits, axis=(0, 2, 3))
    top = jnp.max(logits, axis=-1, keepdims=True)
    log_total = top + jnp.log(jnp.sum(jnp.exp(logits - top), axis=-1, keepdims=True))
    target_hot = targets[..., None] == letters
    picked = jnp.sum(jnp.where(target_hot, logits, 0.0), axis=-1)
    loss = jnp.sum(valid * (log_total[..., 0] - picked))
    grad_logits = (
        valid[..., None] * (jnp.exp(logits - log_total) - target_hot.astype(jnp.float32)) / count
    ).astype(jnp.bfloat16)
    dec_bias = jnp.sum(grad_logits.astype(jnp.float32), axis=(0, 2))
    dec_grad = jnp.einsum("sdbh,sdbv->dhv", mine, grad_logits, preferred_element_type=jnp.float32)

    def backward_step(carry, inputs):
        grad_hidden, grad_cell = carry
        live, cell, in_gate, forget, cell_gate, out_gate, grad_logit = inputs
        grad_hidden = grad_hidden + jnp.einsum(
            "dbv,dhv->dbh", grad_logit, w_dec, preferred_element_type=jnp.float32
        )
        squash = jnp.tanh(forget * cell + in_gate * cell_gate)
        grad_new = jnp.where(live, grad_cell + grad_hidden * out_gate * (1.0 - squash * squash), 0.0)
        grad_out = jnp.where(live, grad_hidden * squash, 0.0)
        grad_pre = joined_gates(
            [
                grad_new * cell_gate * in_gate * (1.0 - in_gate),
                grad_new * cell * forget * (1.0 - forget),
                grad_new * in_gate * (1.0 - cell_gate * cell_gate),
                grad_out * out_gate * (1.0 - out_gate),
            ],
            lanes,
        ).astype(jnp.bfloat16)
        grad_cell_prev = grad_new * forget + jnp.where(live, 0.0, grad_cell)
        held = jnp.where(live, 0.0, grad_hidden)
        terms = jnp.einsum("dbc,dhc->dbh", grad_pre, w_rec, preferred_element_type=jnp.float32)
        through = lax.psum_scatter(
            terms.astype(jnp.bfloat16), "mp", scatter_dimension=2, tiled=True
        ).astype(jnp.float32)
        return ((held + through, grad_cell_prev), grad_pre)

    start = jnp.zeros(c_init.shape, jnp.float32)
    (hidden_grad, cell_grad), grad_pres = lax.scan(
        backward_step, (start, start), (live_steps, cells, *gates, grad_logits), reverse=True
    )
    rec_grad = jnp.einsum("sdbh,sdbc->dhc", wholes, grad_pres, preferred_element_type=jnp.float32)
    letter_grad = jnp.einsum("sdbv,sdbc->dvc", onehot, grad_pres, preferred_element_type=jnp.float32)
    return loss, hidden_sq, logit_sq, dec_bias, dec_grad, hidden_grad, cell_grad, rec_grad, letter_grad


MESH = pl.DeviceIdType.MESH
LANES = 128
VOCAB_PAD = 384
NT = (((1,), (1,)), ((), ()))
TN = (((0,), (0,)), ((), ()))


def sigmoid(x):
    return 0.5 * jnp.tanh(0.5 * x) + 0.5


def matmul(left, right, dims=(((1,), (0,)), ((), ()))):
    return lax.dot_general(left, right, dims, preferred_element_type=jnp.float32)


def neighbours():
    me = lax.axis_index("mp")
    row, column, core = me // 4, (me // 2) % 2, me % 2
    sibling = row * 4 + column * 2 + (1 - core)
    across = (1 - row) * 4 + (1 - column) * 2 + core
    side = row * 4 + (1 - column) * 2 + core
    up = (1 - row) * 4 + column * 2 + core
    return me, sibling, (across, side, up)


def greet(peers, seqs=0):
    seq, me = lax.axis_index("seq"), lax.axis_index("mp")
    barrier = pltpu.get_barrier_semaphore()
    for peer in peers:
        pl.semaphore_signal(barrier, inc=1, device_id=(seq, peer), device_id_type=MESH)
    for n in range(1, seqs):
        pl.semaphore_signal(barrier, inc=1, device_id=((seq + n) % seqs, me), device_id_type=MESH)
    pl.semaphore_wait(barrier, len(peers) + max(seqs - 1, 0))


def remote(src, dst, send, recv, peer):
    return pltpu.make_async_remote_copy(
        src_ref=src, dst_ref=dst, send_sem=send, recv_sem=recv,
        device_id=(lax.axis_index("seq"), peer), device_id_type=MESH,
    )


def other_core(peer):
    return (peer // 2) * 2 + (1 - peer % 2)


def folded(x):
    return jnp.sum(x.reshape(x.shape[0] // 8, 8, x.shape[1]), axis=0)


def regroup_matrix(span):
    source = lax.broadcasted_iota(jnp.int32, (span, span), 0)
    place = (source & 3) * (span // 4) + (source >> 2)
    return (place == lax.broadcasted_iota(jnp.int32, (span, span), 1)).astype(jnp.bfloat16)


def padded(ref, value):
    ref[...] = jnp.zeros(ref.shape, ref.dtype)
    for d in range(2):
        ref[d, :value.shape[1], :value.shape[2]] = value[d]


def column_of(table, lane):
    lanes = lax.broadcasted_iota(jnp.int32, table.shape, 1)
    return jnp.sum(jnp.where(lanes == lane, table, 0.0), axis=1, keepdims=True)


def time_of(direction, step, length):
    return step if direction == 0 else length - 1 - step


def forward_kernel(
    length, letters, ids_in, lens, order, h_in, c_in, embed_in, w_in_raw, bias, b_dec_in, w_dec_in, w_hbm,
    wholes, acts, grads, w_out, loss, logit_sq, hidden_sq, dec_bias, dec_grad, info, ids, w_in,
    w, wd, buf, cell, acc, logit, stage, grad, all_ids, table, matrix, embed, b_dec, inverse, load_sem, ids_send, ids_recv, wd_send, wd_recv, wd_plane_send,
    wd_core_recv, send_sem, recv_sem, save_sem, act_sem, grad_sem,
):
    me, sibling, peers = neighbours()
    seq, seqs, times = lax.axis_index("seq"), all_ids.shape[0], ids_in.shape[0]
    blocks, rows, units = buf.shape[2:]
    groups, span = units // LANES, matrix.shape[0]
    columns = w.shape[-1]
    load_w = pltpu.make_async_copy(w_hbm, w, load_sem.at[0])
    store_w = pltpu.make_async_copy(w, w_out, load_sem.at[1])
    load_w.start()
    all_ids[seq, :times] = ids_in[...].astype(jnp.float32)
    matrix[...] = regroup_matrix(span)
    for s in range(2):
        buf[s, 0, me] = h_in[s]
    greet((sibling,) + peers, seqs)

    def ids_copy(n):
        to = (seq + n) % seqs
        block = all_ids.at[seq]
        return pltpu.make_async_remote_copy(
            src_ref=block, dst_ref=block, send_sem=ids_send.at[n - 1], recv_sem=ids_recv.at[seq],
            device_id=(to, me), device_id_type=MESH,
        )

    def ids_arrival(n):
        source = (seq + n) % seqs
        block = all_ids.at[source]
        return pltpu.make_async_remote_copy(
            src_ref=block, dst_ref=block, send_sem=ids_send.at[n - 1], recv_sem=ids_recv.at[source],
            device_id=(source, me), device_id_type=MESH,
        )

    across, side, up = peers
    depth = rows // 2

    def transfer(s, step, block, h, index, peer):
        slot, par = step % 3, step % 2
        ref = buf.at[s, slot, block, h * depth:(h + 1) * depth]
        return remote(ref, ref, send_sem.at[s, par, index], recv_sem.at[s, slot, block, h], peer)

    def transfer_whole(s, step, block, index):
        slot, par = step % 3, step % 2
        ref = buf.at[s, slot, block]
        return remote(ref, ref, send_sem.at[s, par, index], recv_sem.at[s, slot, block, 0], sibling)

    def direct(s, step):
        plan = ((0, side), (1, up), (1, side), (0, up))
        return [transfer(s, step, me, h, n, peer) for n, (h, peer) in enumerate(plan)]

    def pass_on(s, step):
        for n, (block, h, peer) in enumerate(((side, 0, up), (up, 1, side))):
            transfer(s, step, block, h, 0, sibling).wait_recv()
            transfer(s, step, block, h, 4 + n, peer).start()

    def core_copies(s, step):
        return [transfer_whole(s, step, block, 6 + n) for n, block in enumerate((me, side, up, across))]

    share = units // seqs

    def wd_rows(source, quarter):
        return wd.at[source, :, pl.ds(pl.multiple_of(quarter * share, 16), share)]

    def wd_copy(n):
        ref = wd_rows(me, seq)
        return remote(ref, ref, wd_send.at[n], wd_recv.at[me, seq], peers[n])

    def wd_across(n, k):
        ref = wd_rows(peers[n], seq)
        return pltpu.make_async_remote_copy(
            src_ref=ref, dst_ref=ref, send_sem=wd_plane_send.at[n, k - 1], recv_sem=wd_recv.at[peers[n], seq],
            device_id=((seq + k) % seqs, me), device_id_type=MESH,
        )

    def wd_arrival(n, k):
        ref = wd_rows(peers[n], (seq + k) % seqs)
        return remote(ref, ref, wd_send.at[0], wd_recv.at[peers[n], (seq + k) % seqs], sibling)

    def wd_core(n, block):
        return remote(wd.at[block], wd.at[block], wd_send.at[3 + n], wd_core_recv.at[block], sibling)

    def save(s, step):
        return pltpu.make_async_copy(buf.at[s, step % 3], wholes.at[step, s], save_sem.at[s, step % 2])

    def save_acts(s, step):
        return pltpu.make_async_copy(stage.at[s], acts.at[step, s], act_sem.at[s])

    def save_grad(s, step):
        return pltpu.make_async_copy(grad.at[s], grads.at[step, s], grad_sem.at[s])

    def finish_sends(s, step):
        for copy in direct(s, step) + core_copies(s, step):
            copy.wait_send()
        for n, (block, h, peer) in enumerate(((side, 0, up), (up, 1, side))):
            transfer(s, step, block, h, 4 + n, peer).wait_send()

    for n in range(1, seqs):
        ids_copy(n).start()
    for s in range(2):
        for copy in direct(s, 0):
            copy.start()
        transfer_whole(s, 0, me, 6).start()
    padded(wd.at[me], w_dec_in)
    for n in range(3):
        wd_copy(n).start()
    wd_core(3, me).start()
    padded(embed, embed_in)
    padded(w_in, w_in_raw)
    b_dec[...] = jnp.full(b_dec.shape, -1e30, jnp.float32)
    for d in range(2):
        b_dec[d, :, :letters] = b_dec_in[d:d + 1]
    lengths = lens[...].astype(jnp.float32)
    inverse[...] = 0.5 / (jnp.sum(lengths, axis=1, keepdims=True) - lens.shape[1])
    for ref in (loss, logit_sq, hidden_sq, dec_bias, dec_grad):
        ref[...] = jnp.zeros(ref.shape, ref.dtype)
    cell[...] = c_in[...]
    for d in range(2):
        for g in range(columns // span):
            part = slice(g * span, (g + 1) * span)
            w_in[d, :, part] = matmul(w_in[d, :, part], matrix[...]).astype(jnp.bfloat16)
    load_w.wait()

    def regroup(b, carry):
        for d in range(2):
            for g in range(columns // span):
                part = slice(g * span, (g + 1) * span)
                w[d, b, :, part] = matmul(w[d, b, :, part], matrix[...]).astype(jnp.bfloat16)
        return carry

    for b in range(blocks):
        regroup(b, 0)
    store_w.start()
    for n in range(3):
        wd_arrival(n, 0).wait_recv()
        for k in range(1, seqs):
            wd_across(n, k).start()
    for n in range(1, seqs):
        ids_arrival(n).wait_recv()
    streams = rows
    order_row = order[:, pl.ds(pl.multiple_of(seq * rows, LANES), rows)]
    square = (rows, rows)
    diagonal = lax.broadcasted_iota(jnp.int32, square, 0) == lax.broadcasted_iota(jnp.int32, square, 1)
    order_column = jnp.sum(
        jnp.where(diagonal, jnp.broadcast_to(order_row.astype(jnp.float32), square), 0.0), axis=1, keepdims=True
    ).astype(jnp.int32)
    total_streams = lens.shape[1]
    pick_column = (
        lax.broadcasted_iota(jnp.int32, (streams, total_streams), 1) == order_column
    ).astype(jnp.bfloat16)
    pick_row = (
        lax.broadcasted_iota(jnp.int32, (total_streams, streams), 0) == order_row
    ).astype(jnp.bfloat16)
    table[...] = jnp.zeros(table.shape, table.dtype)
    for d in range(2):
        for t in range(length):
            row = t if d == 0 else length - 1 - t
            table[t:t + 1] = all_ids[row // times, row % times:row % times + 1]
        table[LANES - 1:] = lengths
        high = jnp.floor(table[...] * (1.0 / 16.0))
        low = (table[...] - 16.0 * high).astype(jnp.bfloat16)
        high = high.astype(jnp.bfloat16)
        values = 16.0 * matmul(pick_column, high, NT) + matmul(pick_column, low, NT)
        info[d] = values
        values = 16.0 * matmul(high[:length], pick_row) + matmul(low[:length], pick_row)
        ids[d] = values

    def gates(s, step):
        slot, later = step % 3, (step + 1) % 3
        d = s
        when = time_of(d, step, length)
        live = info[s, :, LANES - 1:] > when.astype(jnp.float32)
        for g in range(groups):
            lanes = slice(g * LANES, (g + 1) * LANES)
            pre = [acc[:, (4 * g + k) * LANES:(4 * g + k + 1) * LANES] for k in range(4)]
            in_gate, forget, out_gate = sigmoid(pre[0]), sigmoid(pre[1]), sigmoid(pre[3])
            cell_gate = jnp.tanh(pre[2])
            old = cell[s, :, lanes]
            new = forget * old + in_gate * cell_gate
            for k, value in enumerate((in_gate, forget, cell_gate, out_gate, old)):
                stage[s, k, :, lanes] = value
            cell[s, :, lanes] = jnp.where(live, new, old)
            before = buf[s, slot, me, :, lanes].astype(jnp.float32)
            hidden = jnp.where(live, out_gate * jnp.tanh(new), before).astype(jnp.bfloat16)
            buf[s, later, me, :, lanes] = hidden
            wide = hidden.astype(jnp.float32)
            hidden_sq[d] += folded(jnp.where(live, wide * wide, 0.0))

    def decode(s, step):
        slot = step % 3
        d = s
        total = jnp.broadcast_to(b_dec[d], logit.shape)
        for b in range(blocks):
            total += matmul(buf[s, slot, b], wd[b, d])
        logit[...] = total
        when = time_of(d, step - 1, length)
        reach = when + 1 if d == 0 else when
        lookup = info[s]
        valid = (lookup[:, LANES - 1:] > reach.astype(jnp.float32)) & (step < length)
        target = column_of(lookup, step)
        value = logit[...]
        lanes = lax.broadcasted_iota(jnp.int32, value.shape, 1)
        hot = lanes.astype(jnp.float32) == target
        top = jnp.max(value, axis=1, keepdims=True)
        power = jnp.exp(value - top)
        total = jnp.sum(power, axis=1, keepdims=True)
        picked = jnp.sum(jnp.where(hot, value, 0.0), axis=1, keepdims=True)
        loss[d] += folded(jnp.broadcast_to(jnp.where(valid, top + jnp.log(total) - picked, 0.0), (rows, LANES)))
        kept = jnp.where(valid & (lanes < letters), value, 0.0)
        square = kept * kept
        logit_sq[d] += folded(sum(square[:, n * LANES:(n + 1) * LANES] for n in range(VOCAB_PAD // LANES)))
        slope = jnp.where(
            valid, (power * (1.0 / total) - jnp.where(hot, 1.0, 0.0)) * inverse[...], 0.0
        ).astype(jnp.bfloat16)
        grad[s] = slope
        dec_bias[d] += folded(slope.astype(jnp.float32))
        dec_grad[d] += matmul(buf[s, slot, me], grad[s], TN)

    others = tuple(other_core(peer) for peer in peers)

    def half(step, s):
        d = s

        @pl.when(step == 2)
        def _():
            if s == 0:
                for n in range(3):
                    for k in range(1, seqs):
                        wd_arrival(n, k).wait_recv()
                    wd_core(n, peers[n]).start()
                for block in (sibling,) + others:
                    wd_core(0, block).wait_recv()
            decode(s, step - 1)
            save_grad(s, step - 2).start()

        @pl.when(step < length)
        def _():
            now = column_of(info[s], step)
            hot = (lax.broadcasted_iota(jnp.int32, (rows, VOCAB_PAD), 1).astype(jnp.float32) == now)
            row = matmul(hot.astype(jnp.bfloat16), embed[d]).astype(jnp.bfloat16)
            acc[...] = matmul(row, w_in[d]).astype(jnp.bfloat16).astype(jnp.float32) + bias[d]

        for n, (block, halves) in enumerate(((side, (1,)), (up, (0,)), (across, (0, 1)))):
            for h in halves:
                transfer(s, step, block, h, 0, sibling).wait_recv()
            transfer_whole(s, step, block, 7 + n).start()

        slot = step % 3

        def advance(block):
            acc[...] += matmul(buf[s, slot, block], w[d, block])

        @pl.when(step < length)
        def _():
            for block in (me,) + peers:
                advance(block)

        if s == 0:
            pass_on(1, step)
        else:
            @pl.when(step < length)
            def _():
                pass_on(0, step + 1)

        for block in (sibling,) + others:
            transfer_whole(s, step, block, 6).wait_recv()

        @pl.when(step < length)
        def _():
            for block in (sibling,) + others:
                advance(block)

        @pl.when(step < length)
        def _():

            @pl.when(step > 0)
            def _():
                save_acts(s, step - 1).wait()

            gates(s, step)

            @pl.when(step > 0)
            def _():
                save(s, step - 1).wait()
                finish_sends(s, step - 1)

            for copy in direct(s, step + 1):
                copy.start()
            transfer_whole(s, step + 1, me, 6).start()
            save_acts(s, step).start()
            save(s, step).start()

        @pl.when(step > 1)
        def _():
            save_grad(s, step - 2).wait()
            decode(s, step)
            save_grad(s, step - 1).start()

    def every(step, carry):
        for s in range(2):
            half(step, s)
        return carry

    pass_on(0, 0)
    lax.fori_loop(0, length + 1, every, 0)
    store_w.wait()
    for n in range(1, seqs):
        ids_copy(n).wait_send()
    for n in range(3):
        wd_copy(n).wait_send()
        for k in range(1, seqs):
            wd_across(n, k).wait_send()
    for n, block in enumerate(peers + (me,)):
        wd_core(n, block).wait_send()
    for s in range(2):
        save(s, length - 1).wait()
        save_acts(s, length - 1).wait()
        save_grad(s, length - 1).wait()
        finish_sends(s, length - 1)
        finish_sends(s, length)


def backward_kernel(
    length, info, ids, w_dec_in, dec_grad, acts, grads, wholes, w_hbm,
    rec_out, letter_grad, hidden_grad, cell_grad, dec_out,
    w, rec, stage, grad, whole, pre, held, own, sent, got, passed, taken, kept, middle, w_dec, dec, dec_in, load_sem, act_sem,
    grad_sem, whole_sem, core_send, core_recv, chip_send, chip_recv, middle_send, middle_recv, dec_send, dec_recv, store_sem,
):
    me, sibling, peers = neighbours()
    rows, units = held.shape[1:]
    groups = units // LANES
    load_w = pltpu.make_async_copy(w_hbm, w, load_sem)
    load_w.start()

    def load_acts(s, step):
        return pltpu.make_async_copy(acts.at[step, s], stage.at[s], act_sem.at[s])

    def load_grad(s, step):
        return pltpu.make_async_copy(grads.at[step, s], grad.at[s], grad_sem.at[s])

    def load_whole(s, step):
        return pltpu.make_async_copy(wholes.at[step, s], whole.at[s], whole_sem.at[s])

    for s in range(2):
        load_acts(s, length - 1).start()
        load_grad(s, length - 1).start()
        load_whole(s, length - 1).start()
    seq, seqs, tall = lax.axis_index("seq"), dec.shape[0], dec.shape[2]
    for q in range(seqs):
        for d in range(2):
            dec[q, d] = dec_grad[d, q * tall:(q + 1) * tall].astype(jnp.bfloat16)
    greet((sibling,) + peers, seqs)

    def dec_copy(n):
        to = (seq + n) % seqs
        return pltpu.make_async_remote_copy(
            src_ref=dec.at[to], dst_ref=dec_in.at[n - 1], send_sem=dec_send.at[n - 1], recv_sem=dec_recv.at[n - 1],
            device_id=(to, me), device_id_type=MESH,
        )

    for n in range(1, seqs):
        dec_copy(n).start()
    padded(w_dec, w_dec_in)
    held[...] = jnp.zeros(held.shape, held.dtype)
    own[...] = jnp.zeros(own.shape, own.dtype)
    cell_grad[...] = jnp.zeros(cell_grad.shape, cell_grad.dtype)
    letter_grad[...] = jnp.zeros(letter_grad.shape, letter_grad.dtype)

    def clear(b, carry):
        for d in range(2):
            rec[d, b] = jnp.zeros(rec.shape[2:], rec.dtype)
        return carry

    lax.fori_loop(0, w.shape[1], clear, 0)
    load_w.wait()

    def to_core(s, turn, n):
        return remote(
            sent.at[s, n], got.at[s, turn % 2, n], core_send.at[s, n], core_recv.at[s, turn % 2, n], sibling
        )

    across, side, up = peers
    depth = rows // 2

    def to_chip(s, turn, n, h):
        part = slice(h * depth, (h + 1) * depth)
        return remote(
            passed.at[s, n, part], taken.at[s, turn % 2, n - 1, part],
            chip_send.at[s, n - 1, h], chip_recv.at[s, turn % 2, n - 1, h], peers[n],
        )

    def to_middle(s, turn, h):
        return remote(
            passed.at[s, 0, h * depth:(h + 1) * depth], middle.at[s, turn % 2, h],
            middle_send.at[s, h], middle_recv.at[s, turn % 2, h], peers[1 + h],
        )

    def chip_copies(s, turn):
        return [to_chip(s, turn, n, h) for n in (1, 2) for h in range(2)]

    def pass_on(s, turn):
        for h in range(2):
            to_middle(s, turn, h).wait_recv()
            total = kept[s, h] + middle[s, turn % 2, h].astype(jnp.float32)
            passed[s, 2 - h, h * depth:(h + 1) * depth] = total.astype(jnp.bfloat16)
            to_chip(s, turn, 2 - h, h).start()

    def half(turn, s):
        step = length - 1 - turn
        d = s
        when = time_of(d, step, length)
        load_acts(s, step).wait()
        load_grad(s, step).wait()
        held[s] += matmul(grad[s], w_dec[d], NT)

        @pl.when(turn > 0)
        def _():
            for copy in chip_copies(s, turn - 1):
                copy.wait_recv()

        live = info[s, :, LANES - 1:] > when.astype(jnp.float32)
        for g in range(groups):
            lanes = slice(g * LANES, (g + 1) * LANES)
            through = own[s, :, lanes]
            for n in range(2):
                through += jnp.where(turn > 0, taken[s, (turn + 1) % 2, n, :, lanes].astype(jnp.float32), 0.0)
            total = held[s, :, lanes] + through
            in_gate, forget, cell_gate, out_gate, old = (stage[s, k, :, lanes] for k in range(5))
            squash = jnp.tanh(forget * old + in_gate * cell_gate)
            later = cell_grad[s, :, lanes]
            new = jnp.where(live, later + total * out_gate * (1.0 - squash * squash), 0.0)
            out = jnp.where(live, total * squash, 0.0)
            values = (
                new * cell_gate * in_gate * (1.0 - in_gate),
                new * old * forget * (1.0 - forget),
                new * in_gate * (1.0 - cell_gate * cell_gate),
                out * out_gate * (1.0 - out_gate),
            )
            for k, value in enumerate(values):
                pre[s, :, (4 * g + k) * LANES:(4 * g + k + 1) * LANES] = value.astype(jnp.bfloat16)
            cell_grad[s, :, lanes] = new * forget + jnp.where(live, 0.0, later)
            held[s, :, lanes] = jnp.where(live, 0.0, total)

        @pl.when(turn > 0)
        def _():
            for n in range(4):
                to_core(s, turn - 1, n).wait_send()
            for h in range(2):
                to_middle(s, turn - 1, h).wait_send()
            for copy in chip_copies(s, turn - 1):
                copy.wait_send()

        for n, block in enumerate(tuple(other_core(peer) for peer in peers) + (sibling,)):
            sent[s, n] = matmul(pre[s], w[d, block], NT).astype(jnp.bfloat16)
            to_core(s, turn, n).start()
        if s == 0:
            @pl.when(turn > 0)
            def _():
                pass_on(1, turn - 1)
        else:
            pass_on(0, turn)

        for n, block in enumerate(peers + (me,)):
            part = matmul(pre[s], w[d, block], NT)
            to_core(s, turn, n).wait_recv()
            part += got[s, turn % 2, n].astype(jnp.float32)
            if n == 0:
                passed[s, 0] = part.astype(jnp.bfloat16)
                for h in range(2):
                    to_middle(s, turn, h).start()
            elif n < 3:
                now, later = n - 1, 2 - n
                kept[s, later] = part[later * depth:(later + 1) * depth]
                passed[s, n, now * depth:(now + 1) * depth] = (
                    part[now * depth:(now + 1) * depth].astype(jnp.bfloat16)
                )
                to_chip(s, turn, n, now).start()
            else:
                own[s] = part

        @pl.when(turn < length - 1)
        def _():
            load_acts(s, step - 1).start()
            load_grad(s, step - 1).start()

        load_whole(s, step).wait()
        for b in range(w.shape[1]):
            rec[s, b] += matmul(whole[s, b], pre[s], TN)

        @pl.when(turn < length - 1)
        def _():
            load_whole(s, step - 1).start()

        letters = lax.broadcasted_iota(jnp.int32, (VOCAB_PAD, rows), 0).astype(jnp.float32)
        hot = letters == ids[s, pl.ds(step, 1), :]
        letter_grad[s] += matmul(hot.astype(jnp.bfloat16), pre[s])

    def every(turn, carry):
        for s in range(2):
            half(turn, s)
        return carry

    lax.fori_loop(0, length, every, 0)
    pass_on(1, length - 1)
    for n in range(1, seqs):
        dec_copy(n).wait()
    for d in range(2):
        dec_out[d] = dec[seq, d].astype(jnp.float32) + sum(
            dec_in[n, d].astype(jnp.float32) for n in range(seqs - 1)
        )
    for s in range(2):
        for copy in chip_copies(s, length - 1):
            copy.wait_recv()
        total = held[s] + own[s]
        for n in range(2):
            total += taken[s, (length - 1) % 2, n].astype(jnp.float32)
        hidden_grad[s] = total
        for n in range(4):
            to_core(s, length - 1, n).wait_send()
        for h in range(2):
            to_middle(s, length - 1, h).wait_send()
        for copy in chip_copies(s, length - 1):
            copy.wait_send()

    def narrow(b, carry):
        for d in range(2):
            w[d, b] = rec[d, b].astype(jnp.bfloat16)
        store(b).start()
        return carry

    def store(b):
        return pltpu.make_async_copy(w.at[:, b], rec_out.at[:, b], store_sem.at[b])

    for b in range(w.shape[1]):
        narrow(b, 0)
    for b in range(w.shape[1]):
        store(b).wait()


def kernel_step(ids, lengths, order, h_init, c_init, embed, w_in, w_rec, bias, w_dec, b_dec):
    seqs = lax.axis_size("seq")
    local_times, all_streams = ids.shape
    length = local_times * seqs
    rows, units = h_init.shape[1:]
    streams = 2
    letters, width = embed.shape[1:]
    columns = w_rec.shape[2]
    blocks = w_rec.shape[1] // units
    any_space, vmem = pl.BlockSpec(memory_space=pl.ANY), pl.BlockSpec(memory_space=pltpu.VMEM)
    bias_grouped = jnp.swapaxes(bias.reshape(2, units // LANES, LANES, 4), -1, -2).reshape(2, 1, columns)
    f32, bf16 = jnp.float32, jnp.bfloat16
    dma = pltpu.SemaphoreType.DMA
    shape = jax.ShapeDtypeStruct
    wholes, acts, grads, w_grouped, loss, logit_sq, hidden_sq, dec_bias, dec_grad, info, slot_ids, w_in_grouped = pl.pallas_call(
        functools.partial(forward_kernel, length, letters),
        out_shape=(
            shape((length, streams, blocks, rows, units), bf16),
            shape((length, streams, 5, rows, units), f32),
            shape((length, streams, rows, VOCAB_PAD), bf16),
            shape((2, blocks, units, columns), bf16),
            shape((2, 8, LANES), f32),
            shape((2, 8, LANES), f32),
            shape((2, 8, LANES), f32),
            shape((2, 8, VOCAB_PAD), f32),
            shape((2, units, VOCAB_PAD), f32),
            shape((streams, rows, LANES), f32),
            shape((streams, length, rows), f32),
            shape((2, LANES, columns), bf16),
        ),
        in_specs=[vmem] * 10 + [any_space],
        out_specs=(any_space,) * 4 + (vmem,) * 8,
        scratch_shapes=[
            pltpu.VMEM((2, blocks, units, columns), bf16),
            pltpu.VMEM((blocks, 2, units, VOCAB_PAD), bf16),
            pltpu.VMEM((streams, 3, blocks, rows, units), bf16),
            pltpu.VMEM((streams, rows, units), f32),
            pltpu.VMEM((rows, columns), f32),
            pltpu.VMEM((rows, VOCAB_PAD), f32),
            pltpu.VMEM((streams, 5, rows, units), f32),
            pltpu.VMEM((streams, rows, VOCAB_PAD), bf16),
            pltpu.VMEM((seqs, 8, all_streams), f32),
            pltpu.VMEM((LANES, all_streams), f32),
            pltpu.VMEM((4 * LANES, 4 * LANES), bf16),
            pltpu.VMEM((2, VOCAB_PAD, LANES), bf16),
            pltpu.VMEM((2, 1, VOCAB_PAD), f32),
            pltpu.VMEM((1, 1), f32),
            dma((2,)),
            dma((seqs - 1,)),
            dma((seqs,)),
            dma((7,)),
            dma((blocks, seqs)),
            dma((3, seqs - 1)),
            dma((blocks,)),
            dma((streams, 2, 10)),
            dma((streams, 3, blocks, 2)),
            dma((streams, 2)),
            dma((streams,)),
            dma((streams,)),
        ],
        compiler_params=pltpu.CompilerParams(
            collective_id=0, has_side_effects=True, vmem_limit_bytes=VMEM_LIMIT
        ),
        name="forward_visits",
    )(
        ids, lengths[None], order[None], h_init, c_init, embed, w_in, bias_grouped, b_dec, w_dec,
        w_rec.reshape(2, blocks, units, columns),
    )
    rec_grad, letter_grad, hidden_grad, cell_grad, dec_part = pl.pallas_call(
        functools.partial(backward_kernel, length),
        out_shape=(
            shape((2, blocks, units, columns), bf16),
            shape((2, VOCAB_PAD, columns), f32),
            shape((streams, rows, units), f32),
            shape((streams, rows, units), f32),
            shape((2, units // seqs, VOCAB_PAD), f32),
        ),
        in_specs=[vmem] * 4 + [any_space] * 4,
        out_specs=(any_space,) + (vmem,) * 4,
        scratch_shapes=[
            pltpu.VMEM((2, blocks, units, columns), bf16),
            pltpu.VMEM((2, blocks, units, columns), f32),
            pltpu.VMEM((streams, 5, rows, units), f32),
            pltpu.VMEM((streams, rows, VOCAB_PAD), bf16),
            pltpu.VMEM((streams, blocks, rows, units), bf16),
            pltpu.VMEM((streams, rows, columns), bf16),
            pltpu.VMEM((streams, rows, units), f32),
            pltpu.VMEM((streams, rows, units), f32),
            pltpu.VMEM((streams, 4, rows, units), bf16),
            pltpu.VMEM((streams, 2, 4, rows, units), bf16),
            pltpu.VMEM((streams, 3, rows, units), bf16),
            pltpu.VMEM((streams, 2, 2, rows, units), bf16),
            pltpu.VMEM((streams, 2, rows // 2, units), f32),
            pltpu.VMEM((streams, 2, 2, rows // 2, units), bf16),
            pltpu.VMEM((2, units, VOCAB_PAD), bf16),
            pltpu.VMEM((seqs, 2, units // seqs, VOCAB_PAD), bf16),
            pltpu.VMEM((seqs - 1, 2, units // seqs, VOCAB_PAD), bf16),
            dma,
            dma((streams,)),
            dma((streams,)),
            dma((streams,)),
            dma((streams, 4)),
            dma((streams, 2, 4)),
            dma((streams, 2, 2)),
            dma((streams, 2, 2, 2)),
            dma((streams, 2)),
            dma((streams, 2, 2)),
            dma((seqs - 1,)),
            dma((seqs - 1,)),
            dma((blocks,)),
        ],
        compiler_params=pltpu.CompilerParams(
            collective_id=1, has_side_effects=True, vmem_limit_bytes=VMEM_LIMIT
        ),
        name="backward_visits",
    )(info, slot_ids, w_dec, dec_grad, acts, grads, wholes, w_grouped)
    rec_part, edge_part, small = kernel_sums(
        rec_grad, letter_grad, embed, w_in_grouped, (loss, logit_sq, hidden_sq, dec_bias)
    )
    outs = (
        shape((1, 1), f32),
        shape(h_init.shape, f32),
        shape(h_init.shape, f32),
        shape(embed.shape, f32),
        shape((2, width, columns // seqs), f32),
        shape((2, w_rec.shape[1] // seqs, columns), f32),
        shape((2, columns // seqs), f32),
        shape((2, units // seqs, letters), f32),
        shape((2, letters), f32),
        shape((1, 2), f32),
        shape((1, 2), f32),
        shape((1, 2), f32),
    )
    tile = rec_part.shape[2]
    parts = rec_part.shape[1]
    results = pl.pallas_call(
        functools.partial(finish_kernel, w_rec.shape[1]),
        grid=(2, parts),
        out_shape=outs,
        in_specs=[vmem] * 7 + [pl.BlockSpec((1, 1, tile, columns), lambda d, r: (d, r, 0, 0))],
        out_specs=tuple(
            pl.BlockSpec((1, tile, columns), lambda d, r: (d, r, 0)) if n == 5 else vmem for n in range(len(outs))
        ),
        scratch_shapes=[pltpu.VMEM((4 * LANES, 4 * LANES), bf16)],
        compiler_params=pltpu.CompilerParams(
            dimension_semantics=("arbitrary", "arbitrary"), vmem_limit_bytes=VMEM_LIMIT
        ),
        name="results",
    )(lengths[None], embed, edge_part, dec_part, small, hidden_grad, cell_grad, rec_part)
    scalar = (0, 9, 10, 11)
    return tuple(
        x.reshape(()) if n == 0 else x.reshape(2) if n in scalar else x for n, x in enumerate(results)
    )


def finish_kernel(
    all_units, lens, embed, edge, dec, small, hidden_in, cell_in, rec,
    loss, hidden_grad, cell_grad, embed_grad, in_grad, rec_grad, bias_grad, dec_grad, dec_bias, rms_embed, rms_hidden,
    rms_logits, matrix,
):
    first = (pl.program_id(0) == 0) & (pl.program_id(1) == 0)
    letters, width = embed.shape[1:]
    span = matrix.shape[0]

    @pl.when(first)
    def _():
        matrix[...] = regroup_matrix(span)
        hidden_grad[...] = hidden_in[...]
        cell_grad[...] = cell_in[...]
        live = jnp.sum(lens[...].astype(jnp.float32), axis=1, keepdims=True)
        count = 2.0 * (live - lens.shape[1])
        at = 2 * TABLE
        loss[...] = small[at:at + 1, :1] / count
        for d in range(2):
            embed_grad[d] = small[d * TABLE:d * TABLE + letters, :width]
            in_grad[d] = edge[d, :width]
            bias_grad[d:d + 1] = edge[d, width:width + 1]
            dec_grad[d] = dec[d, :, :letters]
            for n in range(VOCAB_PAD // LANES):
                row = at + 5 + d * (VOCAB_PAD // LANES) + n
                last = min(LANES, letters - n * LANES)
                dec_bias[d:d + 1, n * LANES:n * LANES + last] = small[row:row + 1, :last]
            table = embed[d].astype(jnp.float32)
            square = jnp.sum(jnp.sum(table * table, axis=1, keepdims=True), axis=0, keepdims=True)
            rms_embed[:, d:d + 1] = jnp.sqrt(square / (letters * width))
            logit_sq = jnp.sum(small[at + 1 + d:at + 2 + d], axis=1, keepdims=True)
            hidden_sq = jnp.sum(small[at + 3 + d:at + 4 + d], axis=1, keepdims=True)
            rms_hidden[:, d:d + 1] = jnp.sqrt(hidden_sq / (all_units * live))
            rms_logits[:, d:d + 1] = jnp.sqrt(logit_sq / (letters * count / 2.0))

    for g in range(rec.shape[-1] // span):
        columns = slice(g * span, (g + 1) * span)
        rec_grad[0, :, columns] = matmul(rec[0, 0, :, columns], matrix[...], NT)


PIECE = 128
LAG = 3
WINDOW = 3
TABLE = 280


def spread(letter_grad, other, dims):
    high = letter_grad.astype(jnp.bfloat16)
    low = (letter_grad - high.astype(jnp.float32)).astype(jnp.bfloat16)
    return matmul(high, other, dims) + matmul(low, other, dims)


def reduce_kernel(
    rec_hbm, letter_grad, embed_in, w_in, loss, logit_sq, hidden_sq, dec_bias,
    rec_out, edge_out, small_out,
    own, ahead, behind, edge, edge_in, small, part, small_in, part_in, summed, matrix, embed,
    load_sem, line_send, line_recv, back_send, back_recv, edge_send, edge_recv,
    scatter_send, scatter_recv, seq_send, seq_recv, gather_send, gather_recv,
):
    seq, me = lax.axis_index("seq"), lax.axis_index("mp")
    count, parts = own.shape[1], own.shape[2]
    peers = lax.axis_size("mp")
    share = small.shape[0] // peers
    half = seq // (count // 2)
    place = seq + half * (count - 1 - 2 * seq)
    onward = 1 - 2 * half
    inner = count // 2 - 1
    lag = LAG + (inner - place) * 5
    load = pltpu.make_async_copy(rec_hbm, own, load_sem)
    load.start()

    def other_seq(n):
        return (seq + n) % count

    def other_mp(n):
        return (me + n) % peers

    barrier = pltpu.get_barrier_semaphore()
    for n in range(1, count):
        pl.semaphore_signal(barrier, inc=1, device_id=(other_seq(n), me), device_id_type=MESH)
    for n in range(1, peers):
        pl.semaphore_signal(barrier, inc=1, device_id=(seq, other_mp(n)), device_id_type=MESH)
    pl.semaphore_wait(barrier, count + peers - 2)
    load.wait()

    def send(src, dst, send_sem, recv_sem, seq_to, mp_to):
        return pltpu.make_async_remote_copy(
            src_ref=src, dst_ref=dst, send_sem=send_sem, recv_sem=recv_sem,
            device_id=(seq_to, mp_to), device_id_type=MESH,
        )

    def actual(chunk):
        return chunk + half * (count - 1 - 2 * chunk)

    pieces = 2 * parts

    def slot(k):
        return k // pieces, (k % pieces) // parts, k % parts

    def piece(chunk, d, r):
        return own.at[d, actual(chunk), r]

    def line_copy(k, crossing):
        i, d, r = slot(k)
        target = behind.at[i, d, r] if crossing else ahead.at[i, d, r]
        sem = back_recv.at[i, d, r] if crossing else line_recv.at[i, d, r]
        return send(piece(count - 1 - i, d, r), target, line_send.at[i, d, r], sem, seq + onward, me)

    def back_copy(k):
        i, d, r = slot(k)
        return send(
            piece(i, d, r), behind.at[i, d, r], back_send.at[i, d, r], back_recv.at[i, d, r], seq - onward, me
        )

    def add(chunk, d, r, term):
        ref = piece(chunk, d, r)
        ref[...] = (ref[...].astype(jnp.float32) + term[...].astype(jnp.float32)).astype(jnp.bfloat16)

    def line(k):
        i, d, r = slot(k)

        @pl.when((place > 0) & (i <= count - 1 - place))
        def _():
            line_copy(k, False).wait_recv()
            add(count - 1 - i, d, r, ahead.at[i, d, r])

        @pl.when((place == 0) & (k >= WINDOW))
        def _():
            line_copy(k - WINDOW, False).wait_send()

        @pl.when((i <= count - 2 - place) & (place < inner))
        def _():
            line_copy(k, False).start()

        @pl.when((i <= count - 2 - place) & (place == inner))
        def _():
            line_copy(k, True).start()

    def back(k):
        i, d, r = slot(k)

        @pl.when(i <= place)
        def _():
            back_copy(k).wait_recv()
            add(i, d, r, behind.at[i, d, r])

        @pl.when(i < place)
        def _():
            back_copy(k).start()

    def advance(k, carry):
        @pl.when(k < (count - 1) * pieces)
        def _():
            line(k)

        @pl.when((k >= lag) & (k - lag < (count // 2) * pieces))
        def _():
            back(k - lag)

        return carry

    def edge_copy(n):
        to = other_seq(n)
        return send(edge.at[to], edge_in.at[n - 1], edge_send.at[n - 1], edge_recv.at[n - 1], to, me)

    def scatter_copy(n):
        to = other_mp(n)
        rows = pl.ds(pl.multiple_of(to * share, 8), share)
        return send(small.at[rows], small_in.at[n - 1], scatter_send.at[n - 1], scatter_recv.at[n - 1], seq, to)

    def seq_copy(n):
        return send(part, part_in.at[n - 1], seq_send.at[n - 1], seq_recv.at[n - 1], other_seq(n), me)

    own_rows = pl.ds(pl.multiple_of(me * share, 8), share)

    def gather_copy(n):
        return send(
            summed.at[own_rows], summed.at[own_rows], gather_send.at[n - 1], gather_recv.at[me], seq, other_mp(n)
        )

    def gather_arrival(n):
        source = other_mp(n)
        rows = pl.ds(pl.multiple_of(source * share, 8), share)
        return send(summed.at[rows], summed.at[rows], gather_send.at[n - 1], gather_recv.at[source], seq, source)

    start = 6
    lax.fori_loop(0, 2, advance, 0)
    matrix[...] = regroup_matrix(matrix.shape[0])
    letters, width = embed_in.shape[1:]
    lanes = lax.broadcasted_iota(jnp.int32, (letters, LANES), 1)
    padded(embed, embed_in)
    for d in range(2):
        embed[d, :letters] = jnp.where(lanes == width, 1.0, embed[d, :letters].astype(jnp.float32)).astype(jnp.bfloat16)
    first = jnp.where(me == 0, 1.0, 0.0)
    for d in range(2):
        small[d * TABLE:(d + 1) * TABLE] = spread(letter_grad[d], w_in[d], NT)[:TABLE]
    small[2 * TABLE:] = jnp.zeros((small.shape[0] - 2 * TABLE, LANES), jnp.float32)
    at = 2 * TABLE
    small[at:at + 1] = jnp.sum(loss[0] + loss[1], axis=0, keepdims=True) * first
    for d in range(2):
        small[at + 1 + d:at + 2 + d] = jnp.sum(logit_sq[d], axis=0, keepdims=True) * first
        small[at + 3 + d:at + 4 + d] = jnp.sum(hidden_sq[d], axis=0, keepdims=True)
        row = jnp.sum(dec_bias[d], axis=0, keepdims=True) * first
        for n in range(VOCAB_PAD // LANES):
            line_at = at + 5 + d * (VOCAB_PAD // LANES) + n
            small[line_at:line_at + 1] = row[:, n * LANES:(n + 1) * LANES]
    for n in range(1, peers):
        scatter_copy(n).start()
    rows = edge.shape[2]
    span = matrix.shape[0]
    wide = own.shape[-1] // count
    for d in range(2):
        full = spread_left(embed[d], letter_grad[d]).astype(jnp.bfloat16)
        flat = [
            matmul(full[:, g * span:(g + 1) * span], matrix[...], NT).astype(jnp.bfloat16)
            for g in range(own.shape[-1] // span)
        ]
        for q in range(count):
            group, offset = (q * wide) // span, (q * wide) % span
            edge[q, d] = flat[group][:rows, offset:offset + wide]
    for n in range(1, count):
        edge_copy(n).start()
    lax.fori_loop(2, start, advance, 0)
    for n in range(1, peers):
        scatter_copy(n).wait()
    total = small[own_rows, :]
    for n in range(1, peers):
        total += small_in[n - 1]
    part[...] = total
    for n in range(1, count):
        seq_copy(n).start()
    lax.fori_loop(start, 2 * start, advance, 0)
    for n in range(1, count):
        seq_copy(n).wait()
        total += part_in[n - 1]
    summed[own_rows, :] = total
    for n in range(1, peers):
        gather_copy(n).start()
    lax.fori_loop(2 * start, (count - 1) * pieces + LAG, advance, 0)
    for n in range(1, peers):
        gather_copy(n).wait_send()
        gather_arrival(n).wait_recv()
    small_out[...] = summed[...]
    for n in range(1, count):
        edge_copy(n).wait()
    for d in range(2):
        edge_out[d] = edge[seq, d].astype(jnp.float32) + sum(
            edge_in[n, d].astype(jnp.float32) for n in range(count - 1)
        )
        rec_out[d] = own[d, seq]

    def finish(k, carry):
        i, d, r = slot(k)

        @pl.when((i <= count - 2 - place) & ((place > 0) | (k >= (count - 1) * pieces - WINDOW)))
        def _():
            line_copy(k, False).wait_send()

        @pl.when((i < place) & (k < (count // 2) * pieces))
        def _():
            back_copy(k).wait_send()

        return carry

    lax.fori_loop(0, (count - 1) * pieces, finish, 0)


def spread_left(other, letter_grad):
    high = letter_grad.astype(jnp.bfloat16)
    low = (letter_grad - high.astype(jnp.float32)).astype(jnp.bfloat16)
    return matmul(other, high, TN) + matmul(other, low, TN)


def kernel_sums(rec_grad, letter_grad, embed, w_in_grouped, stats):
    count = lax.axis_size("seq")
    peers = lax.axis_size("mp")
    columns = rec_grad.shape[-1]
    all_rows = rec_grad.shape[1] * rec_grad.shape[2]
    parts = all_rows // count // PIECE
    width = embed.shape[2]
    edge_rows = -(-(width + 1) // 8) * 8
    small_rows = -(-(2 * TABLE + 16) // (8 * peers)) * 8 * peers
    share = small_rows // peers
    f32, bf16 = jnp.float32, jnp.bfloat16
    dma = pltpu.SemaphoreType.DMA
    shape = jax.ShapeDtypeStruct
    vmem = pl.BlockSpec(memory_space=pltpu.VMEM)
    return pl.pallas_call(
        reduce_kernel,
        out_shape=(
            shape((2, parts, PIECE, columns), bf16),
            shape((2, edge_rows, columns // count), f32),
            shape((small_rows, LANES), f32),
        ),
        in_specs=[pl.BlockSpec(memory_space=pl.ANY)] + [vmem] * 7,
        out_specs=(vmem,) * 3,
        scratch_shapes=[
            pltpu.VMEM((2, count, parts, PIECE, columns), bf16),
            pltpu.VMEM((count - 1, 2, parts, PIECE, columns), bf16),
            pltpu.VMEM((count // 2, 2, parts, PIECE, columns), bf16),
            pltpu.VMEM((count, 2, edge_rows, columns // count), bf16),
            pltpu.VMEM((count - 1, 2, edge_rows, columns // count), bf16),
            pltpu.VMEM((small_rows, LANES), f32),
            pltpu.VMEM((share, LANES), f32),
            pltpu.VMEM((peers - 1, share, LANES), f32),
            pltpu.VMEM((count - 1, share, LANES), f32),
            pltpu.VMEM((small_rows, LANES), f32),
            pltpu.VMEM((4 * LANES, 4 * LANES), bf16),
            pltpu.VMEM((2, VOCAB_PAD, LANES), bf16),
            dma,
            dma((count - 1, 2, parts)),
            dma((count - 1, 2, parts)),
            dma((count // 2, 2, parts)),
            dma((count // 2, 2, parts)),
            dma((count - 1,)),
            dma((count - 1,)),
            dma((peers - 1,)),
            dma((peers - 1,)),
            dma((count - 1,)),
            dma((count - 1,)),
            dma((peers - 1,)),
            dma((peers,)),
        ],
        compiler_params=pltpu.CompilerParams(
            collective_id=2, has_side_effects=True, vmem_limit_bytes=VMEM_LIMIT
        ),
        name="gradient_sums",
    )(
        rec_grad.reshape(2, count, parts, PIECE, columns), letter_grad, embed, w_in_grouped, *stats,
    )


def plain_step(ids, lengths, order, count, h_init, c_init, embed, w_in, w_rec, bias, w_dec, b_dec, matrix):
    first_mp = (lax.axis_index("mp") == 0).astype(jnp.float32)
    per_dev, own_units = h_init.shape[1:]
    lanes = matrix.shape[0] // 4
    wd_full = lax.all_gather(w_dec, "mp", axis=1, tiled=True)
    whole_ids = lax.all_gather(ids, "seq", axis=0, tiled=True)
    own_order = lax.dynamic_slice_in_dim(order, lax.axis_index("seq") * per_dev, per_dev)
    slot_ids = jnp.take(whole_ids, own_order, axis=1)
    own_len = jnp.take(lengths, own_order)
    step_ids = jnp.stack([slot_ids, jnp.flip(slot_ids, 0)])
    w_rec_grouped = grouped(w_rec, matrix)
    w_in_grouped = grouped(w_in, matrix)
    bias_grouped = jnp.swapaxes(
        bias.reshape(2, own_units // lanes, lanes, 4), -1, -2
    ).reshape(bias.shape)
    loss, hidden_sq, logit_sq, dec_bias, dec_grad, hidden_grad, cell_grad, rec_grad, letter_grad = recurrences(
        step_ids, own_len, h_init, c_init, embed, w_in_grouped, w_rec_grouped, bias_grouped, w_dec, wd_full,
        b_dec, count, lanes,
    )
    embed_wide = embed.astype(jnp.float32)
    in_grad = jnp.einsum("dve,dvc->dec", embed_wide, letter_grad, precision=lax.Precision.HIGHEST)
    bias_grad = jnp.sum(letter_grad, axis=1, keepdims=True)
    embed_part = jnp.einsum(
        "dvc,dec->dve", letter_grad, w_in_grouped.astype(jnp.float32), precision=lax.Precision.HIGHEST
    )
    edge = ungrouped_wide(jnp.concatenate([in_grad, bias_grad], axis=1), lanes)
    rec_part = lax.psum_scatter(rec_grad.astype(jnp.bfloat16), "seq", scatter_dimension=1, tiled=True)
    edge_part = lax.psum_scatter(edge.astype(jnp.bfloat16), "seq", scatter_dimension=2, tiled=True)
    dec_part = lax.psum_scatter(dec_grad.astype(jnp.bfloat16), "seq", scatter_dimension=1, tiled=True)
    loss_sum, hidden_all, logit_all, dec_bias_grad, embed_grad = lax.psum(
        (loss * first_mp, hidden_sq, logit_sq * first_mp, dec_bias * first_mp, embed_part), ("seq", "mp")
    )
    rec_out = ungrouped(rec_part, matrix).astype(jnp.float32)
    return (
        loss_sum, hidden_all, logit_all, dec_bias_grad, dec_part.astype(jnp.float32), hidden_grad, cell_grad, rec_out,
        edge_part[:, :-1].astype(jnp.float32), edge_part[:, -1].astype(jnp.float32), embed_grad,
    )


def per_device(ids, lengths, order, h_init, c_init, embed, w_in, w_rec, bias, w_dec, b_dec):
    streams = ids.shape[1]
    per_dev, own_units = h_init.shape[1:]
    all_units, letter_count = w_rec.shape[1], embed.shape[1]
    fits = own_units % LANES == 0 and per_dev % LANES == 0 and per_dev <= 256 and own_units <= 256
    fits = fits and all_units % (lax.axis_size("seq") * PIECE) == 0 and letter_count <= TABLE
    if lax.axis_size("mp") == 8 and lax.axis_size("seq") == 4 and fits and embed.shape[2] < LANES:
        return kernel_step(ids, lengths, order, h_init, c_init, embed, w_in, w_rec, bias, w_dec, b_dec)
    live_total = jnp.sum(lengths).astype(jnp.float32)
    count = 2.0 * (jnp.sum(lengths) - streams).astype(jnp.float32)
    _, matrix = column_order(own_units)
    (
        loss_sum, hidden_all, logit_all, dec_bias_grad, dec_part, hidden_grad, cell_grad, rec_out, in_out, bias_out,
        embed_grad,
    ) = plain_step(ids, lengths, order, count, h_init, c_init, embed, w_in, w_rec, bias, w_dec, b_dec, matrix)
    embed_wide = embed.astype(jnp.float32)
    rms_embed = jnp.sqrt(jnp.mean(embed_wide * embed_wide, axis=(1, 2)))
    return (
        loss_sum / count,
        hidden_grad,
        cell_grad,
        embed_grad,
        in_out,
        rec_out,
        bias_out,
        dec_part,
        dec_bias_grad,
        rms_embed,
        jnp.sqrt(hidden_all / (all_units * live_total)),
        jnp.sqrt(logit_all / (letter_count * count / 2.0)),
    )


def solution(mesh):
    in_specs = (
        P("seq", None),
        P(),
        P(),
        P(None, "seq", "mp"),
        P(None, "seq", "mp"),
        P(),
        P(None, None, "mp"),
        P(None, None, "mp"),
        P(None, "mp"),
        P(None, "mp", None),
        P(),
    )
    out_specs = (
        P(),
        P(None, "seq", "mp"),
        P(None, "seq", "mp"),
        P(),
        P(None, None, ("mp", "seq")),
        P(None, "seq", "mp"),
        P(None, ("mp", "seq")),
        P(None, ("mp", "seq"), None),
        P(),
        P(),
        P(),
        P(),
    )
    return jax.shard_map(
        per_device, mesh=mesh, in_specs=in_specs, out_specs=out_specs, check_vma=False
    )
```

```python
import functools

import jax
import jax.numpy as jnp
from jax import lax
from jax.experimental import pallas as pl
from jax.experimental.pallas import tpu as pltpu
from jax.sharding import PartitionSpec as P

VMEM_LIMIT = 58 * 2**20


def column_order(own_units):
    lanes = min(128, own_units)
    source = jnp.arange(4 * lanes, dtype=jnp.int32)
    place = (source % 4) * lanes + source // 4
    matrix = (place[:, None] == jnp.arange(4 * lanes, dtype=jnp.int32)[None, :]).astype(jnp.bfloat16)
    return lanes, matrix


def grouped(x, matrix):
    width = matrix.shape[0]
    parts = x.reshape(x.shape[:-1] + (x.shape[-1] // width, width))
    out = jnp.einsum("...gc,cp->...gp", parts, matrix, preferred_element_type=jnp.float32)
    return out.astype(x.dtype).reshape(x.shape)


def ungrouped(x, matrix):
    return grouped(x, matrix.T)


def ungrouped_wide(x, lanes):
    parts = x.reshape(x.shape[:-1] + (x.shape[-1] // (4 * lanes), 4, lanes))
    return jnp.swapaxes(parts, -1, -2).reshape(x.shape)


def gates_of(pre, lanes):
    parts = pre.reshape(pre.shape[:-1] + (pre.shape[-1] // (4 * lanes), 4, lanes))
    flat = pre.shape[:-1] + (pre.shape[-1] // 4,)
    return tuple(parts[..., k, :].reshape(flat) for k in range(4))


def joined_gates(gates, lanes):
    split = [g.reshape(g.shape[:-1] + (g.shape[-1] // lanes, 1, lanes)) for g in gates]
    joined = jnp.concatenate(split, axis=-2)
    return joined.reshape(gates[0].shape[:-1] + (4 * gates[0].shape[-1],))


def recurrences(step_ids, own_len, h_init, c_init, embed, w_in, w_rec, bias, w_dec, wd_full, b_dec, count, lanes):
    length, per_dev = step_ids.shape[1:]
    letter_count = embed.shape[1]
    steps = jnp.arange(length, dtype=jnp.int32)
    live_steps = jnp.stack(
        [steps[:, None] < own_len[None, :], (length - 1 - steps)[:, None] < own_len[None, :]], axis=1
    )[..., None]
    letters = jnp.arange(letter_count, dtype=jnp.int32)
    onehot = (jnp.swapaxes(step_ids, 0, 1)[..., None] == letters).astype(jnp.bfloat16)
    letter_rows = jnp.einsum(
        "sdbv,dve->sdbe", onehot, embed, preferred_element_type=jnp.float32
    ).astype(jnp.bfloat16)
    gates_in = jnp.einsum(
        "sdbe,dec->sdbc", letter_rows, w_in, preferred_element_type=jnp.float32
    ).astype(jnp.bfloat16)

    def forward_step(carry, inputs):
        hidden, cell = carry
        gate_in, live = inputs
        whole = lax.all_gather(hidden, "mp", axis=2, tiled=True)
        recurrent = jnp.einsum("dbh,dhc->dbc", whole, w_rec, preferred_element_type=jnp.float32)
        pre = gate_in.astype(jnp.float32) + recurrent + bias[:, None]
        in_pre, forget_pre, cell_pre, out_pre = gates_of(pre, lanes)
        in_gate, forget, out_gate = (jax.nn.sigmoid(x) for x in (in_pre, forget_pre, out_pre))
        cell_gate = jnp.tanh(cell_pre)
        new_cell = forget * cell + in_gate * cell_gate
        cell_next = jnp.where(live, new_cell, cell)
        hidden_next = jnp.where(
            live, out_gate * jnp.tanh(new_cell), hidden.astype(jnp.float32)
        ).astype(jnp.bfloat16)
        return ((hidden_next, cell_next), (whole, cell, in_gate, forget, cell_gate, out_gate))

    (last_hidden, last_cell), (wholes, cells, *gates) = lax.scan(
        forward_step, (h_init, c_init), (gates_in, live_steps)
    )
    last_whole = lax.all_gather(last_hidden, "mp", axis=2, tiled=True)
    after = jnp.concatenate([wholes[1:], last_whole[None]], axis=0)
    own = h_init.shape[2]
    mine = lax.dynamic_slice_in_dim(after, lax.axis_index("mp") * own, own, axis=3)
    mine_wide = mine.astype(jnp.float32)
    hidden_sq = jnp.sum(jnp.where(live_steps, mine_wide * mine_wide, 0.0), axis=(0, 2, 3))
    logits = (
        jnp.einsum("sdbh,dhv->sdbv", after, wd_full, preferred_element_type=jnp.float32) + b_dec[None, :, None]
    )
    targets = jnp.swapaxes(jnp.concatenate([step_ids[:, 1:], step_ids[:, :1]], axis=1), 0, 1)
    fore_valid = (steps[:, None] + 1 < own_len[None, :])
    back_valid = (steps[:, None] < length - 1) & ((length - 1 - steps)[:, None] < own_len[None, :])
    valid = jnp.stack([fore_valid, back_valid], axis=1).astype(jnp.float32)
    logit_sq = jnp.sum(valid[..., None] * logits * logits, axis=(0, 2, 3))
    top = jnp.max(logits, axis=-1, keepdims=True)
    log_total = top + jnp.log(jnp.sum(jnp.exp(logits - top), axis=-1, keepdims=True))
    target_hot = targets[..., None] == letters
    picked = jnp.sum(jnp.where(target_hot, logits, 0.0), axis=-1)
    loss = jnp.sum(valid * (log_total[..., 0] - picked))
    grad_logits = (
        valid[..., None] * (jnp.exp(logits - log_total) - target_hot.astype(jnp.float32)) / count
    ).astype(jnp.bfloat16)
    dec_bias = jnp.sum(grad_logits.astype(jnp.float32), axis=(0, 2))
    dec_grad = jnp.einsum("sdbh,sdbv->dhv", mine, grad_logits, preferred_element_type=jnp.float32)

    def backward_step(carry, inputs):
        grad_hidden, grad_cell = carry
        live, cell, in_gate, forget, cell_gate, out_gate, grad_logit = inputs
        grad_hidden = grad_hidden + jnp.einsum(
            "dbv,dhv->dbh", grad_logit, w_dec, preferred_element_type=jnp.float32
        )
        squash = jnp.tanh(forget * cell + in_gate * cell_gate)
        grad_new = jnp.where(live, grad_cell + grad_hidden * out_gate * (1.0 - squash * squash), 0.0)
        grad_out = jnp.where(live, grad_hidden * squash, 0.0)
        grad_pre = joined_gates(
            [
                grad_new * cell_gate * in_gate * (1.0 - in_gate),
                grad_new * cell * forget * (1.0 - forget),
                grad_new * in_gate * (1.0 - cell_gate * cell_gate),
                grad_out * out_gate * (1.0 - out_gate),
            ],
            lanes,
        ).astype(jnp.bfloat16)
        grad_cell_prev = grad_new * forget + jnp.where(live, 0.0, grad_cell)
        held = jnp.where(live, 0.0, grad_hidden)
        terms = jnp.einsum("dbc,dhc->dbh", grad_pre, w_rec, preferred_element_type=jnp.float32)
        through = lax.psum_scatter(
            terms.astype(jnp.bfloat16), "mp", scatter_dimension=2, tiled=True
        ).astype(jnp.float32)
        return ((held + through, grad_cell_prev), grad_pre)

    start = jnp.zeros(c_init.shape, jnp.float32)
    (hidden_grad, cell_grad), grad_pres = lax.scan(
        backward_step, (start, start), (live_steps, cells, *gates, grad_logits), reverse=True
    )
    rec_grad = jnp.einsum("sdbh,sdbc->dhc", wholes, grad_pres, preferred_element_type=jnp.float32)
    letter_grad = jnp.einsum("sdbv,sdbc->dvc", onehot, grad_pres, preferred_element_type=jnp.float32)
    return loss, hidden_sq, logit_sq, dec_bias, dec_grad, hidden_grad, cell_grad, rec_grad, letter_grad


MESH = pl.DeviceIdType.MESH
LANES = 128
VOCAB_PAD = 384
NT = (((1,), (1,)), ((), ()))
TN = (((0,), (0,)), ((), ()))


def sigmoid(x):
    return 0.5 * jnp.tanh(0.5 * x) + 0.5


def matmul(left, right, dims=(((1,), (0,)), ((), ()))):
    return lax.dot_general(left, right, dims, preferred_element_type=jnp.float32)


def neighbours():
    me = lax.axis_index("mp")
    row, column, core = me // 4, (me // 2) % 2, me % 2
    sibling = row * 4 + column * 2 + (1 - core)
    across = (1 - row) * 4 + (1 - column) * 2 + core
    side = row * 4 + (1 - column) * 2 + core
    up = (1 - row) * 4 + column * 2 + core
    return me, sibling, (across, side, up)


def greet(peers, seqs=0):
    seq, me = lax.axis_index("seq"), lax.axis_index("mp")
    barrier = pltpu.get_barrier_semaphore()
    for peer in peers:
        pl.semaphore_signal(barrier, inc=1, device_id=(seq, peer), device_id_type=MESH)
    for n in range(1, seqs):
        pl.semaphore_signal(barrier, inc=1, device_id=((seq + n) % seqs, me), device_id_type=MESH)
    pl.semaphore_wait(barrier, len(peers) + max(seqs - 1, 0))


def remote(src, dst, send, recv, peer):
    return pltpu.make_async_remote_copy(
        src_ref=src, dst_ref=dst, send_sem=send, recv_sem=recv,
        device_id=(lax.axis_index("seq"), peer), device_id_type=MESH,
    )


def other_core(peer):
    return (peer // 2) * 2 + (1 - peer % 2)


def folded(x):
    return jnp.sum(x.reshape(x.shape[0] // 8, 8, x.shape[1]), axis=0)


def regroup_matrix(span):
    source = lax.broadcasted_iota(jnp.int32, (span, span), 0)
    place = (source & 3) * (span // 4) + (source >> 2)
    return (place == lax.broadcasted_iota(jnp.int32, (span, span), 1)).astype(jnp.bfloat16)


def padded(ref, value):
    ref[...] = jnp.zeros(ref.shape, ref.dtype)
    for d in range(2):
        ref[d, :value.shape[1], :value.shape[2]] = value[d]


def column_of(table, lane):
    lanes = lax.broadcasted_iota(jnp.int32, table.shape, 1)
    return jnp.sum(jnp.where(lanes == lane, table, 0.0), axis=1, keepdims=True)


def time_of(direction, step, length):
    return step if direction == 0 else length - 1 - step


def forward_kernel(
    length, letters, ids_in, lens, order, h_in, c_in, embed_in, w_in_raw, bias, b_dec_in, w_dec_in, w_hbm,
    wholes, acts, grads, w_out, loss, logit_sq, hidden_sq, dec_bias, dec_grad, info, ids, w_in,
    w, wd, buf, cell, acc, logit, stage, grad, all_ids, table, matrix, embed, b_dec, inverse, load_sem, ids_send, ids_recv, wd_send, wd_recv, wd_plane_send,
    wd_core_recv, send_sem, recv_sem, save_sem, act_sem, grad_sem,
):
    me, sibling, peers = neighbours()
    seq, seqs, times = lax.axis_index("seq"), all_ids.shape[0], ids_in.shape[0]
    blocks, rows, units = buf.shape[2:]
    groups, span = units // LANES, matrix.shape[0]
    columns = w.shape[-1]
    load_w = pltpu.make_async_copy(w_hbm, w, load_sem.at[0])
    store_w = pltpu.make_async_copy(w, w_out, load_sem.at[1])
    load_w.start()
    all_ids[seq, :times] = ids_in[...].astype(jnp.float32)
    matrix[...] = regroup_matrix(span)
    for s in range(2):
        buf[s, 0, me] = h_in[s]
    greet((sibling,) + peers, seqs)

    def ids_copy(n):
        to = (seq + n) % seqs
        block = all_ids.at[seq]
        return pltpu.make_async_remote_copy(
            src_ref=block, dst_ref=block, send_sem=ids_send.at[n - 1], recv_sem=ids_recv.at[seq],
            device_id=(to, me), device_id_type=MESH,
        )

    def ids_arrival(n):
        source = (seq + n) % seqs
        block = all_ids.at[source]
        return pltpu.make_async_remote_copy(
            src_ref=block, dst_ref=block, send_sem=ids_send.at[n - 1], recv_sem=ids_recv.at[source],
            device_id=(source, me), device_id_type=MESH,
        )

    across, side, up = peers
    depth = rows // 2

    def transfer(s, step, block, h, index, peer):
        slot, par = step % 3, step % 2
        ref = buf.at[s, slot, block, h * depth:(h + 1) * depth]
        return remote(ref, ref, send_sem.at[s, par, index], recv_sem.at[s, slot, block, h], peer)

    def transfer_whole(s, step, block, index):
        slot, par = step % 3, step % 2
        ref = buf.at[s, slot, block]
        return remote(ref, ref, send_sem.at[s, par, index], recv_sem.at[s, slot, block, 0], sibling)

    def direct(s, step):
        plan = ((0, side), (1, up), (1, side), (0, up))
        return [transfer(s, step, me, h, n, peer) for n, (h, peer) in enumerate(plan)]

    def pass_on(s, step):
        for n, (block, h, peer) in enumerate(((side, 0, up), (up, 1, side))):
            transfer(s, step, block, h, 0, sibling).wait_recv()
            transfer(s, step, block, h, 4 + n, peer).start()

    def core_copies(s, step):
        return [transfer_whole(s, step, block, 6 + n) for n, block in enumerate((me, side, up, across))]

    share = units // seqs

    def wd_rows(source, quarter):
        return wd.at[source, :, pl.ds(pl.multiple_of(quarter * share, 16), share)]

    def wd_copy(n):
        ref = wd_rows(me, seq)
        return remote(ref, ref, wd_send.at[n], wd_recv.at[me, seq], peers[n])

    def wd_across(n, k):
        ref = wd_rows(peers[n], seq)
        return pltpu.make_async_remote_copy(
            src_ref=ref, dst_ref=ref, send_sem=wd_plane_send.at[n, k - 1], recv_sem=wd_recv.at[peers[n], seq],
            device_id=((seq + k) % seqs, me), device_id_type=MESH,
        )

    def wd_arrival(n, k):
        ref = wd_rows(peers[n], (seq + k) % seqs)
        return remote(ref, ref, wd_send.at[0], wd_recv.at[peers[n], (seq + k) % seqs], sibling)

    def wd_core(n, block):
        return remote(wd.at[block], wd.at[block], wd_send.at[3 + n], wd_core_recv.at[block], sibling)

    def save(s, step):
        return pltpu.make_async_copy(buf.at[s, step % 3], wholes.at[step, s], save_sem.at[s, step % 2])

    def save_acts(s, step):
        return pltpu.make_async_copy(stage.at[s], acts.at[step, s], act_sem.at[s])

    def save_grad(s, step):
        return pltpu.make_async_copy(grad.at[s], grads.at[step, s], grad_sem.at[s])

    def finish_sends(s, step):
        for copy in direct(s, step) + core_copies(s, step):
            copy.wait_send()
        for n, (block, h, peer) in enumerate(((side, 0, up), (up, 1, side))):
            transfer(s, step, block, h, 4 + n, peer).wait_send()

    for n in range(1, seqs):
        ids_copy(n).start()
    for s in range(2):
        for copy in direct(s, 0):
            copy.start()
        transfer_whole(s, 0, me, 6).start()
    padded(wd.at[me], w_dec_in)
    for n in range(3):
        wd_copy(n).start()
    wd_core(3, me).start()
    padded(embed, embed_in)
    padded(w_in, w_in_raw)
    b_dec[...] = jnp.full(b_dec.shape, -1e30, jnp.float32)
    for d in range(2):
        b_dec[d, :, :letters] = b_dec_in[d:d + 1]
    lengths = lens[...].astype(jnp.float32)
    inverse[...] = 0.5 / (jnp.sum(lengths, axis=1, keepdims=True) - lens.shape[1])
    for ref in (loss, logit_sq, hidden_sq, dec_bias, dec_grad):
        ref[...] = jnp.zeros(ref.shape, ref.dtype)
    cell[...] = c_in[...]
    for d in range(2):
        for g in range(columns // span):
            part = slice(g * span, (g + 1) * span)
            w_in[d, :, part] = matmul(w_in[d, :, part], matrix[...]).astype(jnp.bfloat16)
    load_w.wait()

    def regroup(b, carry):
        for d in range(2):
            for g in range(columns // span):
                part = slice(g * span, (g + 1) * span)
                w[d, b, :, part] = matmul(w[d, b, :, part], matrix[...]).astype(jnp.bfloat16)
        return carry

    for b in range(blocks):
        regroup(b, 0)
    store_w.start()
    for n in range(3):
        wd_arrival(n, 0).wait_recv()
        for k in range(1, seqs):
            wd_across(n, k).start()
    for n in range(1, seqs):
        ids_arrival(n).wait_recv()
    streams = rows
    order_row = order[:, pl.ds(pl.multiple_of(seq * rows, LANES), rows)]
    square = (rows, rows)
    diagonal = lax.broadcasted_iota(jnp.int32, square, 0) == lax.broadcasted_iota(jnp.int32, square, 1)
    order_column = jnp.sum(
        jnp.where(diagonal, jnp.broadcast_to(order_row.astype(jnp.float32), square), 0.0), axis=1, keepdims=True
    ).astype(jnp.int32)
    total_streams = lens.shape[1]
    pick_column = (
        lax.broadcasted_iota(jnp.int32, (streams, total_streams), 1) == order_column
    ).astype(jnp.bfloat16)
    pick_row = (
        lax.broadcasted_iota(jnp.int32, (total_streams, streams), 0) == order_row
    ).astype(jnp.bfloat16)
    table[...] = jnp.zeros(table.shape, table.dtype)
    for d in range(2):
        for t in range(length):
            row = t if d == 0 else length - 1 - t
            table[t:t + 1] = all_ids[row // times, row % times:row % times + 1]
        table[LANES - 1:] = lengths
        high = jnp.floor(table[...] * (1.0 / 16.0))
        low = (table[...] - 16.0 * high).astype(jnp.bfloat16)
        high = high.astype(jnp.bfloat16)
        values = 16.0 * matmul(pick_column, high, NT) + matmul(pick_column, low, NT)
        info[d] = values
        values = 16.0 * matmul(high[:length], pick_row) + matmul(low[:length], pick_row)
        ids[d] = values

    def gates(s, step):
        slot, later = step % 3, (step + 1) % 3
        d = s
        when = time_of(d, step, length)
        live = info[s, :, LANES - 1:] > when.astype(jnp.float32)
        for g in range(groups):
            lanes = slice(g * LANES, (g + 1) * LANES)
            pre = [acc[:, (4 * g + k) * LANES:(4 * g + k + 1) * LANES] for k in range(4)]
            in_gate, forget, out_gate = sigmoid(pre[0]), sigmoid(pre[1]), sigmoid(pre[3])
            cell_gate = jnp.tanh(pre[2])
            old = cell[s, :, lanes]
            new = forget * old + in_gate * cell_gate
            for k, value in enumerate((in_gate, forget, cell_gate, out_gate, old)):
                stage[s, k, :, lanes] = value
            cell[s, :, lanes] = jnp.where(live, new, old)
            before = buf[s, slot, me, :, lanes].astype(jnp.float32)
            hidden = jnp.where(live, out_gate * jnp.tanh(new), before).astype(jnp.bfloat16)
            buf[s, later, me, :, lanes] = hidden
            wide = hidden.astype(jnp.float32)
            hidden_sq[d] += folded(jnp.where(live, wide * wide, 0.0))

    def decode(s, step):
        slot = step % 3
        d = s
        total = jnp.broadcast_to(b_dec[d], logit.shape)
        for b in range(blocks):
            total += matmul(buf[s, slot, b], wd[b, d])
        logit[...] = total
        when = time_of(d, step - 1, length)
        reach = when + 1 if d == 0 else when
        lookup = info[s]
        valid = (lookup[:, LANES - 1:] > reach.astype(jnp.float32)) & (step < length)
        target = column_of(lookup, step)
        value = logit[...]
        lanes = lax.broadcasted_iota(jnp.int32, value.shape, 1)
        hot = lanes.astype(jnp.float32) == target
        top = jnp.max(value, axis=1, keepdims=True)
        power = jnp.exp(value - top)
        total = jnp.sum(power, axis=1, keepdims=True)
        picked = jnp.sum(jnp.where(hot, value, 0.0), axis=1, keepdims=True)
        loss[d] += folded(jnp.broadcast_to(jnp.where(valid, top + jnp.log(total) - picked, 0.0), (rows, LANES)))
        kept = jnp.where(valid & (lanes < letters), value, 0.0)
        square = kept * kept
        logit_sq[d] += folded(sum(square[:, n * LANES:(n + 1) * LANES] for n in range(VOCAB_PAD // LANES)))
        slope = jnp.where(
            valid, (power * (1.0 / total) - jnp.where(hot, 1.0, 0.0)) * inverse[...], 0.0
        ).astype(jnp.bfloat16)
        grad[s] = slope
        dec_bias[d] += folded(slope.astype(jnp.float32))
        dec_grad[d] += matmul(buf[s, slot, me], grad[s], TN)

    others = tuple(other_core(peer) for peer in peers)

    def half(step, s):
        d = s

        @pl.when(step == 2)
        def _():
            if s == 0:
                for n in range(3):
                    for k in range(1, seqs):
                        wd_arrival(n, k).wait_recv()
                    wd_core(n, peers[n]).start()
                for block in (sibling,) + others:
                    wd_core(0, block).wait_recv()
            decode(s, step - 1)
            save_grad(s, step - 2).start()

        @pl.when(step < length)
        def _():
            now = column_of(info[s], step)
            hot = (lax.broadcasted_iota(jnp.int32, (rows, VOCAB_PAD), 1).astype(jnp.float32) == now)
            row = matmul(hot.astype(jnp.bfloat16), embed[d]).astype(jnp.bfloat16)
            acc[...] = matmul(row, w_in[d]).astype(jnp.bfloat16).astype(jnp.float32) + bias[d]

        for n, (block, halves) in enumerate(((side, (1,)), (up, (0,)), (across, (0, 1)))):
            for h in halves:
                transfer(s, step, block, h, 0, sibling).wait_recv()
            transfer_whole(s, step, block, 7 + n).start()

        slot = step % 3

        def advance(block):
            acc[...] += matmul(buf[s, slot, block], w[d, block])

        @pl.when(step < length)
        def _():
            for block in (me,) + peers:
                advance(block)

        if s == 0:
            pass_on(1, step)
        else:
            @pl.when(step < length)
            def _():
                pass_on(0, step + 1)

        for block in (sibling,) + others:
            transfer_whole(s, step, block, 6).wait_recv()

        @pl.when(step < length)
        def _():
            for block in (sibling,) + others:
                advance(block)

        @pl.when(step < length)
        def _():

            @pl.when(step > 0)
            def _():
                save_acts(s, step - 1).wait()

            gates(s, step)

            @pl.when(step > 0)
            def _():
                save(s, step - 1).wait()
                finish_sends(s, step - 1)

            for copy in direct(s, step + 1):
                copy.start()
            transfer_whole(s, step + 1, me, 6).start()
            save_acts(s, step).start()
            save(s, step).start()

        @pl.when(step > 1)
        def _():
            save_grad(s, step - 2).wait()
            decode(s, step)
            save_grad(s, step - 1).start()

    def every(step, carry):
        for s in range(2):
            half(step, s)
        return carry

    pass_on(0, 0)
    lax.fori_loop(0, length + 1, every, 0)
    store_w.wait()
    for n in range(1, seqs):
        ids_copy(n).wait_send()
    for n in range(3):
        wd_copy(n).wait_send()
        for k in range(1, seqs):
            wd_across(n, k).wait_send()
    for n, block in enumerate(peers + (me,)):
        wd_core(n, block).wait_send()
    for s in range(2):
        save(s, length - 1).wait()
        save_acts(s, length - 1).wait()
        save_grad(s, length - 1).wait()
        finish_sends(s, length - 1)
        finish_sends(s, length)


def backward_kernel(
    length, info, ids, w_dec_in, dec_grad, acts, grads, wholes, w_hbm,
    rec_out, letter_grad, hidden_grad, cell_grad, dec_out,
    w, rec, stage, grad, whole, pre, held, own, sent, got, passed, taken, kept, middle, w_dec, dec, dec_in, load_sem, act_sem,
    grad_sem, whole_sem, core_send, core_recv, chip_send, chip_recv, middle_send, middle_recv, dec_send, dec_recv, store_sem,
):
    me, sibling, peers = neighbours()
    rows, units = held.shape[1:]
    groups = units // LANES
    load_w = pltpu.make_async_copy(w_hbm, w, load_sem)
    load_w.start()

    def load_acts(s, step):
        return pltpu.make_async_copy(acts.at[step, s], stage.at[s], act_sem.at[s])

    def load_grad(s, step):
        return pltpu.make_async_copy(grads.at[step, s], grad.at[s], grad_sem.at[s])

    def load_whole(s, step):
        return pltpu.make_async_copy(wholes.at[step, s], whole.at[s], whole_sem.at[s])

    for s in range(2):
        load_acts(s, length - 1).start()
        load_grad(s, length - 1).start()
        load_whole(s, length - 1).start()
    seq, seqs, tall = lax.axis_index("seq"), dec.shape[0], dec.shape[2]
    for q in range(seqs):
        for d in range(2):
            dec[q, d] = dec_grad[d, q * tall:(q + 1) * tall].astype(jnp.bfloat16)
    greet((sibling,) + peers, seqs)

    def dec_copy(n):
        to = (seq + n) % seqs
        return pltpu.make_async_remote_copy(
            src_ref=dec.at[to], dst_ref=dec_in.at[n - 1], send_sem=dec_send.at[n - 1], recv_sem=dec_recv.at[n - 1],
            device_id=(to, me), device_id_type=MESH,
        )

    for n in range(1, seqs):
        dec_copy(n).start()
    padded(w_dec, w_dec_in)
    held[...] = jnp.zeros(held.shape, held.dtype)
    own[...] = jnp.zeros(own.shape, own.dtype)
    cell_grad[...] = jnp.zeros(cell_grad.shape, cell_grad.dtype)
    letter_grad[...] = jnp.zeros(letter_grad.shape, letter_grad.dtype)

    def clear(b, carry):
        for d in range(2):
            rec[d, b] = jnp.zeros(rec.shape[2:], rec.dtype)
        return carry

    lax.fori_loop(0, w.shape[1], clear, 0)
    load_w.wait()

    def to_core(s, turn, n):
        return remote(
            sent.at[s, n], got.at[s, turn % 2, n], core_send.at[s, n], core_recv.at[s, turn % 2, n], sibling
        )

    across, side, up = peers
    depth = rows // 2

    def to_chip(s, turn, n, h):
        part = slice(h * depth, (h + 1) * depth)
        return remote(
            passed.at[s, n, part], taken.at[s, turn % 2, n - 1, part],
            chip_send.at[s, n - 1, h], chip_recv.at[s, turn % 2, n - 1, h], peers[n],
        )

    def to_middle(s, turn, h):
        return remote(
            passed.at[s, 0, h * depth:(h + 1) * depth], middle.at[s, turn % 2, h],
            middle_send.at[s, h], middle_recv.at[s, turn % 2, h], peers[1 + h],
        )

    def chip_copies(s, turn):
        return [to_chip(s, turn, n, h) for n in (1, 2) for h in range(2)]

    def pass_on(s, turn):
        for h in range(2):
            to_middle(s, turn, h).wait_recv()
            total = kept[s, h] + middle[s, turn % 2, h].astype(jnp.float32)
            passed[s, 2 - h, h * depth:(h + 1) * depth] = total.astype(jnp.bfloat16)
            to_chip(s, turn, 2 - h, h).start()

    def outer(turn, s):
        step = length - 1 - turn
        load_whole(s, step).wait()
        for b in range(w.shape[1]):
            rec[s, b] += matmul(whole[s, b], pre[s], TN)

        @pl.when(turn < length - 1)
        def _():
            load_whole(s, step - 1).start()

        letters = lax.broadcasted_iota(jnp.int32, (VOCAB_PAD, rows), 0).astype(jnp.float32)
        hot = letters == ids[s, pl.ds(step, 1), :]
        letter_grad[s] += matmul(hot.astype(jnp.bfloat16), pre[s])

    def half(turn, s):
        step = length - 1 - turn
        d = s
        when = time_of(d, step, length)
        load_acts(s, step).wait()
        load_grad(s, step).wait()
        held[s] += matmul(grad[s], w_dec[d], NT)

        @pl.when(turn > 0)
        def _():
            for copy in chip_copies(s, turn - 1):
                copy.wait_recv()

        live = info[s, :, LANES - 1:] > when.astype(jnp.float32)
        for g in range(groups):
            lanes = slice(g * LANES, (g + 1) * LANES)
            through = own[s, :, lanes]
            for n in range(2):
                through += jnp.where(turn > 0, taken[s, (turn + 1) % 2, n, :, lanes].astype(jnp.float32), 0.0)
            total = held[s, :, lanes] + through
            in_gate, forget, cell_gate, out_gate, old = (stage[s, k, :, lanes] for k in range(5))
            squash = jnp.tanh(forget * old + in_gate * cell_gate)
            later = cell_grad[s, :, lanes]
            new = jnp.where(live, later + total * out_gate * (1.0 - squash * squash), 0.0)
            out = jnp.where(live, total * squash, 0.0)
            values = (
                new * cell_gate * in_gate * (1.0 - in_gate),
                new * old * forget * (1.0 - forget),
                new * in_gate * (1.0 - cell_gate * cell_gate),
                out * out_gate * (1.0 - out_gate),
            )
            for k, value in enumerate(values):
                pre[s, :, (4 * g + k) * LANES:(4 * g + k + 1) * LANES] = value.astype(jnp.bfloat16)
            cell_grad[s, :, lanes] = new * forget + jnp.where(live, 0.0, later)
            held[s, :, lanes] = jnp.where(live, 0.0, total)

        @pl.when(turn > 0)
        def _():
            for n in range(4):
                to_core(s, turn - 1, n).wait_send()
            for h in range(2):
                to_middle(s, turn - 1, h).wait_send()
            for copy in chip_copies(s, turn - 1):
                copy.wait_send()

        for n, block in enumerate(tuple(other_core(peer) for peer in peers) + (sibling,)):
            sent[s, n] = matmul(pre[s], w[d, block], NT).astype(jnp.bfloat16)
            to_core(s, turn, n).start()
        if s == 0:
            @pl.when(turn > 0)
            def _():
                pass_on(1, turn - 1)
                outer(turn - 1, 1)
        else:
            pass_on(0, turn)
            outer(turn, 0)

        for n, block in enumerate(peers + (me,)):
            part = matmul(pre[s], w[d, block], NT)
            to_core(s, turn, n).wait_recv()
            part += got[s, turn % 2, n].astype(jnp.float32)
            if n == 0:
                passed[s, 0] = part.astype(jnp.bfloat16)
                for h in range(2):
                    to_middle(s, turn, h).start()
            elif n < 3:
                now, later = n - 1, 2 - n
                kept[s, later] = part[later * depth:(later + 1) * depth]
                passed[s, n, now * depth:(now + 1) * depth] = (
                    part[now * depth:(now + 1) * depth].astype(jnp.bfloat16)
                )
                to_chip(s, turn, n, now).start()
            else:
                own[s] = part

        @pl.when(turn < length - 1)
        def _():
            load_acts(s, step - 1).start()
            load_grad(s, step - 1).start()


    def every(turn, carry):
        for s in range(2):
            half(turn, s)
        return carry

    lax.fori_loop(0, length, every, 0)
    pass_on(1, length - 1)
    outer(length - 1, 1)
    for n in range(1, seqs):
        dec_copy(n).wait()
    for d in range(2):
        dec_out[d] = dec[seq, d].astype(jnp.float32) + sum(
            dec_in[n, d].astype(jnp.float32) for n in range(seqs - 1)
        )
    for s in range(2):
        for copy in chip_copies(s, length - 1):
            copy.wait_recv()
        total = held[s] + own[s]
        for n in range(2):
            total += taken[s, (length - 1) % 2, n].astype(jnp.float32)
        hidden_grad[s] = total
        for n in range(4):
            to_core(s, length - 1, n).wait_send()
        for h in range(2):
            to_middle(s, length - 1, h).wait_send()
        for copy in chip_copies(s, length - 1):
            copy.wait_send()

    def narrow(b, carry):
        for d in range(2):
            w[d, b] = rec[d, b].astype(jnp.bfloat16)
        store(b).start()
        return carry

    def store(b):
        return pltpu.make_async_copy(w.at[:, b], rec_out.at[:, b], store_sem.at[b])

    for b in range(w.shape[1]):
        narrow(b, 0)
    for b in range(w.shape[1]):
        store(b).wait()


def kernel_step(ids, lengths, order, h_init, c_init, embed, w_in, w_rec, bias, w_dec, b_dec):
    seqs = lax.axis_size("seq")
    local_times, all_streams = ids.shape
    length = local_times * seqs
    rows, units = h_init.shape[1:]
    streams = 2
    letters, width = embed.shape[1:]
    columns = w_rec.shape[2]
    blocks = w_rec.shape[1] // units
    any_space, vmem = pl.BlockSpec(memory_space=pl.ANY), pl.BlockSpec(memory_space=pltpu.VMEM)
    bias_grouped = jnp.swapaxes(bias.reshape(2, units // LANES, LANES, 4), -1, -2).reshape(2, 1, columns)
    f32, bf16 = jnp.float32, jnp.bfloat16
    dma = pltpu.SemaphoreType.DMA
    shape = jax.ShapeDtypeStruct
    wholes, acts, grads, w_grouped, loss, logit_sq, hidden_sq, dec_bias, dec_grad, info, slot_ids, w_in_grouped = pl.pallas_call(
        functools.partial(forward_kernel, length, letters),
        out_shape=(
            shape((length, streams, blocks, rows, units), bf16),
            shape((length, streams, 5, rows, units), f32),
            shape((length, streams, rows, VOCAB_PAD), bf16),
            shape((2, blocks, units, columns), bf16),
            shape((2, 8, LANES), f32),
            shape((2, 8, LANES), f32),
            shape((2, 8, LANES), f32),
            shape((2, 8, VOCAB_PAD), f32),
            shape((2, units, VOCAB_PAD), f32),
            shape((streams, rows, LANES), f32),
            shape((streams, length, rows), f32),
            shape((2, LANES, columns), bf16),
        ),
        in_specs=[vmem] * 10 + [any_space],
        out_specs=(any_space,) * 4 + (vmem,) * 8,
        scratch_shapes=[
            pltpu.VMEM((2, blocks, units, columns), bf16),
            pltpu.VMEM((blocks, 2, units, VOCAB_PAD), bf16),
            pltpu.VMEM((streams, 3, blocks, rows, units), bf16),
            pltpu.VMEM((streams, rows, units), f32),
            pltpu.VMEM((rows, columns), f32),
            pltpu.VMEM((rows, VOCAB_PAD), f32),
            pltpu.VMEM((streams, 5, rows, units), f32),
            pltpu.VMEM((streams, rows, VOCAB_PAD), bf16),
            pltpu.VMEM((seqs, 8, all_streams), f32),
            pltpu.VMEM((LANES, all_streams), f32),
            pltpu.VMEM((4 * LANES, 4 * LANES), bf16),
            pltpu.VMEM((2, VOCAB_PAD, LANES), bf16),
            pltpu.VMEM((2, 1, VOCAB_PAD), f32),
            pltpu.VMEM((1, 1), f32),
            dma((2,)),
            dma((seqs - 1,)),
            dma((seqs,)),
            dma((7,)),
            dma((blocks, seqs)),
            dma((3, seqs - 1)),
            dma((blocks,)),
            dma((streams, 2, 10)),
            dma((streams, 3, blocks, 2)),
            dma((streams, 2)),
            dma((streams,)),
            dma((streams,)),
        ],
        compiler_params=pltpu.CompilerParams(
            collective_id=0, has_side_effects=True, vmem_limit_bytes=VMEM_LIMIT
        ),
        name="forward_visits",
    )(
        ids, lengths[None], order[None], h_init, c_init, embed, w_in, bias_grouped, b_dec, w_dec,
        w_rec.reshape(2, blocks, units, columns),
    )
    rec_grad, letter_grad, hidden_grad, cell_grad, dec_part = pl.pallas_call(
        functools.partial(backward_kernel, length),
        out_shape=(
            shape((2, blocks, units, columns), bf16),
            shape((2, VOCAB_PAD, columns), f32),
            shape((streams, rows, units), f32),
            shape((streams, rows, units), f32),
            shape((2, units // seqs, VOCAB_PAD), f32),
        ),
        in_specs=[vmem] * 4 + [any_space] * 4,
        out_specs=(any_space,) + (vmem,) * 4,
        scratch_shapes=[
            pltpu.VMEM((2, blocks, units, columns), bf16),
            pltpu.VMEM((2, blocks, units, columns), f32),
            pltpu.VMEM((streams, 5, rows, units), f32),
            pltpu.VMEM((streams, rows, VOCAB_PAD), bf16),
            pltpu.VMEM((streams, blocks, rows, units), bf16),
            pltpu.VMEM((streams, rows, columns), bf16),
            pltpu.VMEM((streams, rows, units), f32),
            pltpu.VMEM((streams, rows, units), f32),
            pltpu.VMEM((streams, 4, rows, units), bf16),
            pltpu.VMEM((streams, 2, 4, rows, units), bf16),
            pltpu.VMEM((streams, 3, rows, units), bf16),
            pltpu.VMEM((streams, 2, 2, rows, units), bf16),
            pltpu.VMEM((streams, 2, rows // 2, units), f32),
            pltpu.VMEM((streams, 2, 2, rows // 2, units), bf16),
            pltpu.VMEM((2, units, VOCAB_PAD), bf16),
            pltpu.VMEM((seqs, 2, units // seqs, VOCAB_PAD), bf16),
            pltpu.VMEM((seqs - 1, 2, units // seqs, VOCAB_PAD), bf16),
            dma,
            dma((streams,)),
            dma((streams,)),
            dma((streams,)),
            dma((streams, 4)),
            dma((streams, 2, 4)),
            dma((streams, 2, 2)),
            dma((streams, 2, 2, 2)),
            dma((streams, 2)),
            dma((streams, 2, 2)),
            dma((seqs - 1,)),
            dma((seqs - 1,)),
            dma((blocks,)),
        ],
        compiler_params=pltpu.CompilerParams(
            collective_id=1, has_side_effects=True, vmem_limit_bytes=VMEM_LIMIT
        ),
        name="backward_visits",
    )(info, slot_ids, w_dec, dec_grad, acts, grads, wholes, w_grouped)
    rec_part, edge_part, small = kernel_sums(
        rec_grad, letter_grad, embed, w_in_grouped, (loss, logit_sq, hidden_sq, dec_bias)
    )
    outs = (
        shape((1, 1), f32),
        shape(h_init.shape, f32),
        shape(h_init.shape, f32),
        shape(embed.shape, f32),
        shape((2, width, columns // seqs), f32),
        shape((2, w_rec.shape[1] // seqs, columns), f32),
        shape((2, columns // seqs), f32),
        shape((2, units // seqs, letters), f32),
        shape((2, letters), f32),
        shape((1, 2), f32),
        shape((1, 2), f32),
        shape((1, 2), f32),
    )
    tile = rec_part.shape[2]
    parts = rec_part.shape[1]
    results = pl.pallas_call(
        functools.partial(finish_kernel, w_rec.shape[1]),
        grid=(2, parts),
        out_shape=outs,
        in_specs=[vmem] * 7 + [pl.BlockSpec((1, 1, tile, columns), lambda d, r: (d, r, 0, 0))],
        out_specs=tuple(
            pl.BlockSpec((1, tile, columns), lambda d, r: (d, r, 0)) if n == 5 else vmem for n in range(len(outs))
        ),
        scratch_shapes=[pltpu.VMEM((4 * LANES, 4 * LANES), bf16)],
        compiler_params=pltpu.CompilerParams(
            dimension_semantics=("arbitrary", "arbitrary"), vmem_limit_bytes=VMEM_LIMIT
        ),
        name="results",
    )(lengths[None], embed, edge_part, dec_part, small, hidden_grad, cell_grad, rec_part)
    scalar = (0, 9, 10, 11)
    return tuple(
        x.reshape(()) if n == 0 else x.reshape(2) if n in scalar else x for n, x in enumerate(results)
    )


def finish_kernel(
    all_units, lens, embed, edge, dec, small, hidden_in, cell_in, rec,
    loss, hidden_grad, cell_grad, embed_grad, in_grad, rec_grad, bias_grad, dec_grad, dec_bias, rms_embed, rms_hidden,
    rms_logits, matrix,
):
    first = (pl.program_id(0) == 0) & (pl.program_id(1) == 0)
    letters, width = embed.shape[1:]
    span = matrix.shape[0]

    @pl.when(first)
    def _():
        matrix[...] = regroup_matrix(span)
        hidden_grad[...] = hidden_in[...]
        cell_grad[...] = cell_in[...]
        live = jnp.sum(lens[...].astype(jnp.float32), axis=1, keepdims=True)
        count = 2.0 * (live - lens.shape[1])
        at = 2 * TABLE
        loss[...] = small[at:at + 1, :1] / count
        for d in range(2):
            embed_grad[d] = small[d * TABLE:d * TABLE + letters, :width]
            in_grad[d] = edge[d, :width]
            bias_grad[d:d + 1] = edge[d, width:width + 1]
            dec_grad[d] = dec[d, :, :letters]
            for n in range(VOCAB_PAD // LANES):
                row = at + 5 + d * (VOCAB_PAD // LANES) + n
                last = min(LANES, letters - n * LANES)
                dec_bias[d:d + 1, n * LANES:n * LANES + last] = small[row:row + 1, :last]
            table = embed[d].astype(jnp.float32)
            square = jnp.sum(jnp.sum(table * table, axis=1, keepdims=True), axis=0, keepdims=True)
            rms_embed[:, d:d + 1] = jnp.sqrt(square / (letters * width))
            logit_sq = jnp.sum(small[at + 1 + d:at + 2 + d], axis=1, keepdims=True)
            hidden_sq = jnp.sum(small[at + 3 + d:at + 4 + d], axis=1, keepdims=True)
            rms_hidden[:, d:d + 1] = jnp.sqrt(hidden_sq / (all_units * live))
            rms_logits[:, d:d + 1] = jnp.sqrt(logit_sq / (letters * count / 2.0))

    for g in range(rec.shape[-1] // span):
        columns = slice(g * span, (g + 1) * span)
        rec_grad[0, :, columns] = matmul(rec[0, 0, :, columns], matrix[...], NT)


PIECE = 128
LAG = 3
WINDOW = 3
TABLE = 280


def spread(letter_grad, other, dims):
    high = letter_grad.astype(jnp.bfloat16)
    low = (letter_grad - high.astype(jnp.float32)).astype(jnp.bfloat16)
    return matmul(high, other, dims) + matmul(low, other, dims)


def reduce_kernel(
    rec_hbm, letter_grad, embed_in, w_in, loss, logit_sq, hidden_sq, dec_bias,
    rec_out, edge_out, small_out,
    own, ahead, behind, edge, edge_in, small, part, small_in, part_in, summed, matrix, embed,
    load_sem, line_send, line_recv, back_send, back_recv, edge_send, edge_recv,
    scatter_send, scatter_recv, seq_send, seq_recv, gather_send, gather_recv,
):
    seq, me = lax.axis_index("seq"), lax.axis_index("mp")
    count, parts = own.shape[1], own.shape[2]
    peers = lax.axis_size("mp")
    share = small.shape[0] // peers
    half = seq // (count // 2)
    place = seq + half * (count - 1 - 2 * seq)
    onward = 1 - 2 * half
    inner = count // 2 - 1
    lag = LAG + (inner - place) * 5
    load = pltpu.make_async_copy(rec_hbm, own, load_sem)
    load.start()

    def other_seq(n):
        return (seq + n) % count

    def other_mp(n):
        return (me + n) % peers

    barrier = pltpu.get_barrier_semaphore()
    for n in range(1, count):
        pl.semaphore_signal(barrier, inc=1, device_id=(other_seq(n), me), device_id_type=MESH)
    for n in range(1, peers):
        pl.semaphore_signal(barrier, inc=1, device_id=(seq, other_mp(n)), device_id_type=MESH)
    pl.semaphore_wait(barrier, count + peers - 2)
    load.wait()

    def send(src, dst, send_sem, recv_sem, seq_to, mp_to):
        return pltpu.make_async_remote_copy(
            src_ref=src, dst_ref=dst, send_sem=send_sem, recv_sem=recv_sem,
            device_id=(seq_to, mp_to), device_id_type=MESH,
        )

    def actual(chunk):
        return chunk + half * (count - 1 - 2 * chunk)

    pieces = 2 * parts

    def slot(k):
        return k // pieces, (k % pieces) // parts, k % parts

    def piece(chunk, d, r):
        return own.at[d, actual(chunk), r]

    def line_copy(k, crossing):
        i, d, r = slot(k)
        target = behind.at[i, d, r] if crossing else ahead.at[i, d, r]
        sem = back_recv.at[i, d, r] if crossing else line_recv.at[i, d, r]
        return send(piece(count - 1 - i, d, r), target, line_send.at[i, d, r], sem, seq + onward, me)

    def back_copy(k):
        i, d, r = slot(k)
        return send(
            piece(i, d, r), behind.at[i, d, r], back_send.at[i, d, r], back_recv.at[i, d, r], seq - onward, me
        )

    def add(chunk, d, r, term):
        ref = piece(chunk, d, r)
        ref[...] = (ref[...].astype(jnp.float32) + term[...].astype(jnp.float32)).astype(jnp.bfloat16)

    def line(k):
        i, d, r = slot(k)

        @pl.when((place > 0) & (i <= count - 1 - place))
        def _():
            line_copy(k, False).wait_recv()
            add(count - 1 - i, d, r, ahead.at[i, d, r])

        @pl.when((place == 0) & (k >= WINDOW))
        def _():
            line_copy(k - WINDOW, False).wait_send()

        @pl.when((i <= count - 2 - place) & (place < inner))
        def _():
            line_copy(k, False).start()

        @pl.when((i <= count - 2 - place) & (place == inner))
        def _():
            line_copy(k, True).start()

    def back(k):
        i, d, r = slot(k)

        @pl.when(i <= place)
        def _():
            back_copy(k).wait_recv()
            add(i, d, r, behind.at[i, d, r])

        @pl.when(i < place)
        def _():
            back_copy(k).start()

    def advance(k, carry):
        @pl.when(k < (count - 1) * pieces)
        def _():
            line(k)

        @pl.when((k >= lag) & (k - lag < (count // 2) * pieces))
        def _():
            back(k - lag)

        return carry

    def edge_copy(n):
        to = other_seq(n)
        return send(edge.at[to], edge_in.at[n - 1], edge_send.at[n - 1], edge_recv.at[n - 1], to, me)

    def scatter_copy(n):
        to = other_mp(n)
        rows = pl.ds(pl.multiple_of(to * share, 8), share)
        return send(small.at[rows], small_in.at[n - 1], scatter_send.at[n - 1], scatter_recv.at[n - 1], seq, to)

    def seq_copy(n):
        return send(part, part_in.at[n - 1], seq_send.at[n - 1], seq_recv.at[n - 1], other_seq(n), me)

    own_rows = pl.ds(pl.multiple_of(me * share, 8), share)

    def gather_copy(n):
        return send(
            summed.at[own_rows], summed.at[own_rows], gather_send.at[n - 1], gather_recv.at[me], seq, other_mp(n)
        )

    def gather_arrival(n):
        source = other_mp(n)
        rows = pl.ds(pl.multiple_of(source * share, 8), share)
        return send(summed.at[rows], summed.at[rows], gather_send.at[n - 1], gather_recv.at[source], seq, source)

    start = 6
    lax.fori_loop(0, 2, advance, 0)
    matrix[...] = regroup_matrix(matrix.shape[0])
    letters, width = embed_in.shape[1:]
    lanes = lax.broadcasted_iota(jnp.int32, (letters, LANES), 1)
    padded(embed, embed_in)
    for d in range(2):
        embed[d, :letters] = jnp.where(lanes == width, 1.0, embed[d, :letters].astype(jnp.float32)).astype(jnp.bfloat16)
    first = jnp.where(me == 0, 1.0, 0.0)
    for d in range(2):
        small[d * TABLE:(d + 1) * TABLE] = spread(letter_grad[d], w_in[d], NT)[:TABLE]
    small[2 * TABLE:] = jnp.zeros((small.shape[0] - 2 * TABLE, LANES), jnp.float32)
    at = 2 * TABLE
    small[at:at + 1] = jnp.sum(loss[0] + loss[1], axis=0, keepdims=True) * first
    for d in range(2):
        small[at + 1 + d:at + 2 + d] = jnp.sum(logit_sq[d], axis=0, keepdims=True) * first
        small[at + 3 + d:at + 4 + d] = jnp.sum(hidden_sq[d], axis=0, keepdims=True)
        row = jnp.sum(dec_bias[d], axis=0, keepdims=True) * first
        for n in range(VOCAB_PAD // LANES):
            line_at = at + 5 + d * (VOCAB_PAD // LANES) + n
            small[line_at:line_at + 1] = row[:, n * LANES:(n + 1) * LANES]
    for n in range(1, peers):
        scatter_copy(n).start()
    rows = edge.shape[2]
    span = matrix.shape[0]
    wide = own.shape[-1] // count
    for d in range(2):
        full = spread_left(embed[d], letter_grad[d]).astype(jnp.bfloat16)
        flat = [
            matmul(full[:, g * span:(g + 1) * span], matrix[...], NT).astype(jnp.bfloat16)
            for g in range(own.shape[-1] // span)
        ]
        for q in range(count):
            group, offset = (q * wide) // span, (q * wide) % span
            edge[q, d] = flat[group][:rows, offset:offset + wide]
    for n in range(1, count):
        edge_copy(n).start()
    lax.fori_loop(2, start, advance, 0)
    for n in range(1, peers):
        scatter_copy(n).wait()
    total = small[own_rows, :]
    for n in range(1, peers):
        total += small_in[n - 1]
    part[...] = total
    for n in range(1, count):
        seq_copy(n).start()
    lax.fori_loop(start, 2 * start, advance, 0)
    for n in range(1, count):
        seq_copy(n).wait()
        total += part_in[n - 1]
    summed[own_rows, :] = total
    for n in range(1, peers):
        gather_copy(n).start()
    lax.fori_loop(2 * start, (count - 1) * pieces + LAG, advance, 0)
    for n in range(1, peers):
        gather_copy(n).wait_send()
        gather_arrival(n).wait_recv()
    small_out[...] = summed[...]
    for n in range(1, count):
        edge_copy(n).wait()
    for d in range(2):
        edge_out[d] = edge[seq, d].astype(jnp.float32) + sum(
            edge_in[n, d].astype(jnp.float32) for n in range(count - 1)
        )
        rec_out[d] = own[d, seq]

    def finish(k, carry):
        i, d, r = slot(k)

        @pl.when((i <= count - 2 - place) & ((place > 0) | (k >= (count - 1) * pieces - WINDOW)))
        def _():
            line_copy(k, False).wait_send()

        @pl.when((i < place) & (k < (count // 2) * pieces))
        def _():
            back_copy(k).wait_send()

        return carry

    lax.fori_loop(0, (count - 1) * pieces, finish, 0)


def spread_left(other, letter_grad):
    high = letter_grad.astype(jnp.bfloat16)
    low = (letter_grad - high.astype(jnp.float32)).astype(jnp.bfloat16)
    return matmul(other, high, TN) + matmul(other, low, TN)


def kernel_sums(rec_grad, letter_grad, embed, w_in_grouped, stats):
    count = lax.axis_size("seq")
    peers = lax.axis_size("mp")
    columns = rec_grad.shape[-1]
    all_rows = rec_grad.shape[1] * rec_grad.shape[2]
    parts = all_rows // count // PIECE
    width = embed.shape[2]
    edge_rows = -(-(width + 1) // 8) * 8
    small_rows = -(-(2 * TABLE + 16) // (8 * peers)) * 8 * peers
    share = small_rows // peers
    f32, bf16 = jnp.float32, jnp.bfloat16
    dma = pltpu.SemaphoreType.DMA
    shape = jax.ShapeDtypeStruct
    vmem = pl.BlockSpec(memory_space=pltpu.VMEM)
    return pl.pallas_call(
        reduce_kernel,
        out_shape=(
            shape((2, parts, PIECE, columns), bf16),
            shape((2, edge_rows, columns // count), f32),
            shape((small_rows, LANES), f32),
        ),
        in_specs=[pl.BlockSpec(memory_space=pl.ANY)] + [vmem] * 7,
        out_specs=(vmem,) * 3,
        scratch_shapes=[
            pltpu.VMEM((2, count, parts, PIECE, columns), bf16),
            pltpu.VMEM((count - 1, 2, parts, PIECE, columns), bf16),
            pltpu.VMEM((count // 2, 2, parts, PIECE, columns), bf16),
            pltpu.VMEM((count, 2, edge_rows, columns // count), bf16),
            pltpu.VMEM((count - 1, 2, edge_rows, columns // count), bf16),
            pltpu.VMEM((small_rows, LANES), f32),
            pltpu.VMEM((share, LANES), f32),
            pltpu.VMEM((peers - 1, share, LANES), f32),
            pltpu.VMEM((count - 1, share, LANES), f32),
            pltpu.VMEM((small_rows, LANES), f32),
            pltpu.VMEM((4 * LANES, 4 * LANES), bf16),
            pltpu.VMEM((2, VOCAB_PAD, LANES), bf16),
            dma,
            dma((count - 1, 2, parts)),
            dma((count - 1, 2, parts)),
            dma((count // 2, 2, parts)),
            dma((count // 2, 2, parts)),
            dma((count - 1,)),
            dma((count - 1,)),
            dma((peers - 1,)),
            dma((peers - 1,)),
            dma((count - 1,)),
            dma((count - 1,)),
            dma((peers - 1,)),
            dma((peers,)),
        ],
        compiler_params=pltpu.CompilerParams(
            collective_id=2, has_side_effects=True, vmem_limit_bytes=VMEM_LIMIT
        ),
        name="gradient_sums",
    )(
        rec_grad.reshape(2, count, parts, PIECE, columns), letter_grad, embed, w_in_grouped, *stats,
    )


def plain_step(ids, lengths, order, count, h_init, c_init, embed, w_in, w_rec, bias, w_dec, b_dec, matrix):
    first_mp = (lax.axis_index("mp") == 0).astype(jnp.float32)
    per_dev, own_units = h_init.shape[1:]
    lanes = matrix.shape[0] // 4
    wd_full = lax.all_gather(w_dec, "mp", axis=1, tiled=True)
    whole_ids = lax.all_gather(ids, "seq", axis=0, tiled=True)
    own_order = lax.dynamic_slice_in_dim(order, lax.axis_index("seq") * per_dev, per_dev)
    slot_ids = jnp.take(whole_ids, own_order, axis=1)
    own_len = jnp.take(lengths, own_order)
    step_ids = jnp.stack([slot_ids, jnp.flip(slot_ids, 0)])
    w_rec_grouped = grouped(w_rec, matrix)
    w_in_grouped = grouped(w_in, matrix)
    bias_grouped = jnp.swapaxes(
        bias.reshape(2, own_units // lanes, lanes, 4), -1, -2
    ).reshape(bias.shape)
    loss, hidden_sq, logit_sq, dec_bias, dec_grad, hidden_grad, cell_grad, rec_grad, letter_grad = recurrences(
        step_ids, own_len, h_init, c_init, embed, w_in_grouped, w_rec_grouped, bias_grouped, w_dec, wd_full,
        b_dec, count, lanes,
    )
    embed_wide = embed.astype(jnp.float32)
    in_grad = jnp.einsum("dve,dvc->dec", embed_wide, letter_grad, precision=lax.Precision.HIGHEST)
    bias_grad = jnp.sum(letter_grad, axis=1, keepdims=True)
    embed_part = jnp.einsum(
        "dvc,dec->dve", letter_grad, w_in_grouped.astype(jnp.float32), precision=lax.Precision.HIGHEST
    )
    edge = ungrouped_wide(jnp.concatenate([in_grad, bias_grad], axis=1), lanes)
    rec_part = lax.psum_scatter(rec_grad.astype(jnp.bfloat16), "seq", scatter_dimension=1, tiled=True)
    edge_part = lax.psum_scatter(edge.astype(jnp.bfloat16), "seq", scatter_dimension=2, tiled=True)
    dec_part = lax.psum_scatter(dec_grad.astype(jnp.bfloat16), "seq", scatter_dimension=1, tiled=True)
    loss_sum, hidden_all, logit_all, dec_bias_grad, embed_grad = lax.psum(
        (loss * first_mp, hidden_sq, logit_sq * first_mp, dec_bias * first_mp, embed_part), ("seq", "mp")
    )
    rec_out = ungrouped(rec_part, matrix).astype(jnp.float32)
    return (
        loss_sum, hidden_all, logit_all, dec_bias_grad, dec_part.astype(jnp.float32), hidden_grad, cell_grad, rec_out,
        edge_part[:, :-1].astype(jnp.float32), edge_part[:, -1].astype(jnp.float32), embed_grad,
    )


def per_device(ids, lengths, order, h_init, c_init, embed, w_in, w_rec, bias, w_dec, b_dec):
    streams = ids.shape[1]
    per_dev, own_units = h_init.shape[1:]
    all_units, letter_count = w_rec.shape[1], embed.shape[1]
    fits = own_units % LANES == 0 and per_dev % LANES == 0 and per_dev <= 256 and own_units <= 256
    fits = fits and all_units % (lax.axis_size("seq") * PIECE) == 0 and letter_count <= TABLE
    if lax.axis_size("mp") == 8 and lax.axis_size("seq") == 4 and fits and embed.shape[2] < LANES:
        return kernel_step(ids, lengths, order, h_init, c_init, embed, w_in, w_rec, bias, w_dec, b_dec)
    live_total = jnp.sum(lengths).astype(jnp.float32)
    count = 2.0 * (jnp.sum(lengths) - streams).astype(jnp.float32)
    _, matrix = column_order(own_units)
    (
        loss_sum, hidden_all, logit_all, dec_bias_grad, dec_part, hidden_grad, cell_grad, rec_out, in_out, bias_out,
        embed_grad,
    ) = plain_step(ids, lengths, order, count, h_init, c_init, embed, w_in, w_rec, bias, w_dec, b_dec, matrix)
    embed_wide = embed.astype(jnp.float32)
    rms_embed = jnp.sqrt(jnp.mean(embed_wide * embed_wide, axis=(1, 2)))
    return (
        loss_sum / count,
        hidden_grad,
        cell_grad,
        embed_grad,
        in_out,
        rec_out,
        bias_out,
        dec_part,
        dec_bias_grad,
        rms_embed,
        jnp.sqrt(hidden_all / (all_units * live_total)),
        jnp.sqrt(logit_all / (letter_count * count / 2.0)),
    )


def solution(mesh):
    in_specs = (
        P("seq", None),
        P(),
        P(),
        P(None, "seq", "mp"),
        P(None, "seq", "mp"),
        P(),
        P(None, None, "mp"),
        P(None, None, "mp"),
        P(None, "mp"),
        P(None, "mp", None),
        P(),
    )
    out_specs = (
        P(),
        P(None, "seq", "mp"),
        P(None, "seq", "mp"),
        P(),
        P(None, None, ("mp", "seq")),
        P(None, "seq", "mp"),
        P(None, ("mp", "seq")),
        P(None, ("mp", "seq"), None),
        P(),
        P(),
        P(),
        P(),
    )
    return jax.shard_map(
        per_device, mesh=mesh, in_specs=in_specs, out_specs=out_specs, check_vma=False
    )
```
